128 devices in a mesh: space: 32 (over y, z, core), scene: 4 (over x).
Axes of the slice: x: 4, y: 4, z: 4, core: 2. Of those that a mesh axis runs over, the one named last changes fastest.
Arguments:
- feats: bfloat16 [1024, 512, 128], P(('scene', 'space')), parts along dimension 0, may hold values from -6 to 6
- mask: int32 [1024, 512], P(('scene', 'space')), parts along dimension 0, may hold values from 0 to 1, as said below
- neighbours: int32 [1024, 8], P(('scene', 'space')), parts along dimension 0, may hold values from -1 to 255, as said below
- weight_one: bfloat16 [27, 128, 128], replicated, may hold values from -0.109375 to 0.109375
- weight_two: bfloat16 [27, 128, 128], replicated, may hold values from -0.109375 to 0.109375
- cotangent: bfloat16 [1024, 512, 128], P(('scene', 'space')), parts along dimension 0, may hold values from -12 to 12
Outputs:
- output: bfloat16 [1024, 512, 128], P(('scene', 'space')), parts along dimension 0
- grad_input: bfloat16 [1024, 512, 128], P(('scene', 'space')), parts along dimension 0
- grad_w1: float32 [108, 128, 128], P('scene'), parts along dimension 0
- grad_w2: float32 [108, 128, 128], P('scene'), parts along dimension 0
The draws below stay inside these ranges and needn't reach their ends.
There are 4 independent parts, one for each index of `scene`. The reference program is written for one: setup_inputs(seed, part) draws one part's arguments, and reference() takes and returns one part's arrays. A program takes and returns all parts, laid end to end along the dimension named above; an argument that names none is the same for every part. Nothing has to cross between parts.
Inputs may be any that keep to these rules, and one draw needn't show every extreme that they name: `mask`: 1 where the voxel is occupied, else 0; an empty brick (see neighbours) is 0 throughout. `neighbours`: A brick number or -1. Brick g is held by index g // 8 of space, and the entries of brick g name only bricks held by that index or by the index one lower or one higher. If brick g names brick h in a direction, h names g in the opposite one (entry 7 - j for entry j). Empty bricks have only -1 entries and are named by no entry. Brick 256 - 1 is named in every draw.
All inputs are finite; a program needn't handle non-finite values.
Results may differ from the reference program's by a relative error of at most 0.02.
Values may be sent and summed in bfloat16 or wider, within the bound.
A program may use at most 192 MiB of HBM per device.

```python
import math
import jax
import jax.numpy as jnp
from jax import lax

C = 128
EDGE = 8
VOX = 512
TILE = 1
WIDE = 8
BR_DEV = 8
BRICKS = 256
N_SPACE = 32


DIRECTIONS = ((-1, -1), (-1, 0), (-1, 1), (0, -1), (0, 1), (1, -1), (1, 0), (1, 1))


def geometry(key):
    base_key = jax.random.fold_in(key, 7)
    key_fill, key_density, key_voxel = jax.random.split(base_key, 3)
    width_x = N_SPACE * TILE
    width_y = WIDE
    coord_x = jnp.arange(width_x, dtype=jnp.int32)[:, None] * jnp.ones((1, width_y), jnp.int32)
    coord_y = jnp.ones((width_x, 1), jnp.int32) * jnp.arange(width_y, dtype=jnp.int32)[None, :]
    present = jax.random.randint(key_fill, (width_x, width_y), 0, 4) > 0
    corner_pair = (coord_x >= width_x - 2) & (coord_y == width_y - 1)
    present = present | corner_pair
    number = coord_x * width_y + coord_y
    padded_present = jnp.pad(present, 1)
    padded_number = jnp.pad(number, 1, constant_values=-1)
    columns = []
    for step_x, step_y in DIRECTIONS:
        beside = padded_present[1 + step_x:1 + step_x + width_x, 1 + step_y:1 + step_y + width_y]
        number_near = padded_number[1 + step_x:1 + step_x + width_x, 1 + step_y:1 + step_y + width_y]
        columns.append(jnp.where(beside & present, number_near, -1))
    neighbour_list = jnp.stack(columns, axis=-1).reshape(-1, 8).astype(jnp.int32)
    density = jax.random.randint(key_density, (width_x, width_y, 1), 2, 9)
    voxel_draw = jax.random.randint(key_voxel, (width_x, width_y, VOX), 0, 8)
    occupancy = ((voxel_draw < density) & present[:, :, None]).astype(jnp.int32).reshape(-1, VOX)
    return (neighbour_list, occupancy)


def draw_neighbours(key, part):
    return geometry(key)[0]


def draw_mask(key, part):
    return geometry(key)[1]


def steps_of(key, shape, shards, smallest, top_value):
    factor_of = 1.0
    for dim, shards_of in shards:
        steps = jax.random.uniform(jax.random.fold_in(jax.random.fold_in(key, 6), dim), (shards_of,), jnp.float32, smallest / len(shards), top_value / len(shards))
        factor_of = factor_of * jnp.repeat(jnp.exp(steps), shape[dim] // shards_of).reshape((-1,) + (1,) * (len(shape) - 1 - dim))
    return factor_of


def noise(own_key, extent, scale, reach, shards=(), kind=jnp.bfloat16):
    values = scale * jax.random.normal(own_key, extent, jnp.float32)
    if shards:
        values = values * steps_of(own_key, extent, shards, -0.22, 0.18)
    return jnp.clip(values, -reach, reach).astype(kind)


def setup_inputs(seed: int = 0, part: int = 0) -> dict:
    splits = jax.random.split(jax.random.key(seed), 7)
    own_keys = jax.random.split(jax.random.fold_in(splits[6], part), 7)
    return {
        "feats": noise(own_keys[0], (BRICKS, VOX, C), 1.0, 6.0, ((0, 32),)),
        "mask": draw_mask(jax.random.fold_in(jax.random.fold_in(splits[6], part), 71), part),
        "neighbours": draw_neighbours(jax.random.fold_in(jax.random.fold_in(splits[6], part), 71), part),
        "weight_one": noise(splits[3], (27, C, C), (27 * C) ** -0.5, 0.109375),
        "weight_two": noise(splits[4], (27, C, C), (27 * C) ** -0.5, 0.109375),
        "cotangent": noise(own_keys[5], (BRICKS, VOX, C), 2.0, 12.0, ((0, 32),)),
    }


DIRECTIONS = ((-1, -1), (-1, 0), (-1, 1), (0, -1), (0, 1), (1, -1), (1, 0), (1, 1))

def rim_slices(step_value, length):
    if step_value < 0:
        return (slice(length - 1, length), slice(0, 1))
    if step_value > 0:
        return (slice(0, 1), slice(length + 1, length + 2))
    return (slice(0, length), slice(1, length + 1))

def assemble(cube_view, sources, source_index):
    length = cube_view.shape[1]
    padded = jnp.pad(cube_view, ((0, 0), (1, 1), (1, 1), (1, 1), (0, 0)))
    for column, (step_x, step_y) in enumerate(DIRECTIONS):
        source_x, target_x = rim_slices(step_x, length)
        source_y, target_y = rim_slices(step_y, length)
        rim_cells = sources[:, source_x, source_y]
        fetched = jnp.take(rim_cells, source_index[:, column].astype(jnp.int32), axis=0)
        padded = padded.at[:, target_x, target_y, 1:length + 1].set(fetched)
    return padded

def window_stack(padded, shift_x, flipped):
    length = padded.shape[1] - 2
    channels = padded.shape[-1]
    pieces = []
    for shift_y in range(3):
        for shift_z in range(3):
            if flipped:
                corner_x, corner_y, corner_z = (2 - shift_x, 2 - shift_y, 2 - shift_z)
            else:
                corner_x, corner_y, corner_z = (shift_x, shift_y, shift_z)
            cells = padded[:, corner_x:corner_x + length, corner_y:corner_y + length, corner_z:corner_z + length]
            pieces.append(cells.reshape(-1, channels))
    return jnp.concatenate(pieces, axis=1)

def convolve(padded, weight, flipped):
    channels = padded.shape[-1]
    summed = None
    for shift_x in range(3):
        stacked = window_stack(padded, shift_x, flipped)
        weight_block = weight[9 * shift_x:9 * shift_x + 9]
        if flipped:
            weight_block = jnp.swapaxes(weight_block, 1, 2)
        partial_sum = jnp.dot(stacked, weight_block.reshape(9 * channels, channels), preferred_element_type=jnp.float32)
        summed = partial_sum if summed is None else summed + partial_sum
    return summed

def weight_grad(padded, grads):
    channels = padded.shape[-1]
    blocks = []
    for shift_x in range(3):
        stacked = window_stack(padded, shift_x, False)
        product = lax.dot_general(stacked, grads, (((0,), (0,)), ((), ())), preferred_element_type=jnp.float32)
        blocks.append(product.reshape(9, channels, channels))
    return jnp.concatenate(blocks, axis=0)

def silu_slope(values):
    sigmoid_value = jax.nn.sigmoid(values)
    return sigmoid_value * (1.0 + values * (1.0 - sigmoid_value))

def reference(feats, mask, neighbours, weight_one, weight_two, cotangent):
    bricks, voxels, channels = feats.shape
    occupied = mask.reshape(-1, 1).astype(jnp.float32)
    source_index = jnp.where(neighbours >= 0, neighbours, bricks).astype(jnp.int32)
    blank_brick = jnp.zeros((1, EDGE, EDGE, EDGE, channels), jnp.bfloat16)

    def extend(flat_field):
        cube_view = flat_field.reshape(bricks, EDGE, EDGE, EDGE, channels)
        return assemble(cube_view, jnp.concatenate([cube_view, blank_brick], axis=0), source_index)
    inputs = feats * mask[:, :, None].astype(jnp.bfloat16)
    padded_in = extend(inputs)
    first_pre = convolve(padded_in, weight_one, False)
    hidden = (occupied * jax.nn.silu(first_pre)).astype(jnp.bfloat16)
    padded_hidden = extend(hidden)
    second_pre = convolve(padded_hidden, weight_two, False)
    output = (occupied * jax.nn.silu(second_pre)).astype(jnp.bfloat16)
    grad_second = (cotangent.reshape(-1, channels).astype(jnp.float32) * occupied * silu_slope(second_pre)).astype(jnp.bfloat16)
    back_second = convolve(extend(grad_second), weight_two, True)
    grad_first = (occupied * silu_slope(first_pre) * back_second).astype(jnp.bfloat16)
    grad_input = (occupied * convolve(extend(grad_first), weight_one, True)).astype(jnp.bfloat16)
    grad_scale = 1.0 / math.sqrt(voxels * BR_DEV)
    grad_w2 = weight_grad(padded_hidden, grad_second) * grad_scale
    grad_w1 = weight_grad(padded_in, grad_first) * grad_scale
    return (output.reshape(bricks, voxels, channels), grad_input.reshape(bricks, voxels, channels), grad_w1, grad_w2)
```

```python
import functools
import math

import jax
import jax.numpy as jnp
from jax import lax
from jax.experimental import pallas as pl
from jax.experimental.pallas import tpu as pltpu
from jax.sharding import PartitionSpec as P

BF = jnp.bfloat16
F32 = jnp.float32
C = 128
MESH = pl.DeviceIdType.MESH

A0, A7, B0, B7 = 0, 1, 2, 3


def shifted(v):
    row = lax.broadcasted_iota(jnp.int32, v.shape, v.ndim - 1 - 1)
    down = jnp.where(row == 0, 0.0, pltpu.roll(v, 1, v.ndim - 2))
    up = jnp.where(row == 7, 0.0, pltpu.roll(v, 7, v.ndim - 2))
    return down, v, up


def put_plane(x_ref, a, v):
    for k, s in enumerate(shifted(v.reshape(64, 8, C))):
        x_ref[:, 1 + a, 1:9, :, C * k : C * k + C] = s.reshape(4, 8, 16, C).astype(BF)


def pair_plane(ref, a):
    v = ref[:, a].astype(F32).reshape(4, 2, 8, 8, C)
    return jnp.stack([v[:, 0], v[:, 1]], axis=2).reshape(4, 8, 16, C)


def unpair_plane(ref, a, v):
    w = v.reshape(4, 8, 2, 8, C)
    for half in range(2):
        ref[:, half, a] = w[:, :, half].astype(BF)


def take_faces(x_ref, h_ref):
    def body(p, _):
        for half in range(2):
            for face, cells in (
                (A0, x_ref[p, 1, 1:9, :, C : 2 * C]),
                (A7, x_ref[p, 8, 1:9, :, C : 2 * C]),
                (B0, x_ref[p, 1:9, 1, :, C : 2 * C]),
                (B7, x_ref[p, 1:9, 8, :, C : 2 * C]),
            ):
                v = cells.astype(F32).reshape(8, 2, 8, C)
                h_ref[8 + 2 * p + half, face] = v[:, half].astype(BF)
        return 0

    lax.fori_loop(0, 4, body, 0)


def fill_rim(x_ref, h_ref, nbr_ref, first):
    def body(p, _):
        def source(column):
            out = []
            for half in range(2):
                n = nbr_ref[2 * p + half, column]
                out.append(jnp.where(n >= 0, jnp.clip(n - first, 0, 23), 24))
            return out

        def line(column, face):
            i, j = source(column)
            u = h_ref[i, face].astype(F32)
            v = h_ref[j, face].astype(F32)
            w = jnp.stack([u, v], axis=1).reshape(16, 8, C)
            return [s.reshape(8, 16, C).astype(BF) for s in shifted(w)]

        def cell(column, face, where):
            i, j = source(column)
            u = h_ref[i, face, where].astype(F32)
            v = h_ref[j, face, where].astype(F32)
            w = jnp.stack([u, v], axis=0)
            return [s.reshape(16, C).astype(BF) for s in shifted(w)]

        for column, face, where, i, j in (
            (0, A7, 7, 0, 0),
            (2, A7, 0, 0, 9),
            (5, A0, 7, 9, 0),
            (7, A0, 0, 9, 9),
        ):
            for k, s in enumerate(cell(column, face, where)):
                x_ref[p, i, j, :, C * k : C * k + C] = s
        for column, face, i in ((1, A7, 0), (6, A0, 9)):
            for k, s in enumerate(line(column, face)):
                x_ref[p, i, 1:9, :, C * k : C * k + C] = s
        for column, face, j in ((3, B7, 0), (4, B0, 9)):
            for k, s in enumerate(line(column, face)):
                x_ref[p, 1:9, j, :, C * k : C * k + C] = s
        return 0

    lax.fori_loop(0, 4, body, 0)


def build_taps(t_ref, w_ref, flipped):
    def body(t, _):
        zero = jnp.zeros((C, C), BF)
        t_ref[t, :, C:] = zero
        t_ref[27 + t, :, :C] = zero
        for k in range(3):
            if flipped:
                w = w_ref[26 - (9 * k + t)].astype(F32).T.astype(BF)
            else:
                w = w_ref[9 * k + t]
            t_ref[9 * k + t, :, :C] = w
            t_ref[9 * k + 9 + t, :, C:] = w
        return 0

    lax.fori_loop(0, 9, body, 0)


def convolve(x_ref, t_ref, epilogue, between=None):
    def body(q, _):
        windows = [
            x_ref[:, 2 * q + p, k : k + 8].reshape(512, 3 * C) for p in range(4) for k in range(3)
        ]
        total = jnp.dot(
            jnp.concatenate(windows, axis=1),
            t_ref[...].reshape(36 * C, 2 * C),
            preferred_element_type=F32,
        )
        for u in range(2):
            epilogue(2 * q + u, total[:, C * u : C * u + C].reshape(4, 8, 16, C))
        if between is not None:
            between(q)
        return 0

    lax.fori_loop(0, 4, body, 0)


def put_transposed(gt_ref, a, v):
    flat = v.reshape(4, C, C)
    for p in range(4):
        gt_ref[p // 2, a + 2, :, C * (p % 2) : C * (p % 2) + C] = flat[p].T.astype(BF)


def weight_grad(x_ref, gt_ref, g_ref, scale):
    def body(k, _):
        total = None
        for i in range(0, 10, 2):
            left = jnp.concatenate(
                [gt_ref[h, i + q : i + q + 3].reshape(384, 256) for q in range(2) for h in range(2)],
                axis=1,
            )
            right = jnp.concatenate(
                [x_ref[:, i + q, pl.ds(k, 8)].reshape(512, 384) for q in range(2)], axis=0
            )
            d = jnp.dot(left, right, preferred_element_type=F32)
            total = d if total is None else total + d
        total = total * scale
        for q in range(3):
            for z in range(3):
                block = total[C * q : C * q + C, C * z : C * z + C].T.astype(BF)
                tap = 9 * (2 - q) + 3 * k + z
                for s in range(8):
                    g_ref[s % 2, s // 2, tap] = block[16 * s : 16 * s + 16]
        return 0

    lax.fori_loop(0, 3, body, 0)


class Reduction:
    def __init__(self, place, refs):
        self.place = place
        (self.g, self.r0, self.s0, self.r1, self.s1, self.r2, self.fin, self.send, self.recv) = refs
        self.started = []

    def copy(self, src, dst, slot, peer):
        return pltpu.make_async_remote_copy(
            src_ref=src,
            dst_ref=dst,
            send_sem=self.send.at[slot],
            recv_sem=self.recv.at[slot],
            device_id={"space": peer},
            device_id_type=MESH,
        )

    def phase(self, n):
        p = self.place
        core, ma, mb = p["core"], p["ma"], p["mb"]
        if n == 0:
            return [self.copy(self.g.at[1 - core], self.r0, 0, p["sibling"])]
        if n == 5:
            return [self.copy(self.fin.at[core], self.fin.at[core], 13, p["sibling"])]
        copies = []
        for d in range(3):
            pa, pb = p["peers_a"][d], p["peers_b"][d]
            if n == 1:
                copies.append(self.copy(self.s0.at[pa[0]], self.r1.at[d], 1 + d, pa[1]))
            elif n == 2:
                copies.append(
                    self.copy(self.s1.at[pl.ds(7 * pb[0], 7)], self.r2.at[d], 4 + d, pb[1])
                )
            elif n == 3:
                mine = self.fin.at[core, ma, pl.ds(7 * mb, 7)]
                copies.append(self.copy(mine, mine, 7 + d, pb[1]))
            else:
                mine = self.fin.at[core, ma]
                copies.append(self.copy(mine, mine, 10 + d, pa[1]))
        return copies

    def start(self, n):
        for c in self.phase(n):
            c.start()

    def wait(self, n):
        for c in self.phase(n):
            c.wait_recv()

    def drain(self):
        for n in range(6):
            for c in self.phase(n):
                c.wait_send()

    def step(self, n):
        p = self.place
        core, ma, mb = p["core"], p["ma"], p["mb"]
        if n == 0:
            self.start(0)
            return
        self.wait(n - 1)
        if n == 1:

            def add(i, _):
                self.s0[i] = (self.g[core, i].astype(F32) + self.r0[i].astype(F32)).astype(BF)
                return 0

            lax.fori_loop(0, 4, add, 0)
        elif n == 2:
            v = self.s0[ma].astype(F32)
            for d in range(3):
                v = v + self.r1[d].astype(F32)
            self.s1[...] = v.astype(BF)
        elif n == 3:
            v = self.s1[pl.ds(7 * mb, 7)].astype(F32)
            for d in range(3):
                v = v + self.r2[d].astype(F32)
            self.fin[core, ma, pl.ds(7 * mb, 7)] = v.astype(BF)
        if n < 6:
            self.start(n)


def silu_parts(v):
    s = 1.0 / (1.0 + jnp.exp(-v))
    return s, s * (1.0 + v * (1.0 - s))


def kernel(
    scale,
    feats_h, mask_h, nbr_ref, w1_h, w2_h, cot_h,
    out_h, gin_h, gw1_h, gw2_h,
    feats, mask, w1, w2, cot, out_s,
    xin, xhid, xg, taps, maskb, pre1, gt,
    h0, h1, h2, h3,
    load_sem, store_sem, face_send, face_recv,
    *red_refs,
):
    me = lax.axis_index("space")
    n_space = 32
    core = lax.rem(me, 2)
    chip = me // 2
    z = lax.rem(chip, 4)
    y = chip // 4
    right, left = lax.rem(me + 1, n_space), lax.rem(me + n_space - 1, n_space)
    ma = (1 - core) * y + core * z
    mb = (1 - core) * z + core * y
    sa = 8 - 6 * core
    sb = 2 + 6 * core
    peers_a, peers_b = [], []
    for d in range(1, 4):
        ca, cb = lax.rem(ma + d, 4), lax.rem(mb + d, 4)
        peers_a.append((ca, me + (ca - ma) * sa))
        peers_b.append((cb, me + (cb - mb) * sb))
    place = {
        "core": core, "ma": ma, "mb": mb, "sibling": me + 1 - 2 * core,
        "peers_a": peers_a, "peers_b": peers_b,
    }
    first = 8 * (me - 1)
    red2 = Reduction(place, red_refs[:9])
    red1 = Reduction(place, red_refs[9:])

    loads = [
        pltpu.make_async_copy(src, dst, load_sem.at[i])
        for i, (src, dst) in enumerate(
            ((feats_h, feats), (mask_h, mask), (w1_h, w1), (w2_h, w2), (cot_h, cot))
        )
    ]
    for c in loads:
        c.start()

    barrier = pltpu.get_barrier_semaphore()
    for peer in [left, right] + [q for _, q in peers_a] + [q for _, q in peers_b]:
        pl.semaphore_signal(barrier, inc=1, device_id={"space": peer}, device_id_type=MESH)
    pl.semaphore_wait(barrier, 8)

    faces = (h0, h1, h2, h3)

    def face_copies(n):
        h = faces[n]
        return [
            pltpu.make_async_remote_copy(
                src_ref=h.at[pl.ds(8, 8)],
                dst_ref=h.at[pl.ds(at, 8)],
                send_sem=face_send.at[n, side],
                recv_sem=face_recv.at[n, side],
                device_id={"space": peer},
                device_id_type=MESH,
            )
            for side, (at, peer) in enumerate(((0, right), (16, left)))
        ]

    def send_faces(n, x_ref):
        take_faces(x_ref, faces[n])
        for c in face_copies(n):
            c.start()

    def receive_faces(n, x_ref):
        for c in face_copies(n):
            c.wait_recv()
        fill_rim(x_ref, faces[n], nbr_ref, first)

    for h in faces:
        h[24] = jnp.zeros((4, 8, 8, C), BF)
    for red in (red1, red2):
        for side in range(2):
            for q in range(4):
                red.g[side, q, 27] = jnp.zeros((16, C), BF)
    for side in range(2):
        for a in (0, 1, 10, 11):
            gt[side, a] = jnp.zeros((C, 2 * C), BF)

    loads[1].wait()
    loads[0].wait()

    def mask_plane(a, _):
        row = lax.broadcasted_iota(jnp.int32, (C, C), 0)
        lane = lax.broadcasted_iota(jnp.int32, (C, C), 1)
        hit = lane == lax.rem(a, 2) * 64 + (row // 16) * 8 + lax.rem(row, 8)
        second = lax.rem(row // 8, 2) == 1
        at = pl.ds(pl.multiple_of((a // 2) * C, C), C)
        pieces = []
        for p in range(4):
            m0 = mask[2 * p : 2 * p + 1, at].astype(F32)
            m1 = mask[2 * p + 1 : 2 * p + 2, at].astype(F32)
            pieces.append(jnp.where(hit, jnp.where(second, m1, m0), 0.0).astype(BF))
        spread = jnp.dot(
            jnp.concatenate(pieces, axis=0), jnp.ones((C, C), BF), preferred_element_type=F32
        )
        m = spread.reshape(4, 8, 16, C)
        maskb[a] = m.astype(BF)
        put_plane(xin, a, pair_plane(feats, a) * m)
        return 0

    lax.fori_loop(0, 8, mask_plane, 0)
    send_faces(0, xin)

    loads[2].wait()
    loads[3].wait()
    build_taps(taps.at[0], w1, False)
    build_taps(taps.at[2], w2, True)
    receive_faces(0, xin)

    def first_done(a, v):
        pre1[a] = v
        s, _ = silu_parts(v)
        put_plane(xhid, a, maskb[a].astype(F32) * (v * s))

    convolve(xin, taps.at[0], first_done)
    send_faces(1, xhid)
    build_taps(taps.at[1], w2, False)
    build_taps(taps.at[3], w1, True)
    loads[4].wait()
    receive_faces(1, xhid)

    def second_done(a, v):
        s, slope = silu_parts(v)
        m = maskb[a].astype(F32)
        unpair_plane(out_s, a, m * (v * s))
        g = pair_plane(cot, a) * m * slope
        put_plane(xg, a, g)
        put_transposed(gt, a, g)

    convolve(xhid, taps.at[1], second_done)
    send_faces(2, xg)
    store_out = pltpu.make_async_copy(out_s, out_h, store_sem.at[0])
    store_out.start()

    weight_grad(xhid, gt, red2.g, scale)
    red2.step(0)
    receive_faces(2, xg)

    def third_done(a, v):
        _, slope = silu_parts(pre1[a])
        g = maskb[a].astype(F32) * slope * v
        put_plane(xhid, a, g)
        put_transposed(gt, a, g)

    convolve(xg, taps.at[2], third_done)
    send_faces(3, xhid)
    red2.step(1)
    store_out.wait()

    weight_grad(xin, gt, red1.g, scale)
    red1.step(0)
    red2.step(2)
    receive_faces(3, xhid)
    red1.step(1)

    def last_done(a, v):
        unpair_plane(out_s, a, maskb[a].astype(F32) * v)

    def between(q):
        for n in range(4):

            @pl.when(q == n)
            def _():
                if n < 3:
                    red2.step(3 + n)
                if n > 0:
                    red1.step(1 + n)

    convolve(xhid, taps.at[3], last_done, between)
    store_gin = pltpu.make_async_copy(out_s, gin_h, store_sem.at[1])
    store_gin.start()
    red2.step(6)
    store_w2 = pltpu.make_async_copy(red2.fin, gw2_h, store_sem.at[2])
    store_w2.start()
    for n in (5, 6):
        red1.step(n)
    store_w1 = pltpu.make_async_copy(red1.fin, gw1_h, store_sem.at[3])
    store_w1.start()
    for n in range(4):
        for c in face_copies(n):
            c.wait_send()
    red1.drain()
    red2.drain()
    store_gin.wait()
    store_w2.wait()
    store_w1.wait()


def body(feats, mask, neighbours, weight_one, weight_two, cotangent):
    bricks, voxels, channels = feats.shape
    scale = 1.0 / math.sqrt(voxels * bricks)
    cube = (bricks, 8, 8, 8, channels)
    field = pltpu.VMEM((4, 10, 10, 16, 3 * C), BF)
    face_buffer = pltpu.VMEM((25, 4, 8, 8, C), BF)
    reduction = [
        pltpu.VMEM((2, 4, 28, 16, C), BF),
        pltpu.VMEM((4, 28, 16, C), BF),
        pltpu.VMEM((4, 28, 16, C), BF),
        pltpu.VMEM((3, 28, 16, C), BF),
        pltpu.VMEM((28, 16, C), BF),
        pltpu.VMEM((3, 7, 16, C), BF),
        pltpu.VMEM((2, 4, 28, 16, C), BF),
        pltpu.SemaphoreType.DMA((14,)),
        pltpu.SemaphoreType.DMA((14,)),
    ]
    anywhere = pl.BlockSpec(memory_space=pl.ANY)
    out, gin, gw1, gw2 = pl.pallas_call(
        functools.partial(kernel, scale),
        out_shape=(
            jax.ShapeDtypeStruct((4, 2, 8, 8, 8, C), BF),
            jax.ShapeDtypeStruct((4, 2, 8, 8, 8, C), BF),
            jax.ShapeDtypeStruct((2, 4, 28, 16, C), BF),
            jax.ShapeDtypeStruct((2, 4, 28, 16, C), BF),
        ),
        in_specs=[
            anywhere, anywhere, pl.BlockSpec(memory_space=pltpu.SMEM), anywhere, anywhere, anywhere,
        ],
        out_specs=(anywhere,) * 4,
        scratch_shapes=[
            pltpu.VMEM(cube, BF),
            pltpu.VMEM((bricks, voxels), jnp.int32),
            pltpu.VMEM((27, C, C), BF),
            pltpu.VMEM((27, C, C), BF),
            pltpu.VMEM(cube, BF),
            pltpu.VMEM((4, 2, 8, 8, 8, C), BF),
            field, field, field,
            pltpu.VMEM((4, 36, C, 2 * C), BF),
            pltpu.VMEM((8, 4, 8, 16, C), BF),
            pltpu.VMEM((8, 4, 8, 16, C), F32),
            pltpu.VMEM((2, 12, C, 2 * C), BF),
            face_buffer, face_buffer, face_buffer, face_buffer,
            pltpu.SemaphoreType.DMA((5,)),
            pltpu.SemaphoreType.DMA((4,)),
            pltpu.SemaphoreType.DMA((4, 2)),
            pltpu.SemaphoreType.DMA((4, 2)),
            *reduction,
            *reduction,
        ],
        compiler_params=pltpu.CompilerParams(
            collective_id=0, has_side_effects=True, vmem_limit_bytes=60 * 2**20
        ),
        name="bricks",
    )(feats.reshape(cube), mask, neighbours, weight_one, weight_two, cotangent.reshape(cube))

    def unfold(g):
        g = g[:, :, :27].transpose(2, 1, 0, 3, 4)
        return g.reshape(27, C, C).astype(F32)

    return (
        out.reshape(bricks, voxels, channels),
        gin.reshape(bricks, voxels, channels),
        unfold(gw1),
        unfold(gw2),
    )


def solution(mesh):
    in_specs = (
        P(("scene", "space"), None, None),
        P(("scene", "space"), None),
        P(("scene", "space"), None),
        P(),
        P(),
        P(("scene", "space"), None, None),
    )
    out_specs = (
        P(("scene", "space"), None, None),
        P(("scene", "space"), None, None),
        P("scene", None, None),
        P("scene", None, None),
    )
    return jax.shard_map(body, mesh=mesh, in_specs=in_specs, out_specs=out_specs, check_vma=False)
```

```python
import functools
import math

import jax
import jax.numpy as jnp
from jax import lax
from jax.experimental import pallas as pl
from jax.experimental.pallas import tpu as pltpu
from jax.sharding import PartitionSpec as P

BF = jnp.bfloat16
F32 = jnp.float32
C = 128
MESH = pl.DeviceIdType.MESH

A0, A7, B0, B7 = 0, 1, 2, 3


def shifted(v):
    row = lax.broadcasted_iota(jnp.int32, v.shape, v.ndim - 1 - 1)
    down = jnp.where(row == 0, 0.0, pltpu.roll(v, 1, v.ndim - 2))
    up = jnp.where(row == 7, 0.0, pltpu.roll(v, 7, v.ndim - 2))
    return down, v, up


def put_plane(x_ref, a, v):
    for k, s in enumerate(shifted(v.reshape(64, 8, C))):
        x_ref[:, 1 + a, 1:9, :, C * k : C * k + C] = s.reshape(4, 8, 16, C).astype(BF)


def pair_plane(ref, a):
    v = ref[:, a].astype(F32).reshape(4, 2, 8, 8, C)
    return jnp.stack([v[:, 0], v[:, 1]], axis=2).reshape(4, 8, 16, C)


def unpair_plane(ref, a, v):
    w = v.reshape(4, 8, 2, 8, C)
    for half in range(2):
        ref[:, half, a] = w[:, :, half].astype(BF)


def take_faces(x_ref, h_ref):
    def body(p, _):
        for half in range(2):
            for face, cells in (
                (A0, x_ref[p, 1, 1:9, :, C : 2 * C]),
                (A7, x_ref[p, 8, 1:9, :, C : 2 * C]),
                (B0, x_ref[p, 1:9, 1, :, C : 2 * C]),
                (B7, x_ref[p, 1:9, 8, :, C : 2 * C]),
            ):
                v = cells.astype(F32).reshape(8, 2, 8, C)
                h_ref[8 + 2 * p + half, face] = v[:, half].astype(BF)
        return 0

    lax.fori_loop(0, 4, body, 0)


def fill_rim(x_ref, h_ref, nbr_ref, first):
    def body(p, _):
        def source(column):
            out = []
            for half in range(2):
                n = nbr_ref[2 * p + half, column]
                out.append(jnp.where(n >= 0, jnp.clip(n - first, 0, 23), 24))
            return out

        def line(column, face):
            i, j = source(column)
            u = h_ref[i, face].astype(F32)
            v = h_ref[j, face].astype(F32)
            w = jnp.stack([u, v], axis=1).reshape(16, 8, C)
            return [s.reshape(8, 16, C).astype(BF) for s in shifted(w)]

        def cell(column, face, where):
            i, j = source(column)
            u = h_ref[i, face, where].astype(F32)
            v = h_ref[j, face, where].astype(F32)
            w = jnp.stack([u, v], axis=0)
            return [s.reshape(16, C).astype(BF) for s in shifted(w)]

        for column, face, where, i, j in (
            (0, A7, 7, 0, 0),
            (2, A7, 0, 0, 9),
            (5, A0, 7, 9, 0),
            (7, A0, 0, 9, 9),
        ):
            for k, s in enumerate(cell(column, face, where)):
                x_ref[p, i, j, :, C * k : C * k + C] = s
        for column, face, i in ((1, A7, 0), (6, A0, 9)):
            for k, s in enumerate(line(column, face)):
                x_ref[p, i, 1:9, :, C * k : C * k + C] = s
        for column, face, j in ((3, B7, 0), (4, B0, 9)):
            for k, s in enumerate(line(column, face)):
                x_ref[p, 1:9, j, :, C * k : C * k + C] = s
        return 0

    lax.fori_loop(0, 4, body, 0)


def build_taps(t_ref, w_ref, flipped):
    def body(t, _):
        zero = jnp.zeros((C, C), BF)
        t_ref[t, :, C:] = zero
        t_ref[27 + t, :, :C] = zero
        for k in range(3):
            if flipped:
                w = w_ref[26 - (9 * k + t)].astype(F32).T.astype(BF)
            else:
                w = w_ref[9 * k + t]
            t_ref[9 * k + t, :, :C] = w
            t_ref[9 * k + 9 + t, :, C:] = w
        return 0

    lax.fori_loop(0, 9, body, 0)


def convolve(x_ref, t_ref, epilogue, between=None):
    def body(q, _):
        windows = [
            x_ref[:, 2 * q + p, k : k + 8].reshape(512, 3 * C) for p in range(4) for k in range(3)
        ]
        total = jnp.dot(
            jnp.concatenate(windows, axis=1),
            t_ref[...].reshape(36 * C, 2 * C),
            preferred_element_type=F32,
        )
        for u in range(2):
            epilogue(2 * q + u, total[:, C * u : C * u + C].reshape(4, 8, 16, C))
        if between is not None:
            between(q)
        return 0

    lax.fori_loop(0, 4, body, 0)


def put_transposed(gt_ref, a, v):
    flat = v.reshape(4, C, C)
    for p in range(4):
        gt_ref[p // 2, a + 2, :, C * (p % 2) : C * (p % 2) + C] = flat[p].T.astype(BF)


def weight_grad(x_ref, gt_ref, columns, scale, store):
    totals = [None] * 3
    for i in range(0, 10, 2):
        low, high = (1 if i == 0 else 0), (2 if i == 8 else 3)
        left = jnp.concatenate(
            [
                gt_ref[h, i + q + low : i + q + high].reshape(C * (high - low), 2 * C)
                for q in range(2)
                for h in range(2)
            ],
            axis=1,
        )
        right = jnp.concatenate(
            [
                jnp.concatenate(
                    [
                        x_ref[:, i + q, c // 3 : c // 3 + 8, :, C * (c % 3) : C * (c % 3) + C]
                        .reshape(512, C)
                        for c in columns
                    ],
                    axis=1,
                )
                for q in range(2)
            ],
            axis=0,
        )
        d = jnp.dot(left, right, preferred_element_type=F32)
        for q in range(low, high):
            part = d[C * (q - low) : C * (q - low) + C]
            totals[q] = part if totals[q] is None else totals[q] + part
    for q in range(3):
        for n, c in enumerate(columns):
            store(q, c, (totals[q][:, C * n : C * n + C] * scale).T)


LEFT_COLUMNS, RIGHT_COLUMNS = range(4), range(4, 9)


def slots_of(taps):
    return (taps + 1) // 2


class Reduction:
    def __init__(self, place, taps, refs):
        self.place = place
        self.taps = taps
        self.g, self.r0, self.s0, self.r1, self.fin, self.send, self.recv = refs

    @staticmethod
    def scratch(taps):
        n = slots_of(taps)
        return [
            pltpu.VMEM((2, 16, n, 8, C), BF),
            pltpu.VMEM((16, n, 8, C), BF),
            pltpu.VMEM((16, n, 8, C), BF),
            pltpu.VMEM((15, n, 8, C), BF),
            pltpu.VMEM((2, 16, n, 8, C), BF),
            pltpu.SemaphoreType.DMA((47,)),
            pltpu.SemaphoreType.DMA((47,)),
        ]

    def clear(self):
        if self.taps % 2:
            self.g[:, 8:, slots_of(self.taps) - 1] = jnp.zeros((2, 8, 8, C), BF)

    def put(self, tap, block):
        for u in range(16):
            n = 8 * tap + u // 2
            self.g[u % 2, n % 16, n // 16] = block[8 * u : 8 * u + 8].astype(BF)

    def copy(self, src, dst, slot, peer):
        return pltpu.make_async_remote_copy(
            src_ref=src,
            dst_ref=dst,
            send_sem=self.send.at[slot],
            recv_sem=self.recv.at[slot],
            device_id={"space": peer},
            device_id_type=MESH,
        )

    def pair(self):
        return self.copy(self.g.at[1 - self.place["core"]], self.r0, 0, self.place["sibling"])

    def scatter(self, d):
        chip = self.place["chip"](d)
        return self.copy(
            self.s0.at[chip], self.r1.at[d - 1], d, 2 * chip + self.place["core"]
        )

    def gather(self, d):
        mine = self.fin.at[self.place["core"], self.place["chip"](0)]
        return self.copy(mine, mine, 15 + d, 2 * self.place["chip"](d) + self.place["core"])

    def forward(self, d):
        one = self.fin.at[self.place["core"], self.place["behind"](d)]
        return self.copy(one, one, 31 + d, self.place["sibling"])

    def step(self, n):
        core, chip = self.place["core"], self.place["chip"]

        def each(low, run):
            def body(d, _):
                run(d)
                return 0

            lax.fori_loop(low, 16, body, 0)

        if n == 0:
            self.pair().start()
        elif n == 1:
            self.pair().wait_recv()

            def add(c):
                self.s0[c] = (self.g[core, c].astype(F32) + self.r0[c].astype(F32)).astype(BF)

            def send(d):
                add(chip(d))
                self.scatter(d).start()

            each(1, send)
            add(chip(0))
        elif n == 2:
            each(1, lambda d: self.scatter(d).wait_recv())
            v = self.s0[chip(0)].astype(F32)
            for d in range(15):
                v = v + self.r1[d].astype(F32)
            self.fin[core, chip(0)] = v.astype(BF)
            each(1, lambda d: self.gather(d).start())
            self.forward(0).start()
        elif n == 3:

            def pass_on(d):
                self.gather(d).wait_recv()
                self.forward(d).start()

            each(1, pass_on)
        else:
            each(0, lambda d: self.forward(d).wait_recv())

    def drain(self):
        self.pair().wait_send()

        def body(d, _):
            self.scatter(d).wait_send()
            self.gather(d).wait_send()
            self.forward(d).wait_send()
            return 0

        self.forward(0).wait_send()
        lax.fori_loop(1, 16, body, 0)


def silu_parts(v):
    s = 1.0 / (1.0 + jnp.exp(-v))
    return s, s * (1.0 + v * (1.0 - s))


def kernel(
    scale,
    feats_h, mask_h, nbr_ref, w1_h, w2_h, cot_h,
    out_h, gin_h, gw2_h, gw1a_h, gw1b_h,
    feats, mask, w1, w2, cot, out_s,
    xin, xhid, xg, taps, maskb, pre1, gt,
    h0, h1, h2, h3,
    load_sem, store_sem, face_send, face_recv,
    *red_refs,
):
    me = lax.axis_index("space")
    n_space = 32
    core = lax.rem(me, 2)
    chip = me // 2
    z = lax.rem(chip, 4)
    y = chip // 4
    right, left = lax.rem(me + 1, n_space), lax.rem(me + n_space - 1, n_space)

    def chip_at(d):
        return 4 * lax.rem(y + d // 4, 4) + lax.rem(z + lax.rem(d, 4), 4)

    def behind(d):
        return 4 * lax.rem(y + 4 - d // 4, 4) + lax.rem(z + 4 - lax.rem(d, 4), 4)

    place = {"core": core, "sibling": me + 1 - 2 * core, "chip": chip_at, "behind": behind}
    first = 8 * (me - 1)
    red2 = Reduction(place, 27, red_refs[:7])
    red1a = Reduction(place, 12, red_refs[7:14])
    red1b = Reduction(place, 15, red_refs[14:])

    loads = [
        pltpu.make_async_copy(src, dst, load_sem.at[i])
        for i, (src, dst) in enumerate(
            ((feats_h, feats), (mask_h, mask), (w1_h, w1), (w2_h, w2), (cot_h, cot))
        )
    ]
    for c in loads:
        c.start()

    barrier = pltpu.get_barrier_semaphore()
    for peer in (left, right):
        pl.semaphore_signal(barrier, inc=1, device_id={"space": peer}, device_id_type=MESH)

    def greet(d, _):
        peer = 2 * chip_at(d) + core
        pl.semaphore_signal(barrier, inc=1, device_id={"space": peer}, device_id_type=MESH)
        return 0

    lax.fori_loop(1, 16, greet, 0)
    pl.semaphore_wait(barrier, 17)

    faces = (h0, h1, h2, h3)

    def face_copies(n):
        h = faces[n]
        return [
            pltpu.make_async_remote_copy(
                src_ref=h.at[pl.ds(8, 8)],
                dst_ref=h.at[pl.ds(at, 8)],
                send_sem=face_send.at[n, side],
                recv_sem=face_recv.at[n, side],
                device_id={"space": peer},
                device_id_type=MESH,
            )
            for side, (at, peer) in enumerate(((0, right), (16, left)))
        ]

    def send_faces(n, x_ref):
        take_faces(x_ref, faces[n])
        for c in face_copies(n):
            c.start()

    def receive_faces(n, x_ref):
        for c in face_copies(n):
            c.wait_recv()
        fill_rim(x_ref, faces[n], nbr_ref, first)

    for h in faces:
        h[24] = jnp.zeros((4, 8, 8, C), BF)
    for red in (red2, red1a, red1b):
        red.clear()
    for side in range(2):
        for a in (0, 1, 10, 11):
            gt[side, a] = jnp.zeros((C, 2 * C), BF)

    loads[1].wait()
    loads[0].wait()

    def mask_plane(a, _):
        row = lax.broadcasted_iota(jnp.int32, (C, C), 0)
        lane = lax.broadcasted_iota(jnp.int32, (C, C), 1)
        hit = lane == lax.rem(a, 2) * 64 + (row // 16) * 8 + lax.rem(row, 8)
        second = lax.rem(row // 8, 2) == 1
        at = pl.ds(pl.multiple_of((a // 2) * C, C), C)
        pieces = []
        for p in range(4):
            m0 = mask[2 * p : 2 * p + 1, at].astype(F32)
            m1 = mask[2 * p + 1 : 2 * p + 2, at].astype(F32)
            pieces.append(jnp.where(hit, jnp.where(second, m1, m0), 0.0).astype(BF))
        spread = jnp.dot(
            jnp.concatenate(pieces, axis=0), jnp.ones((C, C), BF), preferred_element_type=F32
        )
        m = spread.reshape(4, 8, 16, C)
        maskb[a] = m.astype(BF)
        put_plane(xin, a, pair_plane(feats, a) * m)
        return 0

    lax.fori_loop(0, 8, mask_plane, 0)
    send_faces(0, xin)

    loads[2].wait()
    loads[3].wait()
    build_taps(taps.at[0], w1, False)
    build_taps(taps.at[2], w2, True)
    receive_faces(0, xin)

    def first_done(a, v):
        pre1[a] = v
        s, _ = silu_parts(v)
        put_plane(xhid, a, maskb[a].astype(F32) * (v * s))

    convolve(xin, taps.at[0], first_done)
    send_faces(1, xhid)
    build_taps(taps.at[1], w2, False)
    build_taps(taps.at[3], w1, True)
    loads[4].wait()
    receive_faces(1, xhid)

    def second_done(a, v):
        s, slope = silu_parts(v)
        m = maskb[a].astype(F32)
        unpair_plane(out_s, a, m * (v * s))
        g = pair_plane(cot, a) * m * slope
        put_plane(xg, a, g)
        put_transposed(gt, a, g)

    convolve(xhid, taps.at[1], second_done)
    send_faces(2, xg)
    store_out = pltpu.make_async_copy(out_s, out_h, store_sem.at[0])
    store_out.start()

    def put_w2(q, c, block):
        red2.put(9 * (2 - q) + c, block)

    weight_grad(xhid, gt, LEFT_COLUMNS, scale, put_w2)
    weight_grad(xhid, gt, RIGHT_COLUMNS, scale, put_w2)
    red2.step(0)
    receive_faces(2, xg)

    def third_done(a, v):
        _, slope = silu_parts(pre1[a])
        g = maskb[a].astype(F32) * slope * v
        put_plane(xhid, a, g)
        put_transposed(gt, a, g)

    def third_between(q):
        @pl.when(q == 0)
        def _():
            red2.step(1)

    convolve(xg, taps.at[2], third_done, third_between)
    send_faces(3, xhid)
    red2.step(2)
    store_out.wait()

    weight_grad(xin, gt, LEFT_COLUMNS, scale, lambda q, c, v: red1a.put(4 * (2 - q) + c, v))
    red1a.step(0)
    weight_grad(xin, gt, RIGHT_COLUMNS, scale, lambda q, c, v: red1b.put(5 * (2 - q) + c - 4, v))
    red1b.step(0)
    red1a.step(1)
    red2.step(3)
    receive_faces(3, xhid)
    red1b.step(1)

    def last_done(a, v):
        unpair_plane(out_s, a, maskb[a].astype(F32) * v)

    def last_between(q):
        @pl.when(q == 1)
        def _():
            red1a.step(2)

        @pl.when(q == 2)
        def _():
            red1b.step(2)

        @pl.when(q == 3)
        def _():
            red2.step(4)
            red1a.step(3)

    convolve(xhid, taps.at[3], last_done, last_between)
    stores = [
        pltpu.make_async_copy(src, dst, store_sem.at[1 + i])
        for i, (src, dst) in enumerate(
            ((out_s, gin_h), (red2.fin, gw2_h), (red1a.fin, gw1a_h), (red1b.fin, gw1b_h))
        )
    ]
    stores[0].start()
    stores[1].start()
    red1b.step(3)
    red1a.step(4)
    stores[2].start()
    red1b.step(4)
    stores[3].start()
    for n in range(4):
        for c in face_copies(n):
            c.wait_send()
    for red in (red2, red1a, red1b):
        red.drain()
    for c in stores:
        c.wait()


def finish(
    out_t, gin_t, gw2_t, gw1a_t, gw1b_t,
    out_h, gin_h, gw1_h, gw2_h,
    fin2, fin1a, fin1b, w1, w2, sem,
):
    copies = [
        pltpu.make_async_copy(src, dst, sem.at[i])
        for i, (src, dst) in enumerate(
            ((gw2_t, fin2), (gw1a_t, fin1a), (gw1b_t, fin1b), (out_t, out_h), (gin_t, gin_h),
             (w2, gw2_h), (w1, gw1_h))
        )
    ]
    for c in copies[:5]:
        c.start()

    def order(fin, tap, dst, to):
        for u in range(16):
            n = 8 * tap + u // 2
            dst[to, 8 * u : 8 * u + 8] = fin[u % 2, n % 16, n // 16].astype(F32)

    copies[0].wait()
    for tap in range(27):
        order(fin2, tap, w2, tap)
    copies[5].start()
    copies[1].wait()
    copies[2].wait()
    for k in range(3):
        for c in LEFT_COLUMNS:
            order(fin1a, 4 * k + c, w1, 9 * k + c)
        for c in RIGHT_COLUMNS:
            order(fin1b, 5 * k + c - 4, w1, 9 * k + c)
    copies[6].start()
    for c in copies[3:]:
        c.wait()


def body(feats, mask, neighbours, weight_one, weight_two, cotangent):
    bricks, voxels, channels = feats.shape
    scale = 1.0 / math.sqrt(voxels * bricks)
    cube = (bricks, 8, 8, 8, channels)
    field = pltpu.VMEM((4, 10, 10, 16, 3 * C), BF)
    face_buffer = pltpu.VMEM((25, 4, 8, 8, C), BF)
    anywhere = pl.BlockSpec(memory_space=pl.ANY)
    parts = [
        jax.ShapeDtypeStruct((4, 2, 8, 8, 8, C), BF),
        jax.ShapeDtypeStruct((4, 2, 8, 8, 8, C), BF),
        *(jax.ShapeDtypeStruct((2, 16, slots_of(n), 8, C), BF) for n in (27, 12, 15)),
    ]
    left_over = pl.pallas_call(
        functools.partial(kernel, scale),
        out_shape=tuple(parts),
        in_specs=[
            anywhere, anywhere, pl.BlockSpec(memory_space=pltpu.SMEM), anywhere, anywhere, anywhere,
        ],
        out_specs=(anywhere,) * 5,
        scratch_shapes=[
            pltpu.VMEM(cube, BF),
            pltpu.VMEM((bricks, voxels), jnp.int32),
            pltpu.VMEM((27, C, C), BF),
            pltpu.VMEM((27, C, C), BF),
            pltpu.VMEM(cube, BF),
            pltpu.VMEM((4, 2, 8, 8, 8, C), BF),
            field, field, field,
            pltpu.VMEM((4, 36, C, 2 * C), BF),
            pltpu.VMEM((8, 4, 8, 16, C), BF),
            pltpu.VMEM((8, 4, 8, 16, C), F32),
            pltpu.VMEM((2, 12, C, 2 * C), BF),
            face_buffer, face_buffer, face_buffer, face_buffer,
            pltpu.SemaphoreType.DMA((5,)),
            pltpu.SemaphoreType.DMA((5,)),
            pltpu.SemaphoreType.DMA((4, 2)),
            pltpu.SemaphoreType.DMA((4, 2)),
            *Reduction.scratch(27),
            *Reduction.scratch(12),
            *Reduction.scratch(15),
        ],
        compiler_params=pltpu.CompilerParams(
            collective_id=0, has_side_effects=True, vmem_limit_bytes=60 * 2**20
        ),
        name="bricks",
    )(feats.reshape(cube), mask, neighbours, weight_one, weight_two, cotangent.reshape(cube))

    out, gin, gw1, gw2 = pl.pallas_call(
        finish,
        out_shape=(
            *parts[:2],
            jax.ShapeDtypeStruct((27, C, C), F32),
            jax.ShapeDtypeStruct((27, C, C), F32),
        ),
        in_specs=[anywhere] * 5,
        out_specs=(anywhere,) * 4,
        scratch_shapes=[
            *(pltpu.VMEM(p.shape, BF) for p in parts[2:]),
            pltpu.VMEM((27, C, C), F32),
            pltpu.VMEM((27, C, C), F32),
            pltpu.SemaphoreType.DMA((7,)),
        ],
        name="outputs",
    )(*left_over)
    return (
        out.reshape(bricks, voxels, channels),
        gin.reshape(bricks, voxels, channels),
        gw1,
        gw2,
    )


def solution(mesh):
    in_specs = (
        P(("scene", "space"), None, None),
        P(("scene", "space"), None),
        P(("scene", "space"), None),
        P(),
        P(),
        P(("scene", "space"), None, None),
    )
    out_specs = (
        P(("scene", "space"), None, None),
        P(("scene", "space"), None, None),
        P("scene", None, None),
        P("scene", None, None),
    )
    return jax.shard_map(body, mesh=mesh, in_specs=in_specs, out_specs=out_specs, check_vma=False)
```

```python
import functools
import math

import jax
import jax.numpy as jnp
from jax import lax
from jax.experimental import pallas as pl
from jax.experimental.pallas import tpu as pltpu
from jax.sharding import PartitionSpec as P

BF = jnp.bfloat16
F32 = jnp.float32
C = 128
MESH = pl.DeviceIdType.MESH


def shifted(v):
    row = lax.broadcasted_iota(jnp.int32, v.shape, v.ndim - 1 - 1)
    down = jnp.where(row == 0, 0.0, pltpu.roll(v, 1, v.ndim - 2))
    up = jnp.where(row == 7, 0.0, pltpu.roll(v, 7, v.ndim - 2))
    return down, v, up


def put_plane(x_ref, a, v):
    for k, s in enumerate(shifted(v.reshape(64, 8, C))):
        x_ref[:, 1 + a, 1:9, :, C * k : C * k + C] = s.reshape(4, 8, 16, C).astype(BF)


def pair_plane(ref, a):
    v = ref[:, a].astype(F32).reshape(4, 2, 8, 8, C)
    return jnp.stack([v[:, 0], v[:, 1]], axis=2).reshape(4, 8, 16, C)


def unpair_plane(ref, a, v):
    w = v.reshape(4, 8, 2, 8, C)
    for half in range(2):
        ref[:, half, a] = w[:, :, half].astype(BF)


def keep_faces(outer, inner, a, v):
    w = v.reshape(4, 8, 2, 8, C)

    @pl.when((a == 0) | (a == 7))
    def _():
        for p in range(4):
            for half in range(2):
                outer[a // 7, 8 + 2 * p + half] = w[p, :, half].astype(BF)

    @pl.when((a > 0) & (a < 7))
    def _():
        for p in range(4):
            for half in range(2):
                inner[a - 1, 8 + 2 * p + half, 0] = w[p, 0, half].astype(BF)
                inner[a - 1, 8 + 2 * p + half, 1] = w[p, 7, half].astype(BF)


def fill_rim(x_ref, faces, nbr_ref, first):
    outer, inner = faces

    def body(p, _):
        def source(column):
            out = []
            for half in range(2):
                n = nbr_ref[2 * p + half, column]
                out.append(jnp.where(n >= 0, jnp.clip(n - first, 0, 23), 24))
            return out

        def cell(x, y, i, j):
            w = jnp.stack([x.astype(F32), y.astype(F32)], axis=0)
            for k, s in enumerate(shifted(w)):
                x_ref[p, i, j, :, C * k : C * k + C] = s.reshape(16, C).astype(BF)

        for column, side, where, i, j in (
            (0, 1, 7, 0, 0), (2, 1, 0, 0, 9), (5, 0, 7, 9, 0), (7, 0, 0, 9, 9),
        ):
            m, n = source(column)
            cell(outer[side, m, where], outer[side, n, where], i, j)
        for column, side, i in ((1, 1, 0), (6, 0, 9)):
            m, n = source(column)
            u, v = outer[side, m].astype(F32), outer[side, n].astype(F32)
            w = jnp.stack([u, v], axis=1).reshape(16, 8, C)
            for k, s in enumerate(shifted(w)):
                x_ref[p, i, 1:9, :, C * k : C * k + C] = s.reshape(8, 16, C).astype(BF)
        for column, end, j in ((3, 1, 0), (4, 0, 9)):
            m, n = source(column)
            cell(outer[0, m, 7 * end], outer[0, n, 7 * end], 1, j)
            for a in range(1, 7):
                cell(inner[a - 1, m, end], inner[a - 1, n, end], 1 + a, j)
            cell(outer[1, m, 7 * end], outer[1, n, 7 * end], 8, j)
        return 0

    lax.fori_loop(0, 4, body, 0)


def build_taps(t_ref, w_ref, flipped):
    def body(t, _):
        zero = jnp.zeros((C, C), BF)
        t_ref[t, :, C:] = zero
        t_ref[27 + t, :, :C] = zero
        for k in range(3):
            if flipped:
                w = w_ref[26 - (9 * k + t)].astype(F32).T.astype(BF)
            else:
                w = w_ref[9 * k + t]
            t_ref[9 * k + t, :, :C] = w
            t_ref[9 * k + 9 + t, :, C:] = w
        return 0

    lax.fori_loop(0, 9, body, 0)


def convolve(x_ref, t_ref, epilogue, between=None):
    def body(t, _):
        q = jnp.where(t == 0, 0, jnp.where(t == 1, 3, t - 1))
        windows = [
            x_ref[:, 2 * q + p, k : k + 8].reshape(512, 3 * C) for p in range(4) for k in range(3)
        ]
        total = jnp.dot(
            jnp.concatenate(windows, axis=1),
            t_ref[...].reshape(36 * C, 2 * C),
            preferred_element_type=F32,
        )
        for u in range(2):
            epilogue(2 * q + u, total[:, C * u : C * u + C].reshape(4, 8, 16, C))
        if between is not None:
            between(t)
        return 0

    lax.fori_loop(0, 4, body, 0)


def put_transposed(gt_ref, a, v):
    flat = v.reshape(4, C, C)
    for p in range(4):
        gt_ref[p // 2, a + 2, :, C * (p % 2) : C * (p % 2) + C] = flat[p].T.astype(BF)


def weight_grad(x_ref, gt_ref, columns, scale, store):
    totals = [None] * 3
    for i in range(0, 10, 2):
        low, high = (1 if i == 0 else 0), (2 if i == 8 else 3)
        left = jnp.concatenate(
            [
                gt_ref[h, i + q + low : i + q + high].reshape(C * (high - low), 2 * C)
                for q in range(2)
                for h in range(2)
            ],
            axis=1,
        )
        right = jnp.concatenate(
            [
                jnp.concatenate(
                    [
                        x_ref[:, i + q, c // 3 : c // 3 + 8, :, C * (c % 3) : C * (c % 3) + C]
                        .reshape(512, C)
                        for c in columns
                    ],
                    axis=1,
                )
                for q in range(2)
            ],
            axis=0,
        )
        d = jnp.dot(left, right, preferred_element_type=F32)
        for q in range(low, high):
            part = d[C * (q - low) : C * (q - low) + C]
            totals[q] = part if totals[q] is None else totals[q] + part
    for q in range(3):
        for n, c in enumerate(columns):
            store(q, c, (totals[q][:, C * n : C * n + C] * scale).T)


LEFT_COLUMNS, RIGHT_COLUMNS = range(4), range(4, 9)


def slots_of(taps):
    return (taps + 1) // 2


class Reduction:
    def __init__(self, place, taps, refs):
        self.place = place
        self.taps = taps
        self.g, self.r0, self.s0, self.r1, self.fin, self.send, self.recv = refs

    @staticmethod
    def scratch(taps):
        n = slots_of(taps)
        return [
            pltpu.VMEM((2, 16, n, 8, C), BF),
            pltpu.VMEM((16, n, 8, C), BF),
            pltpu.VMEM((16, n, 8, C), BF),
            pltpu.VMEM((15, n, 8, C), BF),
            pltpu.VMEM((2, 16, n, 8, C), BF),
            pltpu.SemaphoreType.DMA((47,)),
            pltpu.SemaphoreType.DMA((47,)),
        ]

    def clear(self):
        if self.taps % 2:
            self.g[:, 8:, slots_of(self.taps) - 1] = jnp.zeros((2, 8, 8, C), BF)

    def put(self, tap, block):
        for u in range(16):
            n = 8 * tap + u // 2
            self.g[u % 2, n % 16, n // 16] = block[8 * u : 8 * u + 8].astype(BF)

    def copy(self, src, dst, slot, peer):
        return pltpu.make_async_remote_copy(
            src_ref=src,
            dst_ref=dst,
            send_sem=self.send.at[slot],
            recv_sem=self.recv.at[slot],
            device_id={"space": peer},
            device_id_type=MESH,
        )

    def pair(self):
        return self.copy(self.g.at[1 - self.place["core"]], self.r0, 0, self.place["sibling"])

    def scatter(self, d):
        chip = self.place["chip"](d)
        return self.copy(
            self.s0.at[chip], self.r1.at[d - 1], d, 2 * chip + self.place["core"]
        )

    def gather(self, d):
        mine = self.fin.at[self.place["core"], self.place["chip"](0)]
        return self.copy(mine, mine, 15 + d, 2 * self.place["chip"](d) + self.place["core"])

    def forward(self, d):
        one = self.fin.at[self.place["core"], self.place["behind"](d)]
        return self.copy(one, one, 31 + d, self.place["sibling"])

    def step(self, n):
        core, chip = self.place["core"], self.place["chip"]

        def each(low, run):
            def body(d, _):
                run(d)
                return 0

            lax.fori_loop(low, 16, body, 0)

        if n == 0:
            self.pair().start()
        elif n == 1:
            self.pair().wait_recv()

            def add(c):
                self.s0[c] = (self.g[core, c].astype(F32) + self.r0[c].astype(F32)).astype(BF)

            def send(d):
                add(chip(d))
                self.scatter(d).start()

            each(1, send)
            add(chip(0))
        elif n == 2:
            each(1, lambda d: self.scatter(d).wait_recv())
            v = self.s0[chip(0)].astype(F32)
            for d in range(15):
                v = v + self.r1[d].astype(F32)
            self.fin[core, chip(0)] = v.astype(BF)
            each(1, lambda d: self.gather(d).start())
            self.forward(0).start()
        elif n == 3:

            def pass_on(d):
                self.gather(d).wait_recv()
                self.forward(d).start()

            each(1, pass_on)
        else:
            each(0, lambda d: self.forward(d).wait_recv())

    def drain(self):
        self.pair().wait_send()

        def body(d, _):
            self.scatter(d).wait_send()
            self.gather(d).wait_send()
            self.forward(d).wait_send()
            return 0

        self.forward(0).wait_send()
        lax.fori_loop(1, 16, body, 0)


def silu_parts(v):
    s = 1.0 / (1.0 + jnp.exp(-v))
    return s, s * (1.0 + v * (1.0 - s))


def kernel(
    scale,
    feats_h, mask_h, nbr_ref, w1_h, w2_h, cot_h,
    out_h, gin_h, gw2_h, gw1a_h, gw1b_h,
    feats, mask, w1, w2, cot, out_s,
    xin, xhid, xg, taps, maskb, pre1, gt,
    o0, o1, o2, o3, i0, i1, i2, i3,
    load_sem, store_sem, face_send, face_recv,
    *red_refs,
):
    me = lax.axis_index("space")
    n_space = 32
    core = lax.rem(me, 2)
    chip = me // 2
    z = lax.rem(chip, 4)
    y = chip // 4
    right, left = lax.rem(me + 1, n_space), lax.rem(me + n_space - 1, n_space)

    def chip_at(d):
        return 4 * lax.rem(y + d // 4, 4) + lax.rem(z + lax.rem(d, 4), 4)

    def behind(d):
        return 4 * lax.rem(y + 4 - d // 4, 4) + lax.rem(z + 4 - lax.rem(d, 4), 4)

    place = {"core": core, "sibling": me + 1 - 2 * core, "chip": chip_at, "behind": behind}
    first = 8 * (me - 1)
    red2 = Reduction(place, 27, red_refs[:7])
    red1a = Reduction(place, 12, red_refs[7:14])
    red1b = Reduction(place, 15, red_refs[14:])

    loads = [
        pltpu.make_async_copy(src, dst, load_sem.at[i])
        for i, (src, dst) in enumerate(
            ((feats_h, feats), (mask_h, mask), (w1_h, w1), (w2_h, w2), (cot_h, cot))
        )
    ]
    for c in loads:
        c.start()

    barrier = pltpu.get_barrier_semaphore()
    for peer in (left, right):
        pl.semaphore_signal(barrier, inc=1, device_id={"space": peer}, device_id_type=MESH)

    def greet(d, _):
        peer = 2 * chip_at(d) + core
        pl.semaphore_signal(barrier, inc=1, device_id={"space": peer}, device_id_type=MESH)
        return 0

    lax.fori_loop(1, 16, greet, 0)
    pl.semaphore_wait(barrier, 17)

    faces = ((o0, i0), (o1, i1), (o2, i2), (o3, i3))

    def plane_copies(n, ref, slab, a):
        return [
            pltpu.make_async_remote_copy(
                src_ref=ref.at[slab, pl.ds(8, 8)],
                dst_ref=ref.at[slab, pl.ds(at, 8)],
                send_sem=face_send.at[n, side, a],
                recv_sem=face_recv.at[n, side, a],
                device_id={"space": peer},
                device_id_type=MESH,
            )
            for side, (at, peer) in enumerate(((0, right), (16, left)))
        ]

    def send_plane(n, a, v):
        outer, inner = faces[n]
        keep_faces(outer, inner, a, v)

        @pl.when((a == 0) | (a == 7))
        def _():
            for c in plane_copies(n, outer, a // 7, a):
                c.start()

        @pl.when((a > 0) & (a < 7))
        def _():
            for c in plane_copies(n, inner, a - 1, a):
                c.start()

    def face_copies(n):
        outer, inner = faces[n]
        copies = []
        for a in range(8):
            if a in (0, 7):
                copies += plane_copies(n, outer, a // 7, a)
            else:
                copies += plane_copies(n, inner, a - 1, a)
        return copies

    def receive_faces(n, x_ref):
        for c in face_copies(n):
            c.wait_recv()
        fill_rim(x_ref, faces[n], nbr_ref, first)

    for outer, inner in faces:
        for side in range(2):
            outer[side, 24] = jnp.zeros((8, 8, C), BF)
        for a in range(6):
            inner[a, 24] = jnp.zeros((2, 8, C), BF)
    for red in (red2, red1a, red1b):
        red.clear()
    for side in range(2):
        for a in (0, 1, 10, 11):
            gt[side, a] = jnp.zeros((C, 2 * C), BF)

    loads[1].wait()
    loads[0].wait()

    def mask_plane(t, _):
        a = jnp.where(t == 0, 0, jnp.where(t == 1, 7, t - 1))
        row = lax.broadcasted_iota(jnp.int32, (C, C), 0)
        lane = lax.broadcasted_iota(jnp.int32, (C, C), 1)
        hit = lane == lax.rem(a, 2) * 64 + (row // 16) * 8 + lax.rem(row, 8)
        second = lax.rem(row // 8, 2) == 1
        at = pl.ds(pl.multiple_of((a // 2) * C, C), C)
        pieces = []
        for p in range(4):
            m0 = mask[2 * p : 2 * p + 1, at].astype(F32)
            m1 = mask[2 * p + 1 : 2 * p + 2, at].astype(F32)
            pieces.append(jnp.where(hit, jnp.where(second, m1, m0), 0.0).astype(BF))
        spread = jnp.dot(
            jnp.concatenate(pieces, axis=0), jnp.ones((C, C), BF), preferred_element_type=F32
        )
        m = spread.reshape(4, 8, 16, C)
        maskb[a] = m.astype(BF)
        v = pair_plane(feats, a) * m
        send_plane(0, a, v)
        put_plane(xin, a, v)
        return 0

    lax.fori_loop(0, 8, mask_plane, 0)

    loads[2].wait()
    loads[3].wait()
    build_taps(taps.at[0], w1, False)
    build_taps(taps.at[2], w2, True)
    receive_faces(0, xin)

    def first_done(a, v):
        pre1[a] = v
        s, _ = silu_parts(v)
        h = maskb[a].astype(F32) * (v * s)
        send_plane(1, a, h)
        put_plane(xhid, a, h)

    convolve(xin, taps.at[0], first_done)
    build_taps(taps.at[1], w2, False)
    build_taps(taps.at[3], w1, True)
    loads[4].wait()
    receive_faces(1, xhid)

    def second_done(a, v):
        s, slope = silu_parts(v)
        m = maskb[a].astype(F32)
        unpair_plane(out_s, a, m * (v * s))
        g = pair_plane(cot, a) * m * slope
        send_plane(2, a, g)
        put_plane(xg, a, g)
        put_transposed(gt, a, g)

    convolve(xhid, taps.at[1], second_done)
    store_out = pltpu.make_async_copy(out_s, out_h, store_sem.at[0])
    store_out.start()

    def put_w2(q, c, block):
        red2.put(9 * (2 - q) + c, block)

    weight_grad(xhid, gt, LEFT_COLUMNS, scale, put_w2)
    weight_grad(xhid, gt, RIGHT_COLUMNS, scale, put_w2)
    red2.step(0)
    receive_faces(2, xg)

    def third_done(a, v):
        _, slope = silu_parts(pre1[a])
        g = maskb[a].astype(F32) * slope * v
        send_plane(3, a, g)
        put_plane(xhid, a, g)
        put_transposed(gt, a, g)

    def third_between(q):
        @pl.when(q == 1)
        def _():
            red2.step(1)

    convolve(xg, taps.at[2], third_done, third_between)
    store_out.wait()

    weight_grad(xin, gt, LEFT_COLUMNS, scale, lambda q, c, v: red1a.put(4 * (2 - q) + c, v))
    red1a.step(0)
    weight_grad(xin, gt, RIGHT_COLUMNS, scale, lambda q, c, v: red1b.put(5 * (2 - q) + c - 4, v))
    red1b.step(0)
    red1a.step(1)
    red2.step(2)
    receive_faces(3, xhid)
    red1b.step(1)

    def last_done(a, v):
        unpair_plane(out_s, a, maskb[a].astype(F32) * v)

    def last_between(q):
        @pl.when(q == 2)
        def _():
            red1a.step(2)

        @pl.when(q == 3)
        def _():
            red1b.step(2)

    convolve(xhid, taps.at[3], last_done, last_between)
    stores = [
        pltpu.make_async_copy(src, dst, store_sem.at[1 + i])
        for i, (src, dst) in enumerate(
            ((out_s, gin_h), (red2.fin, gw2_h), (red1a.fin, gw1a_h), (red1b.fin, gw1b_h))
        )
    ]
    stores[0].start()
    red2.step(3)
    red1a.step(3)
    red2.step(4)
    stores[1].start()
    red1b.step(3)
    red1a.step(4)
    stores[2].start()
    red1b.step(4)
    stores[3].start()
    for n in range(4):
        for c in face_copies(n):
            c.wait_send()
    for red in (red2, red1a, red1b):
        red.drain()
    for c in stores:
        c.wait()


def finish(
    out_t, gin_t, gw2_t, gw1a_t, gw1b_t,
    out_h, gin_h, gw1_h, gw2_h,
    fin2, fin1a, fin1b, w1, w2, out_s, gin_s, sem,
):
    pairs = ((gw2_t, fin2), (gw1a_t, fin1a), (gw1b_t, fin1b), (out_t, out_s), (gin_t, gin_s))
    reads = [pltpu.make_async_copy(src, dst, sem.at[i]) for i, (src, dst) in enumerate(pairs)]
    pairs = ((w2, gw2_h), (w1, gw1_h), (out_s, out_h), (gin_s, gin_h))
    writes = [pltpu.make_async_copy(src, dst, sem.at[5 + i]) for i, (src, dst) in enumerate(pairs)]
    for c in reads:
        c.start()

    def order(fin, tap, dst, to):
        for u in range(16):
            n = 8 * tap + u // 2
            dst[to, 8 * u : 8 * u + 8] = fin[u % 2, n % 16, n // 16].astype(F32)

    reads[0].wait()
    for tap in range(27):
        order(fin2, tap, w2, tap)
    writes[0].start()
    reads[1].wait()
    reads[2].wait()
    for k in range(3):
        for c in LEFT_COLUMNS:
            order(fin1a, 4 * k + c, w1, 9 * k + c)
        for c in RIGHT_COLUMNS:
            order(fin1b, 5 * k + c - 4, w1, 9 * k + c)
    writes[1].start()
    for i in (3, 4):
        reads[i].wait()
        writes[i - 1].start()
    for c in writes:
        c.wait()


def body(feats, mask, neighbours, weight_one, weight_two, cotangent):
    bricks, voxels, channels = feats.shape
    scale = 1.0 / math.sqrt(voxels * bricks)
    cube = (bricks, 8, 8, 8, channels)
    field = pltpu.VMEM((4, 10, 10, 16, 3 * C), BF)
    outer, inner = pltpu.VMEM((2, 25, 8, 8, C), BF), pltpu.VMEM((6, 25, 2, 8, C), BF)
    anywhere = pl.BlockSpec(memory_space=pl.ANY)
    parts = [
        jax.ShapeDtypeStruct((4, 2, 8, 8, 8, C), BF),
        jax.ShapeDtypeStruct((4, 2, 8, 8, 8, C), BF),
        *(jax.ShapeDtypeStruct((2, 16, slots_of(n), 8, C), BF) for n in (27, 12, 15)),
    ]
    left_over = pl.pallas_call(
        functools.partial(kernel, scale),
        out_shape=tuple(parts),
        in_specs=[
            anywhere, anywhere, pl.BlockSpec(memory_space=pltpu.SMEM), anywhere, anywhere, anywhere,
        ],
        out_specs=(anywhere,) * 5,
        scratch_shapes=[
            pltpu.VMEM(cube, BF),
            pltpu.VMEM((bricks, voxels), jnp.int32),
            pltpu.VMEM((27, C, C), BF),
            pltpu.VMEM((27, C, C), BF),
            pltpu.VMEM(cube, BF),
            pltpu.VMEM((4, 2, 8, 8, 8, C), BF),
            field, field, field,
            pltpu.VMEM((4, 36, C, 2 * C), BF),
            pltpu.VMEM((8, 4, 8, 16, C), BF),
            pltpu.VMEM((8, 4, 8, 16, C), F32),
            pltpu.VMEM((2, 12, C, 2 * C), BF),
            *[outer] * 4,
            *[inner] * 4,
            pltpu.SemaphoreType.DMA((5,)),
            pltpu.SemaphoreType.DMA((5,)),
            pltpu.SemaphoreType.DMA((4, 2, 8)),
            pltpu.SemaphoreType.DMA((4, 2, 8)),
            *Reduction.scratch(27),
            *Reduction.scratch(12),
            *Reduction.scratch(15),
        ],
        compiler_params=pltpu.CompilerParams(
            collective_id=0, has_side_effects=True, vmem_limit_bytes=60 * 2**20
        ),
        name="bricks",
    )(feats.reshape(cube), mask, neighbours, weight_one, weight_two, cotangent.reshape(cube))

    out, gin, gw1, gw2 = pl.pallas_call(
        finish,
        out_shape=(
            *parts[:2],
            jax.ShapeDtypeStruct((27, C, C), F32),
            jax.ShapeDtypeStruct((27, C, C), F32),
        ),
        in_specs=[anywhere] * 5,
        out_specs=(anywhere,) * 4,
        scratch_shapes=[
            *(pltpu.VMEM(p.shape, BF) for p in parts[2:]),
            pltpu.VMEM((27, C, C), F32),
            pltpu.VMEM((27, C, C), F32),
            pltpu.VMEM(parts[0].shape, BF),
            pltpu.VMEM(parts[1].shape, BF),
            pltpu.SemaphoreType.DMA((9,)),
        ],
        name="outputs",
    )(*left_over)
    return (
        out.reshape(bricks, voxels, channels),
        gin.reshape(bricks, voxels, channels),
        gw1,
        gw2,
    )


def solution(mesh):
    in_specs = (
        P(("scene", "space"), None, None),
        P(("scene", "space"), None),
        P(("scene", "space"), None),
        P(),
        P(),
        P(("scene", "space"), None, None),
    )
    out_specs = (
        P(("scene", "space"), None, None),
        P(("scene", "space"), None, None),
        P("scene", None, None),
        P("scene", None, None),
    )
    return jax.shard_map(body, mesh=mesh, in_specs=in_specs, out_specs=out_specs, check_vma=False)
```

```python
import functools
import math

import jax
import jax.numpy as jnp
from jax import lax
from jax.experimental import pallas as pl
from jax.experimental.pallas import tpu as pltpu
from jax.sharding import PartitionSpec as P

BF = jnp.bfloat16
F32 = jnp.float32
C = 128
MESH = pl.DeviceIdType.MESH


def shifted(v):
    row = lax.broadcasted_iota(jnp.int32, v.shape, v.ndim - 1 - 1)
    down = jnp.where(row == 0, 0.0, pltpu.roll(v, 1, v.ndim - 2))
    up = jnp.where(row == 7, 0.0, pltpu.roll(v, 7, v.ndim - 2))
    return down, v, up


def put_plane(x_ref, a, v):
    for k, s in enumerate(shifted(v.reshape(64, 8, C))):
        x_ref[:, 1 + a, 1:9, :, C * k : C * k + C] = s.reshape(4, 8, 16, C).astype(BF)


def pair_plane(ref, a):
    v = ref[:, a].astype(F32).reshape(4, 2, 8, 8, C)
    return jnp.stack([v[:, 0], v[:, 1]], axis=2).reshape(4, 8, 16, C)


def unpair_plane(ref, a, v):
    w = v.reshape(4, 8, 2, 8, C)
    for half in range(2):
        ref[:, half, a] = w[:, :, half].astype(BF)


def when_outer(a, run_outer, run_inner):
    if isinstance(a, int):
        run_outer() if a in (0, 7) else run_inner()
        return
    pl.when((a == 0) | (a == 7))(run_outer)
    pl.when((a > 0) & (a < 7))(run_inner)


def keep_faces(outer, inner, a, v):
    w = v.reshape(4, 8, 2, 8, C)

    def whole():
        for p in range(4):
            for half in range(2):
                outer[a // 7, 8 + 2 * p + half] = w[p, :, half].astype(BF)

    def ends():
        for p in range(4):
            for half in range(2):
                inner[a - 1, 8 + 2 * p + half, 0] = w[p, 0, half].astype(BF)
                inner[a - 1, 8 + 2 * p + half, 1] = w[p, 7, half].astype(BF)

    when_outer(a, whole, ends)


def fill_rim(x_ref, faces, nbr_ref, first):
    outer, inner = faces

    def body(p, _):
        def source(column):
            out = []
            for half in range(2):
                n = nbr_ref[2 * p + half, column]
                out.append(jnp.where(n >= 0, jnp.clip(n - first, 0, 23), 24))
            return out

        def cell(x, y, i, j):
            w = jnp.stack([x.astype(F32), y.astype(F32)], axis=0)
            for k, s in enumerate(shifted(w)):
                x_ref[p, i, j, :, C * k : C * k + C] = s.reshape(16, C).astype(BF)

        for column, side, where, i, j in (
            (0, 1, 7, 0, 0), (2, 1, 0, 0, 9), (5, 0, 7, 9, 0), (7, 0, 0, 9, 9),
        ):
            m, n = source(column)
            cell(outer[side, m, where], outer[side, n, where], i, j)
        for column, side, i in ((1, 1, 0), (6, 0, 9)):
            m, n = source(column)
            u, v = outer[side, m].astype(F32), outer[side, n].astype(F32)
            w = jnp.stack([u, v], axis=1).reshape(16, 8, C)
            for k, s in enumerate(shifted(w)):
                x_ref[p, i, 1:9, :, C * k : C * k + C] = s.reshape(8, 16, C).astype(BF)
        for column, end, j in ((3, 1, 0), (4, 0, 9)):
            m, n = source(column)
            cell(outer[0, m, 7 * end], outer[0, n, 7 * end], 1, j)
            for a in range(1, 7):
                cell(inner[a - 1, m, end], inner[a - 1, n, end], 1 + a, j)
            cell(outer[1, m, 7 * end], outer[1, n, 7 * end], 8, j)
        return 0

    lax.fori_loop(0, 4, body, 0)


def build_taps(t_ref, w_ref, flipped):
    def body(t, _):
        zero = jnp.zeros((C, C), BF)
        t_ref[t, :, C:] = zero
        t_ref[27 + t, :, :C] = zero
        for k in range(3):
            if flipped:
                w = w_ref[26 - (9 * k + t)].astype(F32).T.astype(BF)
            else:
                w = w_ref[9 * k + t]
            t_ref[9 * k + t, :, :C] = w
            t_ref[9 * k + 9 + t, :, C:] = w
        return 0

    lax.fori_loop(0, 9, body, 0)


def convolve(x_ref, t_ref, epilogue, between=None):
    def body(t, _):
        q = jnp.where(t == 0, 0, jnp.where(t == 1, 3, t - 1))
        windows = [
            x_ref[:, 2 * q + p, k : k + 8].reshape(512, 3 * C) for p in range(4) for k in range(3)
        ]
        total = jnp.dot(
            jnp.concatenate(windows, axis=1),
            t_ref[...].reshape(36 * C, 2 * C),
            preferred_element_type=F32,
        )
        for u in range(2):
            epilogue(2 * q + u, total[:, C * u : C * u + C].reshape(4, 8, 16, C))
        if between is not None:
            between(t)
        return 0

    lax.fori_loop(0, 4, body, 0)


def convolve_split(x_ref, t_ref, inner_ref, arrive, epilogue):
    def pair(q):
        windows = [
            x_ref[:, 2 * q + p, k : k + 8].reshape(512, 3 * C) for p in range(4) for k in range(3)
        ]
        total = jnp.dot(
            jnp.concatenate(windows, axis=1),
            t_ref[...].reshape(36 * C, 2 * C),
            preferred_element_type=F32,
        )
        return [total[:, C * u : C * u + C].reshape(4, 8, 16, C) for u in range(2)]

    def early(t, _):
        for u, v in enumerate(pair(1 + t)):
            inner_ref[2 * t + u] = v
        return 0

    lax.fori_loop(0, 2, early, 0)
    arrive()
    for end, column, k in ((0, 0, 0), (7, 9, 2)):
        left = [x_ref[:, 2 + p : 6 + p, column].reshape(256, 3 * C) for p in range(3)]
        right = [t_ref[9 * p + 3 * k : 9 * p + 3 * k + 3, :, :C].reshape(3 * C, C) for p in range(3)]
        d = jnp.dot(
            jnp.concatenate(left, axis=1),
            jnp.concatenate(right, axis=0),
            preferred_element_type=F32,
        ).reshape(4, 4, 16, C)
        for a in range(4):
            inner_ref[a, :, end] += d[:, a]
    for t in range(2):
        outer = pair(3 * t)
        for u in range(2):
            epilogue(2 + 2 * t + u, inner_ref[2 * t + u])
        for u in range(2):
            epilogue(6 * t + u, outer[u])


def put_transposed(gt_ref, a, v):
    flat = v.reshape(4, C, C)
    for p in range(4):
        gt_ref[p // 2, a + 2, :, C * (p % 2) : C * (p % 2) + C] = flat[p].T.astype(BF)


def weight_grad(x_ref, gt_ref, columns, scale, store):
    totals = [None] * 3
    for i in range(0, 10, 2):
        low, high = (1 if i == 0 else 0), (2 if i == 8 else 3)
        left = jnp.concatenate(
            [
                gt_ref[h, i + q + low : i + q + high].reshape(C * (high - low), 2 * C)
                for q in range(2)
                for h in range(2)
            ],
            axis=1,
        )
        right = jnp.concatenate(
            [
                jnp.concatenate(
                    [
                        x_ref[:, i + q, c // 3 : c // 3 + 8, :, C * (c % 3) : C * (c % 3) + C]
                        .reshape(512, C)
                        for c in columns
                    ],
                    axis=1,
                )
                for q in range(2)
            ],
            axis=0,
        )
        d = jnp.dot(left, right, preferred_element_type=F32)
        for q in range(low, high):
            part = d[C * (q - low) : C * (q - low) + C]
            totals[q] = part if totals[q] is None else totals[q] + part
    for q in range(3):
        for n, c in enumerate(columns):
            store(q, c, (totals[q][:, C * n : C * n + C] * scale).T)


LEFT_COLUMNS, RIGHT_COLUMNS = range(4), range(4, 9)


def slots_of(taps):
    return (taps + 1) // 2


class Reduction:
    def __init__(self, place, taps, refs):
        self.place = place
        self.taps = taps
        self.g, self.r0, self.s0, self.r1, self.fin, self.send, self.recv = refs

    @staticmethod
    def scratch(taps):
        n = slots_of(taps)
        return [
            pltpu.VMEM((2, 16, n, 8, C), BF),
            pltpu.VMEM((16, n, 8, C), BF),
            pltpu.VMEM((16, n, 8, C), BF),
            pltpu.VMEM((15, n, 8, C), BF),
            pltpu.VMEM((2, 16, n, 8, C), BF),
            pltpu.SemaphoreType.DMA((47,)),
            pltpu.SemaphoreType.DMA((47,)),
        ]

    def clear(self):
        if self.taps % 2:
            self.g[:, 8:, slots_of(self.taps) - 1] = jnp.zeros((2, 8, 8, C), BF)

    def put(self, tap, block):
        for u in range(16):
            n = 8 * tap + u // 2
            self.g[u % 2, n % 16, n // 16] = block[8 * u : 8 * u + 8].astype(BF)

    def copy(self, src, dst, slot, peer):
        return pltpu.make_async_remote_copy(
            src_ref=src,
            dst_ref=dst,
            send_sem=self.send.at[slot],
            recv_sem=self.recv.at[slot],
            device_id={"space": peer},
            device_id_type=MESH,
        )

    def pair(self):
        return self.copy(self.g.at[1 - self.place["core"]], self.r0, 0, self.place["sibling"])

    def scatter(self, d):
        chip = self.place["chip"](d)
        return self.copy(
            self.s0.at[chip], self.r1.at[d - 1], d, 2 * chip + self.place["core"]
        )

    def gather(self, d):
        mine = self.fin.at[self.place["core"], self.place["chip"](0)]
        return self.copy(mine, mine, 15 + d, 2 * self.place["chip"](d) + self.place["core"])

    def forward(self, d):
        one = self.fin.at[self.place["core"], self.place["behind"](d)]
        return self.copy(one, one, 31 + d, self.place["sibling"])

    def step(self, n):
        core, chip = self.place["core"], self.place["chip"]

        def each(low, run):
            def body(d, _):
                run(d)
                return 0

            lax.fori_loop(low, 16, body, 0)

        if n == 0:
            self.pair().start()
        elif n == 1:
            self.pair().wait_recv()

            def add(c):
                self.s0[c] = (self.g[core, c].astype(F32) + self.r0[c].astype(F32)).astype(BF)

            def send(d):
                add(chip(d))
                self.scatter(d).start()

            each(1, send)
            add(chip(0))
        elif n == 2:
            each(1, lambda d: self.scatter(d).wait_recv())
            v = self.s0[chip(0)].astype(F32)
            for d in range(15):
                v = v + self.r1[d].astype(F32)
            self.fin[core, chip(0)] = v.astype(BF)
            each(1, lambda d: self.gather(d).start())
            self.forward(0).start()
        elif n == 3:

            def pass_on(d):
                self.gather(d).wait_recv()
                self.forward(d).start()

            each(1, pass_on)
        else:
            each(0, lambda d: self.forward(d).wait_recv())

    def drain(self):
        self.pair().wait_send()

        def body(d, _):
            self.scatter(d).wait_send()
            self.gather(d).wait_send()
            self.forward(d).wait_send()
            return 0

        self.forward(0).wait_send()
        lax.fori_loop(1, 16, body, 0)


def silu_parts(v):
    s = 1.0 / (1.0 + jnp.exp(-v))
    return s, s * (1.0 + v * (1.0 - s))


def kernel(
    scale,
    feats_h, mask_h, nbr_ref, w1_h, w2_h, cot_h,
    out_h, gin_h, gw2a_h, gw2b_h, gw1a_h, gw1b_h,
    feats, mask, w1, w2, cot, out_s,
    xin, xhid, xg, taps, maskb, pre1, early, gt,
    o0, o1, o2, o3, i0, i1, i2, i3,
    load_sem, store_sem, face_send, face_recv,
    *red_refs,
):
    grads_h = (gw2a_h, gw2b_h, gw1a_h, gw1b_h)
    me = lax.axis_index("space")
    n_space = 32
    core = lax.rem(me, 2)
    chip = me // 2
    z = lax.rem(chip, 4)
    y = chip // 4
    right, left = lax.rem(me + 1, n_space), lax.rem(me + n_space - 1, n_space)

    def chip_at(d):
        return 4 * lax.rem(y + d // 4, 4) + lax.rem(z + lax.rem(d, 4), 4)

    def behind(d):
        return 4 * lax.rem(y + 4 - d // 4, 4) + lax.rem(z + 4 - lax.rem(d, 4), 4)

    place = {"core": core, "sibling": me + 1 - 2 * core, "chip": chip_at, "behind": behind}
    first = 8 * (me - 1)
    red2a, red2b, red1a, red1b = (
        Reduction(place, taps_of, red_refs[7 * i : 7 * i + 7])
        for i, taps_of in enumerate((12, 15, 12, 15))
    )

    loads = [
        pltpu.make_async_copy(src, dst, load_sem.at[i])
        for i, (src, dst) in enumerate(
            ((feats_h, feats), (mask_h, mask), (w1_h, w1), (w2_h, w2), (cot_h, cot))
        )
    ]
    for c in loads:
        c.start()

    barrier = pltpu.get_barrier_semaphore()
    for peer in (left, right):
        pl.semaphore_signal(barrier, inc=1, device_id={"space": peer}, device_id_type=MESH)

    def greet(d, _):
        peer = 2 * chip_at(d) + core
        pl.semaphore_signal(barrier, inc=1, device_id={"space": peer}, device_id_type=MESH)
        return 0

    lax.fori_loop(1, 16, greet, 0)
    pl.semaphore_wait(barrier, 17)

    faces = ((o0, i0), (o1, i1), (o2, i2), (o3, i3))

    def plane_copies(n, ref, slab, a):
        return [
            pltpu.make_async_remote_copy(
                src_ref=ref.at[slab, pl.ds(8, 8)],
                dst_ref=ref.at[slab, pl.ds(at, 8)],
                send_sem=face_send.at[n, side, a],
                recv_sem=face_recv.at[n, side, a],
                device_id={"space": peer},
                device_id_type=MESH,
            )
            for side, (at, peer) in enumerate(((0, right), (16, left)))
        ]

    def send_plane(n, a, v):
        outer, inner = faces[n]
        keep_faces(outer, inner, a, v)

        def start(ref, slab):
            for c in plane_copies(n, ref, slab, a):
                c.start()

        when_outer(a, lambda: start(outer, a // 7), lambda: start(inner, a - 1))

    def face_copies(n):
        outer, inner = faces[n]
        copies = []
        for a in range(8):
            if a in (0, 7):
                copies += plane_copies(n, outer, a // 7, a)
            else:
                copies += plane_copies(n, inner, a - 1, a)
        return copies

    def receive_faces(n, x_ref):
        for c in face_copies(n):
            c.wait_recv()
        fill_rim(x_ref, faces[n], nbr_ref, first)

    for outer, inner in faces:
        for side in range(2):
            outer[side, 24] = jnp.zeros((8, 8, C), BF)
        for a in range(6):
            inner[a, 24] = jnp.zeros((2, 8, C), BF)
    for red in (red2a, red2b, red1a, red1b):
        red.clear()
    for side in range(2):
        for a in (0, 1, 10, 11):
            gt[side, a] = jnp.zeros((C, 2 * C), BF)

    for x_ref in (xin, xhid):
        for column in (0, 9):
            x_ref[:, :, column] = jnp.zeros((4, 10, 16, 3 * C), BF)

    loads[1].wait()
    loads[0].wait()

    def mask_plane(t, _):
        a = jnp.where(t == 0, 0, jnp.where(t == 1, 7, t - 1))
        row = lax.broadcasted_iota(jnp.int32, (C, C), 0)
        lane = lax.broadcasted_iota(jnp.int32, (C, C), 1)
        hit = lane == lax.rem(a, 2) * 64 + (row // 16) * 8 + lax.rem(row, 8)
        second = lax.rem(row // 8, 2) == 1
        at = pl.ds(pl.multiple_of((a // 2) * C, C), C)
        pieces = []
        for p in range(4):
            m0 = mask[2 * p : 2 * p + 1, at].astype(F32)
            m1 = mask[2 * p + 1 : 2 * p + 2, at].astype(F32)
            pieces.append(jnp.where(hit, jnp.where(second, m1, m0), 0.0).astype(BF))
        spread = jnp.dot(
            jnp.concatenate(pieces, axis=0), jnp.ones((C, C), BF), preferred_element_type=F32
        )
        m = spread.reshape(4, 8, 16, C)
        maskb[a] = m.astype(BF)
        v = pair_plane(feats, a) * m
        send_plane(0, a, v)
        put_plane(xin, a, v)
        return 0

    lax.fori_loop(0, 8, mask_plane, 0)

    loads[2].wait()
    loads[3].wait()
    build_taps(taps.at[0], w1, False)
    build_taps(taps.at[2], w2, True)
    def first_done(a, v):
        pre1[a] = v
        s, _ = silu_parts(v)
        h = maskb[a].astype(F32) * (v * s)
        send_plane(1, a, h)
        put_plane(xhid, a, h)

    convolve_split(xin, taps.at[0], early, lambda: receive_faces(0, xin), first_done)
    build_taps(taps.at[1], w2, False)
    build_taps(taps.at[3], w1, True)
    loads[4].wait()

    def second_done(a, v):
        s, slope = silu_parts(v)
        m = maskb[a].astype(F32)
        unpair_plane(out_s, a, m * (v * s))
        g = pair_plane(cot, a) * m * slope
        send_plane(2, a, g)
        put_plane(xg, a, g)
        put_transposed(gt, a, g)

    convolve_split(xhid, taps.at[1], early, lambda: receive_faces(1, xhid), second_done)
    store_out = pltpu.make_async_copy(out_s, out_h, store_sem.at[0])
    store_out.start()

    weight_grad(xhid, gt, LEFT_COLUMNS, scale, lambda q, c, v: red2a.put(4 * (2 - q) + c, v))
    red2a.step(0)
    weight_grad(xhid, gt, RIGHT_COLUMNS, scale, lambda q, c, v: red2b.put(5 * (2 - q) + c - 4, v))
    red2b.step(0)
    red2a.step(1)
    receive_faces(2, xg)

    def third_done(a, v):
        _, slope = silu_parts(pre1[a])
        g = maskb[a].astype(F32) * slope * v
        send_plane(3, a, g)
        put_plane(xhid, a, g)
        put_transposed(gt, a, g)

    def third_between(q):
        @pl.when(q == 0)
        def _():
            red2b.step(1)

        @pl.when(q == 3)
        def _():
            red2a.step(2)

    convolve(xg, taps.at[2], third_done, third_between)
    store_out.wait()

    weight_grad(xin, gt, LEFT_COLUMNS, scale, lambda q, c, v: red1a.put(4 * (2 - q) + c, v))
    red1a.step(0)
    red2b.step(2)
    weight_grad(xin, gt, RIGHT_COLUMNS, scale, lambda q, c, v: red1b.put(5 * (2 - q) + c - 4, v))
    red1b.step(0)
    red1a.step(1)
    receive_faces(3, xhid)
    red1b.step(1)

    def last_done(a, v):
        unpair_plane(out_s, a, maskb[a].astype(F32) * v)

    def last_between(q):
        @pl.when(q == 1)
        def _():
            red2a.step(3)

        @pl.when(q == 2)
        def _():
            red1a.step(2)

        @pl.when(q == 3)
        def _():
            red1b.step(2)

    convolve(xhid, taps.at[3], last_done, last_between)
    reductions = (red2a, red2b, red1a, red1b)
    stores = [
        pltpu.make_async_copy(src, dst, store_sem.at[1 + i])
        for i, (src, dst) in enumerate(
            ((out_s, gin_h), *((red.fin, dst) for red, dst in zip(reductions, grads_h)))
        )
    ]
    stores[0].start()
    red2b.step(3)
    red1a.step(3)
    red2a.step(4)
    stores[1].start()
    red2b.step(4)
    stores[2].start()
    red1b.step(3)
    red1a.step(4)
    stores[3].start()
    red1b.step(4)
    stores[4].start()
    for n in range(4):
        for c in face_copies(n):
            c.wait_send()
    for red in (red2a, red2b, red1a, red1b):
        red.drain()
    for c in stores:
        c.wait()


def finish(
    out_t, gin_t, gw2a_t, gw2b_t, gw1a_t, gw1b_t,
    out_h, gin_h, gw1_h, gw2_h,
    fin2a, fin2b, fin1a, fin1b, w1, w2, out_s, gin_s, sem,
):
    pairs = (
        (gw2a_t, fin2a), (gw2b_t, fin2b), (gw1a_t, fin1a), (gw1b_t, fin1b),
        (out_t, out_s), (gin_t, gin_s),
    )
    reads = [pltpu.make_async_copy(src, dst, sem.at[i]) for i, (src, dst) in enumerate(pairs)]
    pairs = ((w2, gw2_h), (w1, gw1_h), (out_s, out_h), (gin_s, gin_h))
    writes = [pltpu.make_async_copy(src, dst, sem.at[6 + i]) for i, (src, dst) in enumerate(pairs)]
    for c in reads:
        c.start()

    def order(fin, tap, dst, to):
        for u in range(16):
            n = 8 * tap + u // 2
            dst[to, 8 * u : 8 * u + 8] = fin[u % 2, n % 16, n // 16].astype(F32)

    for i, (left, right, dst) in enumerate(((fin2a, fin2b, w2), (fin1a, fin1b, w1))):
        reads[2 * i].wait()
        reads[2 * i + 1].wait()
        for k in range(3):
            for c in LEFT_COLUMNS:
                order(left, 4 * k + c, dst, 9 * k + c)
            for c in RIGHT_COLUMNS:
                order(right, 5 * k + c - 4, dst, 9 * k + c)
        writes[i].start()
    for i in (4, 5):
        reads[i].wait()
        writes[i - 2].start()
    for c in writes:
        c.wait()


def body(feats, mask, neighbours, weight_one, weight_two, cotangent):
    bricks, voxels, channels = feats.shape
    scale = 1.0 / math.sqrt(voxels * bricks)
    cube = (bricks, 8, 8, 8, channels)
    field = pltpu.VMEM((4, 10, 10, 16, 3 * C), BF)
    outer, inner = pltpu.VMEM((2, 25, 8, 8, C), BF), pltpu.VMEM((6, 25, 2, 8, C), BF)
    anywhere = pl.BlockSpec(memory_space=pl.ANY)
    parts = [
        jax.ShapeDtypeStruct((4, 2, 8, 8, 8, C), BF),
        jax.ShapeDtypeStruct((4, 2, 8, 8, 8, C), BF),
        *(jax.ShapeDtypeStruct((2, 16, slots_of(n), 8, C), BF) for n in (12, 15, 12, 15)),
    ]
    left_over = pl.pallas_call(
        functools.partial(kernel, scale),
        out_shape=tuple(parts),
        in_specs=[
            anywhere, anywhere, pl.BlockSpec(memory_space=pltpu.SMEM), anywhere, anywhere, anywhere,
        ],
        out_specs=(anywhere,) * 6,
        scratch_shapes=[
            pltpu.VMEM(cube, BF),
            pltpu.VMEM((bricks, voxels), jnp.int32),
            pltpu.VMEM((27, C, C), BF),
            pltpu.VMEM((27, C, C), BF),
            pltpu.VMEM(cube, BF),
            pltpu.VMEM((4, 2, 8, 8, 8, C), BF),
            field, field, field,
            pltpu.VMEM((4, 36, C, 2 * C), BF),
            pltpu.VMEM((8, 4, 8, 16, C), BF),
            pltpu.VMEM((8, 4, 8, 16, C), F32),
            pltpu.VMEM((4, 4, 8, 16, C), F32),
            pltpu.VMEM((2, 12, C, 2 * C), BF),
            *[outer] * 4,
            *[inner] * 4,
            pltpu.SemaphoreType.DMA((5,)),
            pltpu.SemaphoreType.DMA((6,)),
            pltpu.SemaphoreType.DMA((4, 2, 8)),
            pltpu.SemaphoreType.DMA((4, 2, 8)),
            *(ref for n in (12, 15, 12, 15) for ref in Reduction.scratch(n)),
        ],
        compiler_params=pltpu.CompilerParams(
            collective_id=0, has_side_effects=True, vmem_limit_bytes=60 * 2**20
        ),
        name="bricks",
    )(feats.reshape(cube), mask, neighbours, weight_one, weight_two, cotangent.reshape(cube))

    out, gin, gw1, gw2 = pl.pallas_call(
        finish,
        out_shape=(
            *parts[:2],
            jax.ShapeDtypeStruct((27, C, C), F32),
            jax.ShapeDtypeStruct((27, C, C), F32),
        ),
        in_specs=[anywhere] * 6,
        out_specs=(anywhere,) * 4,
        scratch_shapes=[
            *(pltpu.VMEM(p.shape, BF) for p in parts[2:]),
            pltpu.VMEM((27, C, C), F32),
            pltpu.VMEM((27, C, C), F32),
            pltpu.VMEM(parts[0].shape, BF),
            pltpu.VMEM(parts[1].shape, BF),
            pltpu.SemaphoreType.DMA((10,)),
        ],
        name="outputs",
    )(*left_over)
    return (
        out.reshape(bricks, voxels, channels),
        gin.reshape(bricks, voxels, channels),
        gw1,
        gw2,
    )


def solution(mesh):
    in_specs = (
        P(("scene", "space"), None, None),
        P(("scene", "space"), None),
        P(("scene", "space"), None),
        P(),
        P(),
        P(("scene", "space"), None, None),
    )
    out_specs = (
        P(("scene", "space"), None, None),
        P(("scene", "space"), None, None),
        P("scene", None, None),
        P("scene", None, None),
    )
    return jax.shard_map(body, mesh=mesh, in_specs=in_specs, out_specs=out_specs, check_vma=False)
```

```python
import functools
import math

import jax
import jax.numpy as jnp
from jax import lax
from jax.experimental import pallas as pl
from jax.experimental.pallas import tpu as pltpu
from jax.sharding import PartitionSpec as P

BF = jnp.bfloat16
F32 = jnp.float32
C = 128
MESH = pl.DeviceIdType.MESH


def shifted(v):
    row = lax.broadcasted_iota(jnp.int32, v.shape, v.ndim - 1 - 1)
    down = jnp.where(row == 0, 0.0, pltpu.roll(v, 1, v.ndim - 2))
    up = jnp.where(row == 7, 0.0, pltpu.roll(v, 7, v.ndim - 2))
    return down, v, up


def put_plane(x_ref, a, v):
    for k, s in enumerate(shifted(v.reshape(64, 8, C))):
        x_ref[:, 1 + a, 1:9, :, C * k : C * k + C] = s.reshape(4, 8, 16, C).astype(BF)


def pair_plane(ref, a):
    v = ref[:, a].astype(F32).reshape(4, 2, 8, 8, C)
    return jnp.stack([v[:, 0], v[:, 1]], axis=2).reshape(4, 8, 16, C)


def unpair_plane(ref, a, v):
    w = v.reshape(4, 8, 2, 8, C)
    for half in range(2):
        ref[:, half, a] = w[:, :, half].astype(BF)


def when_outer(a, run_outer, run_inner):
    if isinstance(a, int):
        run_outer() if a in (0, 7) else run_inner()
        return
    pl.when((a == 0) | (a == 7))(run_outer)
    pl.when((a > 0) & (a < 7))(run_inner)


def keep_faces(outer, inner, a, v):
    w = v.reshape(4, 8, 2, 8, C)

    def whole():
        for p in range(4):
            for half in range(2):
                outer[a // 7, 8 + 2 * p + half] = w[p, :, half].astype(BF)

    def ends():
        for p in range(4):
            for half in range(2):
                inner[a - 1, 8 + 2 * p + half, 0] = w[p, 0, half].astype(BF)
                inner[a - 1, 8 + 2 * p + half, 1] = w[p, 7, half].astype(BF)

    when_outer(a, whole, ends)


def fill_rim(x_ref, faces, nbr_ref, first):
    outer, inner = faces

    def body(p, _):
        def source(column):
            out = []
            for half in range(2):
                n = nbr_ref[2 * p + half, column]
                out.append(jnp.where(n >= 0, jnp.clip(n - first, 0, 23), 24))
            return out

        def cell(x, y, i, j):
            w = jnp.stack([x.astype(F32), y.astype(F32)], axis=0)
            for k, s in enumerate(shifted(w)):
                x_ref[p, i, j, :, C * k : C * k + C] = s.reshape(16, C).astype(BF)

        for column, side, where, i, j in (
            (0, 1, 7, 0, 0), (2, 1, 0, 0, 9), (5, 0, 7, 9, 0), (7, 0, 0, 9, 9),
        ):
            m, n = source(column)
            cell(outer[side, m, where], outer[side, n, where], i, j)
        for column, side, i in ((1, 1, 0), (6, 0, 9)):
            m, n = source(column)
            u, v = outer[side, m].astype(F32), outer[side, n].astype(F32)
            w = jnp.stack([u, v], axis=1).reshape(16, 8, C)
            for k, s in enumerate(shifted(w)):
                x_ref[p, i, 1:9, :, C * k : C * k + C] = s.reshape(8, 16, C).astype(BF)
        for column, end, j in ((3, 1, 0), (4, 0, 9)):
            m, n = source(column)
            cell(outer[0, m, 7 * end], outer[0, n, 7 * end], 1, j)
            for a in range(1, 7):
                cell(inner[a - 1, m, end], inner[a - 1, n, end], 1 + a, j)
            cell(outer[1, m, 7 * end], outer[1, n, 7 * end], 8, j)
        return 0

    lax.fori_loop(0, 4, body, 0)


def build_taps(t_ref, w_ref, flipped):
    def body(t, _):
        zero = jnp.zeros((C, C), BF)
        t_ref[t, :, C:] = zero
        t_ref[27 + t, :, :C] = zero
        for k in range(3):
            if flipped:
                w = w_ref[26 - (9 * k + t)].astype(F32).T.astype(BF)
            else:
                w = w_ref[9 * k + t]
            t_ref[9 * k + t, :, :C] = w
            t_ref[9 * k + 9 + t, :, C:] = w
        return 0

    lax.fori_loop(0, 9, body, 0)


def convolve(x_ref, t_ref, epilogue, between=None):
    def body(t, _):
        q = jnp.where(t == 0, 0, jnp.where(t == 1, 3, t - 1))
        windows = [
            x_ref[:, 2 * q + p, k : k + 8].reshape(512, 3 * C) for p in range(4) for k in range(3)
        ]
        total = jnp.dot(
            jnp.concatenate(windows, axis=1),
            t_ref[...].reshape(36 * C, 2 * C),
            preferred_element_type=F32,
        )
        for u in range(2):
            epilogue(2 * q + u, total[:, C * u : C * u + C].reshape(4, 8, 16, C))
        if between is not None:
            between(t)
        return 0

    lax.fori_loop(0, 4, body, 0)


def convolve_split(x_ref, t_ref, inner_ref, arrive, epilogue):
    def pair(q):
        windows = [
            x_ref[:, 2 * q + p, k : k + 8].reshape(512, 3 * C) for p in range(4) for k in range(3)
        ]
        total = jnp.dot(
            jnp.concatenate(windows, axis=1),
            t_ref[...].reshape(36 * C, 2 * C),
            preferred_element_type=F32,
        )
        return [total[:, C * u : C * u + C].reshape(4, 8, 16, C) for u in range(2)]

    def early(t, _):
        for u, v in enumerate(pair(1 + t)):
            inner_ref[2 * t + u] = v
        return 0

    lax.fori_loop(0, 2, early, 0)
    arrive()
    for end, column, k in ((0, 0, 0), (7, 9, 2)):
        left = [x_ref[:, 2 + p : 6 + p, column].reshape(256, 3 * C) for p in range(3)]
        right = [t_ref[9 * p + 3 * k : 9 * p + 3 * k + 3, :, :C].reshape(3 * C, C) for p in range(3)]
        d = jnp.dot(
            jnp.concatenate(left, axis=1),
            jnp.concatenate(right, axis=0),
            preferred_element_type=F32,
        ).reshape(4, 4, 16, C)
        for a in range(4):
            inner_ref[a, :, end] += d[:, a]
    for t in range(2):
        outer = pair(3 * t)
        for u in range(2):
            epilogue(2 + 2 * t + u, inner_ref[2 * t + u])
        for u in range(2):
            epilogue(6 * t + u, outer[u])


def put_transposed(gt_ref, a, v):
    flat = v.reshape(4, C, C)
    for p in range(4):
        gt_ref[p // 2, a + 2, :, C * (p % 2) : C * (p % 2) + C] = flat[p].T.astype(BF)


def weight_grad(x_ref, gt_ref, columns, scale, store):
    totals = [None] * 3
    for i in range(0, 10, 2):
        low, high = (1 if i == 0 else 0), (2 if i == 8 else 3)
        left = jnp.concatenate(
            [
                gt_ref[h, i + q + low : i + q + high].reshape(C * (high - low), 2 * C)
                for q in range(2)
                for h in range(2)
            ],
            axis=1,
        )
        right = jnp.concatenate(
            [
                jnp.concatenate(
                    [
                        x_ref[:, i + q, c // 3 : c // 3 + 8, :, C * (c % 3) : C * (c % 3) + C]
                        .reshape(512, C)
                        for c in columns
                    ],
                    axis=1,
                )
                for q in range(2)
            ],
            axis=0,
        )
        d = jnp.dot(left, right, preferred_element_type=F32)
        for q in range(low, high):
            part = d[C * (q - low) : C * (q - low) + C]
            totals[q] = part if totals[q] is None else totals[q] + part
    for q in range(3):
        for n, c in enumerate(columns):
            store(q, c, (totals[q][:, C * n : C * n + C] * scale).T)


LEFT_COLUMNS, RIGHT_COLUMNS = range(4), range(4, 9)


def slots_of(taps):
    return (taps + 1) // 2


class Reduction:
    def __init__(self, place, taps, refs):
        self.place = place
        self.taps = taps
        self.g, self.r0, self.s0, self.r1, self.fin, self.send, self.recv = refs

    @staticmethod
    def scratch(taps):
        n = slots_of(taps)
        return [
            pltpu.VMEM((2, 16, n, 8, C), BF),
            pltpu.VMEM((16, n, 8, C), BF),
            pltpu.VMEM((16, n, 8, C), BF),
            pltpu.VMEM((15, n, 8, C), BF),
            pltpu.VMEM((2, 16, n, 8, C), BF),
            pltpu.SemaphoreType.DMA((47,)),
            pltpu.SemaphoreType.DMA((47,)),
        ]

    def clear(self):
        if self.taps % 2:
            self.g[:, 8:, slots_of(self.taps) - 1] = jnp.zeros((2, 8, 8, C), BF)

    def put(self, tap, block):
        for u in range(16):
            n = 8 * tap + u // 2
            self.g[u % 2, n % 16, n // 16] = block[8 * u : 8 * u + 8].astype(BF)

    def copy(self, src, dst, slot, peer):
        return pltpu.make_async_remote_copy(
            src_ref=src,
            dst_ref=dst,
            send_sem=self.send.at[slot],
            recv_sem=self.recv.at[slot],
            device_id={"space": peer},
            device_id_type=MESH,
        )

    def pair(self):
        return self.copy(self.g.at[1 - self.place["core"]], self.r0, 0, self.place["sibling"])

    def scatter(self, d):
        chip = self.place["chip"](d)
        return self.copy(
            self.s0.at[chip], self.r1.at[d - 1], d, 2 * chip + self.place["core"]
        )

    def gather(self, d):
        mine = self.fin.at[self.place["core"], self.place["chip"](0)]
        return self.copy(mine, mine, 15 + d, 2 * self.place["chip"](d) + self.place["core"])

    def forward(self, d):
        one = self.fin.at[self.place["core"], self.place["behind"](d)]
        return self.copy(one, one, 31 + d, self.place["sibling"])

    def step(self, n):
        core, chip = self.place["core"], self.place["chip"]

        def each(low, run):
            def body(d, _):
                run(d)
                return 0

            lax.fori_loop(low, 16, body, 0)

        if n == 0:
            self.pair().start()
        elif n == 1:
            self.pair().wait_recv()

            def add(c):
                self.s0[c] = (self.g[core, c].astype(F32) + self.r0[c].astype(F32)).astype(BF)

            def send(d):
                add(chip(d))
                self.scatter(d).start()

            each(1, send)
            add(chip(0))
        elif n == 2:
            each(1, lambda d: self.scatter(d).wait_recv())
            v = self.s0[chip(0)].astype(F32)
            for d in range(15):
                v = v + self.r1[d].astype(F32)
            self.fin[core, chip(0)] = v.astype(BF)
            each(1, lambda d: self.gather(d).start())
            self.forward(0).start()
        elif n == 3:

            def pass_on(d):
                self.gather(d).wait_recv()
                self.forward(d).start()

            each(1, pass_on)
        else:
            each(0, lambda d: self.forward(d).wait_recv())

    def drain(self):
        self.pair().wait_send()

        def body(d, _):
            self.scatter(d).wait_send()
            self.gather(d).wait_send()
            self.forward(d).wait_send()
            return 0

        self.forward(0).wait_send()
        lax.fori_loop(1, 16, body, 0)


def silu_parts(v):
    s = 1.0 / (1.0 + jnp.exp(-v))
    return s, s * (1.0 + v * (1.0 - s))


def kernel(
    scale,
    feats_h, mask_h, nbr_ref, w1_h, w2_h, cot_h,
    out_h, gin_h, gw2a_h, gw2b_h, gw1a_h, gw1b_h,
    feats, mask, w1, w2, cot, out_s,
    xin, xhid, xg, taps, maskb, pre1, early, gt,
    o0, o1, o2, o3, i0, i1, i2, i3,
    load_sem, store_sem, face_send, face_recv,
    *red_refs,
):
    grads_h = (gw2a_h, gw2b_h, gw1a_h, gw1b_h)
    me = lax.axis_index("space")
    n_space = 32
    core = lax.rem(me, 2)
    chip = me // 2
    z = lax.rem(chip, 4)
    y = chip // 4
    right, left = lax.rem(me + 1, n_space), lax.rem(me + n_space - 1, n_space)

    def chip_at(d):
        return 4 * lax.rem(y + d // 4, 4) + lax.rem(z + lax.rem(d, 4), 4)

    def behind(d):
        return 4 * lax.rem(y + 4 - d // 4, 4) + lax.rem(z + 4 - lax.rem(d, 4), 4)

    place = {"core": core, "sibling": me + 1 - 2 * core, "chip": chip_at, "behind": behind}
    first = 8 * (me - 1)
    red2a, red2b, red1a, red1b = (
        Reduction(place, taps_of, red_refs[7 * i : 7 * i + 7])
        for i, taps_of in enumerate((12, 15, 12, 15))
    )

    loads = [
        pltpu.make_async_copy(src, dst, load_sem.at[i])
        for i, (src, dst) in enumerate(
            ((feats_h, feats), (mask_h, mask), (w1_h, w1), (w2_h, w2), (cot_h, cot))
        )
    ]
    for c in loads:
        c.start()

    barrier = pltpu.get_barrier_semaphore()
    for peer in (left, right):
        pl.semaphore_signal(barrier, inc=1, device_id={"space": peer}, device_id_type=MESH)

    def greet(d, _):
        peer = 2 * chip_at(d) + core
        pl.semaphore_signal(barrier, inc=1, device_id={"space": peer}, device_id_type=MESH)
        return 0

    lax.fori_loop(1, 16, greet, 0)
    pl.semaphore_wait(barrier, 17)

    faces = ((o0, i0), (o1, i1), (o2, i2), (o3, i3))

    def plane_copies(n, ref, slab, a):
        return [
            pltpu.make_async_remote_copy(
                src_ref=ref.at[slab, pl.ds(8, 8)],
                dst_ref=ref.at[slab, pl.ds(at, 8)],
                send_sem=face_send.at[n, side, a],
                recv_sem=face_recv.at[n, side, a],
                device_id={"space": peer},
                device_id_type=MESH,
            )
            for side, (at, peer) in enumerate(((0, right), (16, left)))
        ]

    def send_plane(n, a, v):
        outer, inner = faces[n]
        keep_faces(outer, inner, a, v)

        def start(ref, slab):
            for c in plane_copies(n, ref, slab, a):
                c.start()

        when_outer(a, lambda: start(outer, a // 7), lambda: start(inner, a - 1))

    def face_copies(n):
        outer, inner = faces[n]
        copies = []
        for a in range(8):
            if a in (0, 7):
                copies += plane_copies(n, outer, a // 7, a)
            else:
                copies += plane_copies(n, inner, a - 1, a)
        return copies

    def receive_faces(n, x_ref):
        for c in face_copies(n):
            c.wait_recv()
        fill_rim(x_ref, faces[n], nbr_ref, first)

    for outer, inner in faces:
        for side in range(2):
            outer[side, 24] = jnp.zeros((8, 8, C), BF)
        for a in range(6):
            inner[a, 24] = jnp.zeros((2, 8, C), BF)
    for red in (red2a, red2b, red1a, red1b):
        red.clear()
    for side in range(2):
        for a in (0, 1, 10, 11):
            gt[side, a] = jnp.zeros((C, 2 * C), BF)

    for x_ref in (xin, xhid):
        for column in (0, 9):
            x_ref[:, :, column] = jnp.zeros((4, 10, 16, 3 * C), BF)

    loads[1].wait()
    loads[0].wait()

    def mask_plane(t, _):
        a = jnp.where(t == 0, 0, jnp.where(t == 1, 7, t - 1))
        row = lax.broadcasted_iota(jnp.int32, (C, C), 0)
        lane = lax.broadcasted_iota(jnp.int32, (C, C), 1)
        hit = lane == lax.rem(a, 2) * 64 + (row // 16) * 8 + lax.rem(row, 8)
        second = lax.rem(row // 8, 2) == 1
        at = pl.ds(pl.multiple_of((a // 2) * C, C), C)
        pieces = []
        for p in range(4):
            m0 = mask[2 * p : 2 * p + 1, at].astype(F32)
            m1 = mask[2 * p + 1 : 2 * p + 2, at].astype(F32)
            pieces.append(jnp.where(hit, jnp.where(second, m1, m0), 0.0).astype(BF))
        spread = jnp.dot(
            jnp.concatenate(pieces, axis=0), jnp.ones((C, C), BF), preferred_element_type=F32
        )
        m = spread.reshape(4, 8, 16, C)
        maskb[a] = m.astype(BF)
        v = pair_plane(feats, a) * m
        send_plane(0, a, v)
        put_plane(xin, a, v)
        return 0

    lax.fori_loop(0, 8, mask_plane, 0)

    loads[2].wait()
    loads[3].wait()
    build_taps(taps.at[0], w1, False)
    build_taps(taps.at[2], w2, True)
    def first_done(a, v):
        pre1[a] = v
        s, _ = silu_parts(v)
        h = maskb[a].astype(F32) * (v * s)
        send_plane(1, a, h)
        put_plane(xhid, a, h)

    convolve_split(xin, taps.at[0], early, lambda: receive_faces(0, xin), first_done)
    build_taps(taps.at[1], w2, False)
    build_taps(taps.at[3], w1, True)
    loads[4].wait()

    def second_done(a, v):
        s, slope = silu_parts(v)
        m = maskb[a].astype(F32)
        unpair_plane(out_s, a, m * (v * s))
        g = pair_plane(cot, a) * m * slope
        send_plane(2, a, g)
        put_plane(xg, a, g)
        put_transposed(gt, a, g)

    convolve_split(xhid, taps.at[1], early, lambda: receive_faces(1, xhid), second_done)
    store_out = pltpu.make_async_copy(out_s, out_h, store_sem.at[0])
    store_out.start()

    weight_grad(xhid, gt, LEFT_COLUMNS, scale, lambda q, c, v: red2a.put(4 * (2 - q) + c, v))
    red2a.step(0)
    weight_grad(xhid, gt, RIGHT_COLUMNS, scale, lambda q, c, v: red2b.put(5 * (2 - q) + c - 4, v))
    red2b.step(0)
    red2a.step(1)
    receive_faces(2, xg)

    def third_done(a, v):
        _, slope = silu_parts(pre1[a])
        g = maskb[a].astype(F32) * slope * v
        send_plane(3, a, g)
        put_plane(xhid, a, g)
        put_transposed(gt, a, g)

    def third_between(q):
        @pl.when(q == 0)
        def _():
            red2b.step(1)

        @pl.when(q == 2)
        def _():
            red2a.step(2)

        @pl.when(q == 3)
        def _():
            red2b.step(2)

    convolve(xg, taps.at[2], third_done, third_between)
    store_out.wait()

    weight_grad(xin, gt, RIGHT_COLUMNS, scale, lambda q, c, v: red1b.put(5 * (2 - q) + c - 4, v))
    red1b.step(0)
    weight_grad(xin, gt, LEFT_COLUMNS, scale, lambda q, c, v: red1a.put(4 * (2 - q) + c, v))
    red1a.step(0)
    red1b.step(1)
    receive_faces(3, xhid)

    def last_done(a, v):
        unpair_plane(out_s, a, maskb[a].astype(F32) * v)

    def last_between(q):
        @pl.when(q == 0)
        def _():
            red1a.step(1)

        @pl.when(q == 2)
        def _():
            red2a.step(3)

        @pl.when(q == 3)
        def _():
            red1b.step(2)

    convolve(xhid, taps.at[3], last_done, last_between)
    reductions = (red2a, red2b, red1a, red1b)
    stores = [
        pltpu.make_async_copy(src, dst, store_sem.at[1 + i])
        for i, (src, dst) in enumerate(
            ((out_s, gin_h), *((red.fin, dst) for red, dst in zip(reductions, grads_h)))
        )
    ]
    stores[0].start()
    red1a.step(2)
    red2b.step(3)
    red2a.step(4)
    stores[1].start()
    red2b.step(4)
    stores[2].start()
    red1b.step(3)
    red1a.step(3)
    red1b.step(4)
    stores[4].start()
    red1a.step(4)
    stores[3].start()
    for n in range(4):
        for c in face_copies(n):
            c.wait_send()
    for red in (red2a, red2b, red1a, red1b):
        red.drain()
    for c in stores:
        c.wait()


def finish(
    out_t, gin_t, gw2a_t, gw2b_t, gw1a_t, gw1b_t,
    out_h, gin_h, gw1_h, gw2_h,
    fin2a, fin2b, fin1a, fin1b, w1, w2, out_s, gin_s, sem,
):
    pairs = (
        (gw2a_t, fin2a), (gw2b_t, fin2b), (gw1a_t, fin1a), (gw1b_t, fin1b),
        (out_t, out_s), (gin_t, gin_s),
    )
    reads = [pltpu.make_async_copy(src, dst, sem.at[i]) for i, (src, dst) in enumerate(pairs)]
    pairs = ((w2, gw2_h), (w1, gw1_h), (out_s, out_h), (gin_s, gin_h))
    writes = [pltpu.make_async_copy(src, dst, sem.at[6 + i]) for i, (src, dst) in enumerate(pairs)]
    for c in reads:
        c.start()

    def order(fin, tap, dst, to):
        for u in range(16):
            n = 8 * tap + u // 2
            dst[to, 8 * u : 8 * u + 8] = fin[u % 2, n % 16, n // 16].astype(F32)

    for i, (left, right, dst) in enumerate(((fin2a, fin2b, w2), (fin1a, fin1b, w1))):
        reads[2 * i].wait()
        reads[2 * i + 1].wait()
        for k in range(3):
            for c in LEFT_COLUMNS:
                order(left, 4 * k + c, dst, 9 * k + c)
            for c in RIGHT_COLUMNS:
                order(right, 5 * k + c - 4, dst, 9 * k + c)
        writes[i].start()
    for i in (4, 5):
        reads[i].wait()
        writes[i - 2].start()
    for c in writes:
        c.wait()


def body(feats, mask, neighbours, weight_one, weight_two, cotangent):
    bricks, voxels, channels = feats.shape
    scale = 1.0 / math.sqrt(voxels * bricks)
    cube = (bricks, 8, 8, 8, channels)
    field = pltpu.VMEM((4, 10, 10, 16, 3 * C), BF)
    outer, inner = pltpu.VMEM((2, 25, 8, 8, C), BF), pltpu.VMEM((6, 25, 2, 8, C), BF)
    anywhere = pl.BlockSpec(memory_space=pl.ANY)
    parts = [
        jax.ShapeDtypeStruct((4, 2, 8, 8, 8, C), BF),
        jax.ShapeDtypeStruct((4, 2, 8, 8, 8, C), BF),
        *(jax.ShapeDtypeStruct((2, 16, slots_of(n), 8, C), BF) for n in (12, 15, 12, 15)),
    ]
    left_over = pl.pallas_call(
        functools.partial(kernel, scale),
        out_shape=tuple(parts),
        in_specs=[
            anywhere, anywhere, pl.BlockSpec(memory_space=pltpu.SMEM), anywhere, anywhere, anywhere,
        ],
        out_specs=(anywhere,) * 6,
        scratch_shapes=[
            pltpu.VMEM(cube, BF),
            pltpu.VMEM((bricks, voxels), jnp.int32),
            pltpu.VMEM((27, C, C), BF),
            pltpu.VMEM((27, C, C), BF),
            pltpu.VMEM(cube, BF),
            pltpu.VMEM((4, 2, 8, 8, 8, C), BF),
            field, field, field,
            pltpu.VMEM((4, 36, C, 2 * C), BF),
            pltpu.VMEM((8, 4, 8, 16, C), BF),
            pltpu.VMEM((8, 4, 8, 16, C), F32),
            pltpu.VMEM((4, 4, 8, 16, C), F32),
            pltpu.VMEM((2, 12, C, 2 * C), BF),
            *[outer] * 4,
            *[inner] * 4,
            pltpu.SemaphoreType.DMA((5,)),
            pltpu.SemaphoreType.DMA((6,)),
            pltpu.SemaphoreType.DMA((4, 2, 8)),
            pltpu.SemaphoreType.DMA((4, 2, 8)),
            *(ref for n in (12, 15, 12, 15) for ref in Reduction.scratch(n)),
        ],
        compiler_params=pltpu.CompilerParams(
            collective_id=0, has_side_effects=True, vmem_limit_bytes=60 * 2**20
        ),
        name="bricks",
    )(feats.reshape(cube), mask, neighbours, weight_one, weight_two, cotangent.reshape(cube))

    out, gin, gw1, gw2 = pl.pallas_call(
        finish,
        out_shape=(
            *parts[:2],
            jax.ShapeDtypeStruct((27, C, C), F32),
            jax.ShapeDtypeStruct((27, C, C), F32),
        ),
        in_specs=[anywhere] * 6,
        out_specs=(anywhere,) * 4,
        scratch_shapes=[
            *(pltpu.VMEM(p.shape, BF) for p in parts[2:]),
            pltpu.VMEM((27, C, C), F32),
            pltpu.VMEM((27, C, C), F32),
            pltpu.VMEM(parts[0].shape, BF),
            pltpu.VMEM(parts[1].shape, BF),
            pltpu.SemaphoreType.DMA((10,)),
        ],
        name="outputs",
    )(*left_over)
    return (
        out.reshape(bricks, voxels, channels),
        gin.reshape(bricks, voxels, channels),
        gw1,
        gw2,
    )


def solution(mesh):
    in_specs = (
        P(("scene", "space"), None, None),
        P(("scene", "space"), None),
        P(("scene", "space"), None),
        P(),
        P(),
        P(("scene", "space"), None, None),
    )
    out_specs = (
        P(("scene", "space"), None, None),
        P(("scene", "space"), None, None),
        P("scene", None, None),
        P("scene", None, None),
    )
    return jax.shard_map(body, mesh=mesh, in_specs=in_specs, out_specs=out_specs, check_vma=False)
```

```python
import functools
import math

import jax
import jax.numpy as jnp
from jax import lax
from jax.experimental import pallas as pl
from jax.experimental.pallas import tpu as pltpu
from jax.sharding import PartitionSpec as P

BF = jnp.bfloat16
F32 = jnp.float32
C = 128
MESH = pl.DeviceIdType.MESH


def shifted(v):
    row = lax.broadcasted_iota(jnp.int32, v.shape, v.ndim - 1 - 1)
    down = jnp.where(row == 0, 0.0, pltpu.roll(v, 1, v.ndim - 2))
    up = jnp.where(row == 7, 0.0, pltpu.roll(v, 7, v.ndim - 2))
    return down, v, up


def put_plane(x_ref, a, v):
    for k, s in enumerate(shifted(v.reshape(64, 8, C))):
        x_ref[:, 1 + a, 1:9, :, C * k : C * k + C] = s.reshape(4, 8, 16, C).astype(BF)


def pair_plane(ref, a):
    v = ref[:, a].astype(F32).reshape(4, 2, 8, 8, C)
    return jnp.stack([v[:, 0], v[:, 1]], axis=2).reshape(4, 8, 16, C)


def unpair_plane(ref, a, v):
    w = v.reshape(4, 8, 2, 8, C)
    for half in range(2):
        ref[:, half, a] = w[:, :, half].astype(BF)


def when_outer(a, run_outer, run_inner):
    if isinstance(a, int):
        run_outer() if a in (0, 7) else run_inner()
        return
    pl.when((a == 0) | (a == 7))(run_outer)
    pl.when((a > 0) & (a < 7))(run_inner)


def keep_faces(outer, inner, a, v):
    w = v.reshape(4, 8, 2, 8, C)

    def whole():
        for p in range(4):
            for half in range(2):
                outer[a // 7, 8 + 2 * p + half] = w[p, :, half].astype(BF)

    def ends():
        for p in range(4):
            for half in range(2):
                inner[a - 1, 8 + 2 * p + half, 0] = w[p, 0, half].astype(BF)
                inner[a - 1, 8 + 2 * p + half, 1] = w[p, 7, half].astype(BF)

    when_outer(a, whole, ends)


def fill_rim(x_ref, faces, nbr_ref, first):
    outer, inner = faces

    def body(p, _):
        def source(column):
            out = []
            for half in range(2):
                n = nbr_ref[2 * p + half, column]
                out.append(jnp.where(n >= 0, jnp.clip(n - first, 0, 23), 24))
            return out

        def cell(x, y, i, j):
            w = jnp.stack([x.astype(F32), y.astype(F32)], axis=0)
            for k, s in enumerate(shifted(w)):
                x_ref[p, i, j, :, C * k : C * k + C] = s.reshape(16, C).astype(BF)

        for column, side, where, i, j in (
            (0, 1, 7, 0, 0), (2, 1, 0, 0, 9), (5, 0, 7, 9, 0), (7, 0, 0, 9, 9),
        ):
            m, n = source(column)
            cell(outer[side, m, where], outer[side, n, where], i, j)
        for column, side, i in ((1, 1, 0), (6, 0, 9)):
            m, n = source(column)
            u, v = outer[side, m].astype(F32), outer[side, n].astype(F32)
            w = jnp.stack([u, v], axis=1).reshape(16, 8, C)
            for k, s in enumerate(shifted(w)):
                x_ref[p, i, 1:9, :, C * k : C * k + C] = s.reshape(8, 16, C).astype(BF)
        for column, end, j in ((3, 1, 0), (4, 0, 9)):
            m, n = source(column)
            cell(outer[0, m, 7 * end], outer[0, n, 7 * end], 1, j)
            for a in range(1, 7):
                cell(inner[a - 1, m, end], inner[a - 1, n, end], 1 + a, j)
            cell(outer[1, m, 7 * end], outer[1, n, 7 * end], 8, j)
        return 0

    lax.fori_loop(0, 4, body, 0)


def build_taps(t_ref, w_ref, flipped):
    def body(t, _):
        zero = jnp.zeros((C, C), BF)
        t_ref[t, :, C:] = zero
        t_ref[27 + t, :, :C] = zero
        for k in range(3):
            if flipped:
                w = w_ref[26 - (9 * k + t)].astype(F32).T.astype(BF)
            else:
                w = w_ref[9 * k + t]
            t_ref[9 * k + t, :, :C] = w
            t_ref[9 * k + 9 + t, :, C:] = w
        return 0

    lax.fori_loop(0, 9, body, 0)


def convolve(x_ref, t_ref, epilogue, between=None):
    def body(t, _):
        q = jnp.where(t == 0, 0, jnp.where(t == 1, 3, t - 1))
        windows = [
            x_ref[:, 2 * q + p, k : k + 8].reshape(512, 3 * C) for p in range(4) for k in range(3)
        ]
        total = jnp.dot(
            jnp.concatenate(windows, axis=1),
            t_ref[...].reshape(36 * C, 2 * C),
            preferred_element_type=F32,
        )
        for u in range(2):
            epilogue(2 * q + u, total[:, C * u : C * u + C].reshape(4, 8, 16, C))
        if between is not None:
            between(t)
        return 0

    lax.fori_loop(0, 4, body, 0)


def convolve_split(x_ref, t_ref, inner_ref, arrive, epilogue):
    def pair(q):
        windows = [
            x_ref[:, 2 * q + p, k : k + 8].reshape(512, 3 * C) for p in range(4) for k in range(3)
        ]
        total = jnp.dot(
            jnp.concatenate(windows, axis=1),
            t_ref[...].reshape(36 * C, 2 * C),
            preferred_element_type=F32,
        )
        return [total[:, C * u : C * u + C].reshape(4, 8, 16, C) for u in range(2)]

    def early(t, _):
        for u, v in enumerate(pair(1 + t)):
            inner_ref[2 * t + u] = v
        return 0

    lax.fori_loop(0, 2, early, 0)
    arrive()
    for end, column, k in ((0, 0, 0), (7, 9, 2)):
        left = [x_ref[:, 2 + p : 6 + p, column].reshape(256, 3 * C) for p in range(3)]
        right = [t_ref[9 * p + 3 * k : 9 * p + 3 * k + 3, :, :C].reshape(3 * C, C) for p in range(3)]
        d = jnp.dot(
            jnp.concatenate(left, axis=1),
            jnp.concatenate(right, axis=0),
            preferred_element_type=F32,
        ).reshape(4, 4, 16, C)
        for a in range(4):
            inner_ref[a, :, end] += d[:, a]
    for t in range(2):
        outer = pair(3 * t)
        for u in range(2):
            epilogue(2 + 2 * t + u, inner_ref[2 * t + u])
        for u in range(2):
            epilogue(6 * t + u, outer[u])


def put_transposed(gt_ref, a, v):
    flat = v.reshape(4, C, C)
    for p in range(4):
        gt_ref[p // 2, a + 2, :, C * (p % 2) : C * (p % 2) + C] = flat[p].T.astype(BF)


def weight_grad(x_ref, gt_ref, columns, scale, store):
    totals = [None] * 3
    for i in range(0, 10, 2):
        low, high = (1 if i == 0 else 0), (2 if i == 8 else 3)
        left = jnp.concatenate(
            [
                gt_ref[h, i + q + low : i + q + high].reshape(C * (high - low), 2 * C)
                for q in range(2)
                for h in range(2)
            ],
            axis=1,
        )
        right = jnp.concatenate(
            [
                jnp.concatenate(
                    [
                        x_ref[:, i + q, c // 3 : c // 3 + 8, :, C * (c % 3) : C * (c % 3) + C]
                        .reshape(512, C)
                        for c in columns
                    ],
                    axis=1,
                )
                for q in range(2)
            ],
            axis=0,
        )
        d = jnp.dot(left, right, preferred_element_type=F32)
        for q in range(low, high):
            part = d[C * (q - low) : C * (q - low) + C]
            totals[q] = part if totals[q] is None else totals[q] + part
    for q in range(3):
        for n, c in enumerate(columns):
            store(q, c, (totals[q][:, C * n : C * n + C] * scale).T)


LEFT_COLUMNS, RIGHT_COLUMNS = range(4), range(4, 9)


def slots_of(taps):
    return (taps + 1) // 2


class Reduction:
    def __init__(self, place, taps, refs):
        self.place = place
        self.taps = taps
        self.g, self.r0, self.s0, self.r1, self.fin, self.send, self.recv = refs

    @staticmethod
    def scratch(taps):
        n = slots_of(taps)
        return [
            pltpu.VMEM((2, 16, n, 8, C), BF),
            pltpu.VMEM((16, n, 8, C), BF),
            pltpu.VMEM((16, n, 8, C), BF),
            pltpu.VMEM((15, n, 8, C), BF),
            pltpu.VMEM((2, 16, n, 8, C), BF),
            pltpu.SemaphoreType.DMA((47,)),
            pltpu.SemaphoreType.DMA((47,)),
        ]

    def clear(self):
        if self.taps % 2:
            self.g[:, 8:, slots_of(self.taps) - 1] = jnp.zeros((2, 8, 8, C), BF)

    def put(self, tap, block):
        for u in range(16):
            n = 8 * tap + u // 2
            self.g[u % 2, n % 16, n // 16] = block[8 * u : 8 * u + 8].astype(BF)

    def copy(self, src, dst, slot, peer):
        return pltpu.make_async_remote_copy(
            src_ref=src,
            dst_ref=dst,
            send_sem=self.send.at[slot],
            recv_sem=self.recv.at[slot],
            device_id={"space": peer},
            device_id_type=MESH,
        )

    def pair(self):
        return self.copy(self.g.at[1 - self.place["core"]], self.r0, 0, self.place["sibling"])

    def scatter(self, d):
        chip = self.place["chip"](d)
        return self.copy(
            self.s0.at[chip], self.r1.at[d - 1], d, 2 * chip + self.place["core"]
        )

    def gather(self, d):
        mine = self.fin.at[self.place["core"], self.place["chip"](0)]
        return self.copy(mine, mine, 15 + d, 2 * self.place["chip"](d) + self.place["core"])

    def forward(self, d):
        one = self.fin.at[self.place["core"], self.place["behind"](d)]
        return self.copy(one, one, 31 + d, self.place["sibling"])

    def step(self, n):
        core, chip = self.place["core"], self.place["chip"]

        def each(low, run):
            def body(d, _):
                run(d)
                return 0

            lax.fori_loop(low, 16, body, 0)

        if n == 0:
            self.pair().start()
        elif n == 1:
            self.pair().wait_recv()

            def add(c):
                self.s0[c] = (self.g[core, c].astype(F32) + self.r0[c].astype(F32)).astype(BF)

            def send(d):
                add(chip(d))
                self.scatter(d).start()

            each(1, send)
            add(chip(0))
        elif n == 2:
            each(1, lambda d: self.scatter(d).wait_recv())
            v = self.s0[chip(0)].astype(F32)
            for d in range(15):
                v = v + self.r1[d].astype(F32)
            self.fin[core, chip(0)] = v.astype(BF)
            each(1, lambda d: self.gather(d).start())
            self.forward(0).start()
        elif n == 3:

            def pass_on(d):
                self.gather(d).wait_recv()
                self.forward(d).start()

            each(1, pass_on)
        else:
            each(0, lambda d: self.forward(d).wait_recv())

    def drain(self):
        self.pair().wait_send()

        def body(d, _):
            self.scatter(d).wait_send()
            self.gather(d).wait_send()
            self.forward(d).wait_send()
            return 0

        self.forward(0).wait_send()
        lax.fori_loop(1, 16, body, 0)


class TwoLevel(Reduction):
    @staticmethod
    def scratch(taps):
        n = slots_of(taps)
        return [
            pltpu.VMEM((2, 16, n, 8, C), BF),
            pltpu.VMEM((16, n, 8, C), BF),
            pltpu.VMEM((16, n, 8, C), BF),
            pltpu.VMEM((19, n, 8, C), BF),
            pltpu.VMEM((2, 16, n, 8, C), BF),
            pltpu.SemaphoreType.DMA((14,)),
            pltpu.SemaphoreType.DMA((14,)),
        ]

    def phase(self, n):
        p = self.place
        core, y, z, me = p["core"], p["y"], p["z"], p["me"]
        if n == 0:
            return [self.pair()]
        if n == 5:
            return [self.copy(self.fin.at[core], self.fin.at[core], 13, p["sibling"])]
        copies = []
        for d in range(3):
            yd, zd = lax.rem(y + d + 1, 4), lax.rem(z + d + 1, 4)
            above, beside = me + (yd - y) * 8, me + (zd - z) * 2
            if n == 1:
                src, dst = self.s0.at[pl.ds(4 * yd, 4)], self.r1.at[pl.ds(4 * d, 4)]
                copies.append(self.copy(src, dst, 1 + d, above))
            elif n == 2:
                copies.append(self.copy(self.r1.at[12 + zd], self.r1.at[16 + d], 4 + d, beside))
            elif n == 3:
                one = self.fin.at[core, 4 * y + z]
                copies.append(self.copy(one, one, 7 + d, beside))
            else:
                row = self.fin.at[core, pl.ds(4 * y, 4)]
                copies.append(self.copy(row, row, 10 + d, above))
        return copies

    def step(self, n):
        p = self.place
        core, y, z = p["core"], p["y"], p["z"]
        if n > 0:
            for c in self.phase(n - 1):
                c.wait_recv()
        if n == 1:

            def add(i, _):
                self.s0[i] = (self.g[core, i].astype(F32) + self.r0[i].astype(F32)).astype(BF)
                return 0

            lax.fori_loop(0, 16, add, 0)
        elif n == 2:
            for i in range(4):
                v = self.s0[4 * y + i].astype(F32)
                for d in range(3):
                    v = v + self.r1[4 * d + i].astype(F32)
                self.r1[12 + i] = v.astype(BF)
        elif n == 3:
            v = self.r1[12 + z].astype(F32)
            for d in range(3):
                v = v + self.r1[16 + d].astype(F32)
            self.fin[core, 4 * y + z] = v.astype(BF)
        if n < 6:
            for c in self.phase(n):
                c.start()

    def drain(self):
        for n in range(6):
            for c in self.phase(n):
                c.wait_send()


REDUCTIONS = ((TwoLevel, 12), (TwoLevel, 15), (Reduction, 12), (Reduction, 15))


def silu_parts(v):
    s = 1.0 / (1.0 + jnp.exp(-v))
    return s, s * (1.0 + v * (1.0 - s))


def kernel(
    scale,
    feats_h, mask_h, nbr_ref, w1_h, w2_h, cot_h,
    out_h, gin_h, gw2a_h, gw2b_h, gw1a_h, gw1b_h,
    feats, mask, w1, w2, cot, out_s,
    xin, xhid, xg, taps, maskb, pre1, early, gt,
    o0, o1, o2, o3, i0, i1, i2, i3,
    load_sem, store_sem, face_send, face_recv,
    *red_refs,
):
    grads_h = (gw2a_h, gw2b_h, gw1a_h, gw1b_h)
    me = lax.axis_index("space")
    n_space = 32
    core = lax.rem(me, 2)
    chip = me // 2
    z = lax.rem(chip, 4)
    y = chip // 4
    right, left = lax.rem(me + 1, n_space), lax.rem(me + n_space - 1, n_space)

    def chip_at(d):
        return 4 * lax.rem(y + d // 4, 4) + lax.rem(z + lax.rem(d, 4), 4)

    def behind(d):
        return 4 * lax.rem(y + 4 - d // 4, 4) + lax.rem(z + 4 - lax.rem(d, 4), 4)

    place = {
        "core": core, "sibling": me + 1 - 2 * core, "chip": chip_at, "behind": behind,
        "y": y, "z": z, "me": me,
    }
    first = 8 * (me - 1)
    red2a, red2b, red1a, red1b = (
        kind(place, taps_of, red_refs[7 * i : 7 * i + 7])
        for i, (kind, taps_of) in enumerate(REDUCTIONS)
    )

    loads = [
        pltpu.make_async_copy(src, dst, load_sem.at[i])
        for i, (src, dst) in enumerate(
            ((feats_h, feats), (mask_h, mask), (w1_h, w1), (w2_h, w2), (cot_h, cot))
        )
    ]
    for c in loads:
        c.start()

    barrier = pltpu.get_barrier_semaphore()
    for peer in (left, right):
        pl.semaphore_signal(barrier, inc=1, device_id={"space": peer}, device_id_type=MESH)

    def greet(d, _):
        peer = 2 * chip_at(d) + core
        pl.semaphore_signal(barrier, inc=1, device_id={"space": peer}, device_id_type=MESH)
        return 0

    lax.fori_loop(1, 16, greet, 0)
    pl.semaphore_wait(barrier, 17)

    faces = ((o0, i0), (o1, i1), (o2, i2), (o3, i3))

    def plane_copies(n, ref, slab, a):
        return [
            pltpu.make_async_remote_copy(
                src_ref=ref.at[slab, pl.ds(8, 8)],
                dst_ref=ref.at[slab, pl.ds(at, 8)],
                send_sem=face_send.at[n, side, a],
                recv_sem=face_recv.at[n, side, a],
                device_id={"space": peer},
                device_id_type=MESH,
            )
            for side, (at, peer) in enumerate(((0, right), (16, left)))
        ]

    def send_plane(n, a, v):
        outer, inner = faces[n]
        keep_faces(outer, inner, a, v)

        def start(ref, slab):
            for c in plane_copies(n, ref, slab, a):
                c.start()

        when_outer(a, lambda: start(outer, a // 7), lambda: start(inner, a - 1))

    def face_copies(n):
        outer, inner = faces[n]
        copies = []
        for a in range(8):
            if a in (0, 7):
                copies += plane_copies(n, outer, a // 7, a)
            else:
                copies += plane_copies(n, inner, a - 1, a)
        return copies

    def receive_faces(n, x_ref):
        for c in face_copies(n):
            c.wait_recv()
        fill_rim(x_ref, faces[n], nbr_ref, first)

    for outer, inner in faces:
        for side in range(2):
            outer[side, 24] = jnp.zeros((8, 8, C), BF)
        for a in range(6):
            inner[a, 24] = jnp.zeros((2, 8, C), BF)
    for red in (red2a, red2b, red1a, red1b):
        red.clear()
    for side in range(2):
        for a in (0, 1, 10, 11):
            gt[side, a] = jnp.zeros((C, 2 * C), BF)

    for x_ref in (xin, xhid):
        for column in (0, 9):
            x_ref[:, :, column] = jnp.zeros((4, 10, 16, 3 * C), BF)

    loads[1].wait()
    loads[0].wait()

    def mask_plane(t, _):
        a = jnp.where(t == 0, 0, jnp.where(t == 1, 7, t - 1))
        row = lax.broadcasted_iota(jnp.int32, (C, C), 0)
        lane = lax.broadcasted_iota(jnp.int32, (C, C), 1)
        hit = lane == lax.rem(a, 2) * 64 + (row // 16) * 8 + lax.rem(row, 8)
        second = lax.rem(row // 8, 2) == 1
        at = pl.ds(pl.multiple_of((a // 2) * C, C), C)
        pieces = []
        for p in range(4):
            m0 = mask[2 * p : 2 * p + 1, at].astype(F32)
            m1 = mask[2 * p + 1 : 2 * p + 2, at].astype(F32)
            pieces.append(jnp.where(hit, jnp.where(second, m1, m0), 0.0).astype(BF))
        spread = jnp.dot(
            jnp.concatenate(pieces, axis=0), jnp.ones((C, C), BF), preferred_element_type=F32
        )
        m = spread.reshape(4, 8, 16, C)
        maskb[a] = m.astype(BF)
        v = pair_plane(feats, a) * m
        send_plane(0, a, v)
        put_plane(xin, a, v)
        return 0

    lax.fori_loop(0, 8, mask_plane, 0)

    loads[2].wait()
    loads[3].wait()
    build_taps(taps.at[0], w1, False)
    build_taps(taps.at[2], w2, True)
    def first_done(a, v):
        pre1[a] = v
        s, _ = silu_parts(v)
        h = maskb[a].astype(F32) * (v * s)
        send_plane(1, a, h)
        put_plane(xhid, a, h)

    convolve_split(xin, taps.at[0], early, lambda: receive_faces(0, xin), first_done)
    build_taps(taps.at[1], w2, False)
    build_taps(taps.at[3], w1, True)
    loads[4].wait()

    def second_done(a, v):
        s, slope = silu_parts(v)
        m = maskb[a].astype(F32)
        unpair_plane(out_s, a, m * (v * s))
        g = pair_plane(cot, a) * m * slope
        send_plane(2, a, g)
        put_plane(xg, a, g)
        put_transposed(gt, a, g)

    convolve_split(xhid, taps.at[1], early, lambda: receive_faces(1, xhid), second_done)
    store_out = pltpu.make_async_copy(out_s, out_h, store_sem.at[0])
    store_out.start()

    weight_grad(xhid, gt, LEFT_COLUMNS, scale, lambda q, c, v: red2a.put(4 * (2 - q) + c, v))
    red2a.step(0)
    weight_grad(xhid, gt, RIGHT_COLUMNS, scale, lambda q, c, v: red2b.put(5 * (2 - q) + c - 4, v))
    red2b.step(0)
    red2a.step(1)
    receive_faces(2, xg)

    def third_done(a, v):
        _, slope = silu_parts(pre1[a])
        g = maskb[a].astype(F32) * slope * v
        send_plane(3, a, g)
        put_plane(xhid, a, g)
        put_transposed(gt, a, g)

    def third_between(q):
        @pl.when(q == 1)
        def _():
            red2b.step(1)

        @pl.when(q == 2)
        def _():
            red2a.step(2)

    convolve(xg, taps.at[2], third_done, third_between)
    store_out.wait()

    weight_grad(xin, gt, RIGHT_COLUMNS, scale, lambda q, c, v: red1b.put(5 * (2 - q) + c - 4, v))
    red1b.step(0)
    red2a.step(3)
    red2b.step(2)
    weight_grad(xin, gt, LEFT_COLUMNS, scale, lambda q, c, v: red1a.put(4 * (2 - q) + c, v))
    red1a.step(0)
    red1b.step(1)
    receive_faces(3, xhid)
    red2a.step(4)

    def last_done(a, v):
        unpair_plane(out_s, a, maskb[a].astype(F32) * v)

    def last_between(q):
        @pl.when(q == 0)
        def _():
            red1a.step(1)
            red2b.step(3)

        @pl.when(q == 3)
        def _():
            red2b.step(4)
            red1b.step(2)

    convolve(xhid, taps.at[3], last_done, last_between)
    reductions = (red2a, red2b, red1a, red1b)
    stores = [
        pltpu.make_async_copy(src, dst, store_sem.at[1 + i])
        for i, (src, dst) in enumerate(
            ((out_s, gin_h), *((red.fin, dst) for red, dst in zip(reductions, grads_h)))
        )
    ]
    stores[0].start()
    red1a.step(2)
    red2a.step(5)
    red2a.step(6)
    stores[1].start()
    red2b.step(5)
    red1b.step(3)
    red2b.step(6)
    stores[2].start()
    red1a.step(3)
    red1b.step(4)
    stores[4].start()
    red1a.step(4)
    stores[3].start()
    for n in range(4):
        for c in face_copies(n):
            c.wait_send()
    for red in (red2a, red2b, red1a, red1b):
        red.drain()
    for c in stores:
        c.wait()


def finish(
    out_t, gin_t, gw2a_t, gw2b_t, gw1a_t, gw1b_t,
    out_h, gin_h, gw1_h, gw2_h,
    fin2a, fin2b, fin1a, fin1b, w1, w2, out_s, gin_s, sem,
):
    pairs = (
        (gw2a_t, fin2a), (gw2b_t, fin2b), (gw1a_t, fin1a), (gw1b_t, fin1b),
        (out_t, out_s), (gin_t, gin_s),
    )
    reads = [pltpu.make_async_copy(src, dst, sem.at[i]) for i, (src, dst) in enumerate(pairs)]
    pairs = ((w2, gw2_h), (w1, gw1_h), (out_s, out_h), (gin_s, gin_h))
    writes = [pltpu.make_async_copy(src, dst, sem.at[6 + i]) for i, (src, dst) in enumerate(pairs)]
    for c in reads:
        c.start()

    def order(fin, tap, dst, to):
        for u in range(16):
            n = 8 * tap + u // 2
            dst[to, 8 * u : 8 * u + 8] = fin[u % 2, n % 16, n // 16].astype(F32)

    for i, (left, right, dst) in enumerate(((fin2a, fin2b, w2), (fin1a, fin1b, w1))):
        reads[2 * i].wait()
        reads[2 * i + 1].wait()
        for k in range(3):
            for c in LEFT_COLUMNS:
                order(left, 4 * k + c, dst, 9 * k + c)
            for c in RIGHT_COLUMNS:
                order(right, 5 * k + c - 4, dst, 9 * k + c)
        writes[i].start()
    for i in (4, 5):
        reads[i].wait()
        writes[i - 2].start()
    for c in writes:
        c.wait()


def body(feats, mask, neighbours, weight_one, weight_two, cotangent):
    bricks, voxels, channels = feats.shape
    scale = 1.0 / math.sqrt(voxels * bricks)
    cube = (bricks, 8, 8, 8, channels)
    field = pltpu.VMEM((4, 10, 10, 16, 3 * C), BF)
    outer, inner = pltpu.VMEM((2, 25, 8, 8, C), BF), pltpu.VMEM((6, 25, 2, 8, C), BF)
    anywhere = pl.BlockSpec(memory_space=pl.ANY)
    parts = [
        jax.ShapeDtypeStruct((4, 2, 8, 8, 8, C), BF),
        jax.ShapeDtypeStruct((4, 2, 8, 8, 8, C), BF),
        *(jax.ShapeDtypeStruct((2, 16, slots_of(n), 8, C), BF) for _, n in REDUCTIONS),
    ]
    left_over = pl.pallas_call(
        functools.partial(kernel, scale),
        out_shape=tuple(parts),
        in_specs=[
            anywhere, anywhere, pl.BlockSpec(memory_space=pltpu.SMEM), anywhere, anywhere, anywhere,
        ],
        out_specs=(anywhere,) * 6,
        scratch_shapes=[
            pltpu.VMEM(cube, BF),
            pltpu.VMEM((bricks, voxels), jnp.int32),
            pltpu.VMEM((27, C, C), BF),
            pltpu.VMEM((27, C, C), BF),
            pltpu.VMEM(cube, BF),
            pltpu.VMEM((4, 2, 8, 8, 8, C), BF),
            field, field, field,
            pltpu.VMEM((4, 36, C, 2 * C), BF),
            pltpu.VMEM((8, 4, 8, 16, C), BF),
            pltpu.VMEM((8, 4, 8, 16, C), F32),
            pltpu.VMEM((4, 4, 8, 16, C), F32),
            pltpu.VMEM((2, 12, C, 2 * C), BF),
            *[outer] * 4,
            *[inner] * 4,
            pltpu.SemaphoreType.DMA((5,)),
            pltpu.SemaphoreType.DMA((6,)),
            pltpu.SemaphoreType.DMA((4, 2, 8)),
            pltpu.SemaphoreType.DMA((4, 2, 8)),
            *(ref for kind, n in REDUCTIONS for ref in kind.scratch(n)),
        ],
        compiler_params=pltpu.CompilerParams(
            collective_id=0, has_side_effects=True, vmem_limit_bytes=60 * 2**20
        ),
        name="bricks",
    )(feats.reshape(cube), mask, neighbours, weight_one, weight_two, cotangent.reshape(cube))

    out, gin, gw1, gw2 = pl.pallas_call(
        finish,
        out_shape=(
            *parts[:2],
            jax.ShapeDtypeStruct((27, C, C), F32),
            jax.ShapeDtypeStruct((27, C, C), F32),
        ),
        in_specs=[anywhere] * 6,
        out_specs=(anywhere,) * 4,
        scratch_shapes=[
            *(pltpu.VMEM(p.shape, BF) for p in parts[2:]),
            pltpu.VMEM((27, C, C), F32),
            pltpu.VMEM((27, C, C), F32),
            pltpu.VMEM(parts[0].shape, BF),
            pltpu.VMEM(parts[1].shape, BF),
            pltpu.SemaphoreType.DMA((10,)),
        ],
        name="outputs",
    )(*left_over)
    return (
        out.reshape(bricks, voxels, channels),
        gin.reshape(bricks, voxels, channels),
        gw1,
        gw2,
    )


def solution(mesh):
    in_specs = (
        P(("scene", "space"), None, None),
        P(("scene", "space"), None),
        P(("scene", "space"), None),
        P(),
        P(),
        P(("scene", "space"), None, None),
    )
    out_specs = (
        P(("scene", "space"), None, None),
        P(("scene", "space"), None, None),
        P("scene", None, None),
        P("scene", None, None),
    )
    return jax.shard_map(body, mesh=mesh, in_specs=in_specs, out_specs=out_specs, check_vma=False)
```

```python
import functools
import math

import jax
import jax.numpy as jnp
from jax import lax
from jax.experimental import pallas as pl
from jax.experimental.pallas import tpu as pltpu
from jax.sharding import PartitionSpec as P

BF = jnp.bfloat16
F32 = jnp.float32
C = 128
MESH = pl.DeviceIdType.MESH


def shifted(v):
    row = lax.broadcasted_iota(jnp.int32, v.shape, v.ndim - 1 - 1)
    down = jnp.where(row == 0, 0.0, pltpu.roll(v, 1, v.ndim - 2))
    up = jnp.where(row == 7, 0.0, pltpu.roll(v, 7, v.ndim - 2))
    return down, v, up


def put_plane(x_ref, a, v):
    for k, s in enumerate(shifted(v.reshape(64, 8, C))):
        x_ref[:, 1 + a, 1:9, :, C * k : C * k + C] = s.reshape(4, 8, 16, C).astype(BF)


def pair_plane(ref, a):
    v = ref[:, a].astype(F32).reshape(4, 2, 8, 8, C)
    return jnp.stack([v[:, 0], v[:, 1]], axis=2).reshape(4, 8, 16, C)


def unpair_plane(ref, a, v):
    w = v.reshape(4, 8, 2, 8, C)
    for half in range(2):
        ref[:, half, a] = w[:, :, half].astype(BF)


def when_outer(a, run_outer, run_inner):
    if isinstance(a, int):
        run_outer() if a in (0, 7) else run_inner()
        return
    pl.when((a == 0) | (a == 7))(run_outer)
    pl.when((a > 0) & (a < 7))(run_inner)


def keep_faces(outer, inner, a, v):
    w = v.reshape(4, 8, 2, 8, C)

    def whole():
        for p in range(4):
            for half in range(2):
                outer[a // 7, 8 + 2 * p + half] = w[p, :, half].astype(BF)

    def ends():
        for p in range(4):
            for half in range(2):
                inner[a - 1, 8 + 2 * p + half, 0] = w[p, 0, half].astype(BF)
                inner[a - 1, 8 + 2 * p + half, 1] = w[p, 7, half].astype(BF)

    when_outer(a, whole, ends)


def fill_rim(x_ref, faces, nbr_ref, first):
    outer, inner = faces

    def body(p, _):
        def source(column):
            out = []
            for half in range(2):
                n = nbr_ref[2 * p + half, column]
                out.append(jnp.where(n >= 0, jnp.clip(n - first, 0, 23), 24))
            return out

        def cell(x, y, i, j):
            w = jnp.stack([x.astype(F32), y.astype(F32)], axis=0)
            for k, s in enumerate(shifted(w)):
                x_ref[p, i, j, :, C * k : C * k + C] = s.reshape(16, C).astype(BF)

        for column, side, where, i, j in (
            (0, 1, 7, 0, 0), (2, 1, 0, 0, 9), (5, 0, 7, 9, 0), (7, 0, 0, 9, 9),
        ):
            m, n = source(column)
            cell(outer[side, m, where], outer[side, n, where], i, j)
        for column, side, i in ((1, 1, 0), (6, 0, 9)):
            m, n = source(column)
            u, v = outer[side, m].astype(F32), outer[side, n].astype(F32)
            w = jnp.stack([u, v], axis=1).reshape(16, 8, C)
            for k, s in enumerate(shifted(w)):
                x_ref[p, i, 1:9, :, C * k : C * k + C] = s.reshape(8, 16, C).astype(BF)
        for column, end, j in ((3, 1, 0), (4, 0, 9)):
            m, n = source(column)
            cell(outer[0, m, 7 * end], outer[0, n, 7 * end], 1, j)
            for a in range(1, 7):
                cell(inner[a - 1, m, end], inner[a - 1, n, end], 1 + a, j)
            cell(outer[1, m, 7 * end], outer[1, n, 7 * end], 8, j)
        return 0

    lax.fori_loop(0, 4, body, 0)


def build_taps(t_ref, w_ref, flipped):
    def body(t, _):
        zero = jnp.zeros((C, C), BF)
        t_ref[t, :, C:] = zero
        t_ref[27 + t, :, :C] = zero
        for k in range(3):
            if flipped:
                w = w_ref[26 - (9 * k + t)].T
            else:
                w = w_ref[9 * k + t]
            t_ref[9 * k + t, :, :C] = w
            t_ref[9 * k + 9 + t, :, C:] = w
        return 0

    lax.fori_loop(0, 9, body, 0)


def convolve(x_ref, t_ref, epilogue, between=None):
    def body(t, _):
        q = jnp.where(t == 0, 0, jnp.where(t == 1, 3, t - 1))
        windows = [
            x_ref[:, 2 * q + p, k : k + 8].reshape(512, 3 * C) for p in range(4) for k in range(3)
        ]
        total = jnp.dot(
            jnp.concatenate(windows, axis=1),
            t_ref[...].reshape(36 * C, 2 * C),
            preferred_element_type=F32,
        )
        for u in range(2):
            epilogue(2 * q + u, total[:, C * u : C * u + C].reshape(4, 8, 16, C))
        if between is not None:
            between(t)
        return 0

    lax.fori_loop(0, 4, body, 0)


def convolve_split(x_ref, t_ref, inner_ref, arrive, epilogue):
    def pair(q):
        windows = [
            x_ref[:, 2 * q + p, k : k + 8].reshape(512, 3 * C) for p in range(4) for k in range(3)
        ]
        total = jnp.dot(
            jnp.concatenate(windows, axis=1),
            t_ref[...].reshape(36 * C, 2 * C),
            preferred_element_type=F32,
        )
        return [total[:, C * u : C * u + C].reshape(4, 8, 16, C) for u in range(2)]

    def early(t, _):
        for u, v in enumerate(pair(1 + t)):
            inner_ref[2 * t + u] = v
        return 0

    lax.fori_loop(0, 2, early, 0)
    arrive()
    for end, column, k in ((0, 0, 0), (7, 9, 2)):
        left = [x_ref[:, 2 + p : 6 + p, column].reshape(256, 3 * C) for p in range(3)]
        right = [t_ref[9 * p + 3 * k : 9 * p + 3 * k + 3, :, :C].reshape(3 * C, C) for p in range(3)]
        d = jnp.dot(
            jnp.concatenate(left, axis=1),
            jnp.concatenate(right, axis=0),
            preferred_element_type=F32,
        ).reshape(4, 4, 16, C)
        for a in range(4):
            inner_ref[a, :, end] += d[:, a]
    for t in range(2):
        outer = pair(3 * t)
        for u in range(2):
            epilogue(2 + 2 * t + u, inner_ref[2 * t + u])
        for u in range(2):
            epilogue(6 * t + u, outer[u])


def put_transposed(gt_ref, a, v):
    flat = v.reshape(4, C, C).astype(BF)
    for p in range(4):
        gt_ref[p // 2, a + 2, :, C * (p % 2) : C * (p % 2) + C] = flat[p].T


def weight_grad(x_ref, gt_ref, columns, scale, store):
    totals = [None] * 3
    for i in range(0, 10, 2):
        low, high = (1 if i == 0 else 0), (2 if i == 8 else 3)
        left = jnp.concatenate(
            [
                gt_ref[h, i + q + low : i + q + high].reshape(C * (high - low), 2 * C)
                for q in range(2)
                for h in range(2)
            ],
            axis=1,
        )
        right = jnp.concatenate(
            [
                jnp.concatenate(
                    [
                        x_ref[:, i + q, c // 3 : c // 3 + 8, :, C * (c % 3) : C * (c % 3) + C]
                        .reshape(512, C)
                        for c in columns
                    ],
                    axis=1,
                )
                for q in range(2)
            ],
            axis=0,
        )
        d = jnp.dot(left, right, preferred_element_type=F32)
        for q in range(low, high):
            part = d[C * (q - low) : C * (q - low) + C]
            totals[q] = part if totals[q] is None else totals[q] + part
    for q in range(3):
        for n, c in enumerate(columns):
            store(q, c, (totals[q][:, C * n : C * n + C] * scale).T)


LEFT_COLUMNS, RIGHT_COLUMNS = range(4), range(4, 9)


def slots_of(taps):
    return (taps + 1) // 2


class Reduction:
    def __init__(self, place, taps, refs):
        self.place = place
        self.taps = taps
        self.g, self.r0, self.s0, self.r1, self.fin, self.send, self.recv = refs

    @staticmethod
    def scratch(taps):
        n = slots_of(taps)
        return [
            pltpu.VMEM((2, 16, n, 8, C), BF),
            pltpu.VMEM((16, n, 8, C), BF),
            pltpu.VMEM((16, n, 8, C), BF),
            pltpu.VMEM((15, n, 8, C), BF),
            pltpu.VMEM((2, 16, n, 8, C), BF),
            pltpu.SemaphoreType.DMA((47,)),
            pltpu.SemaphoreType.DMA((47,)),
        ]

    def clear(self):
        if self.taps % 2:
            self.g[:, 8:, slots_of(self.taps) - 1] = jnp.zeros((2, 8, 8, C), BF)

    def put(self, tap, block):
        for u in range(16):
            n = 8 * tap + u // 2
            self.g[u % 2, n % 16, n // 16] = block[8 * u : 8 * u + 8].astype(BF)

    def copy(self, src, dst, slot, peer):
        return pltpu.make_async_remote_copy(
            src_ref=src,
            dst_ref=dst,
            send_sem=self.send.at[slot],
            recv_sem=self.recv.at[slot],
            device_id={"space": peer},
            device_id_type=MESH,
        )

    def pair(self):
        return self.copy(self.g.at[1 - self.place["core"]], self.r0, 0, self.place["sibling"])

    def scatter(self, d):
        chip = self.place["chip"](d)
        return self.copy(
            self.s0.at[chip], self.r1.at[d - 1], d, 2 * chip + self.place["core"]
        )

    def gather(self, d):
        mine = self.fin.at[self.place["core"], self.place["chip"](0)]
        return self.copy(mine, mine, 15 + d, 2 * self.place["chip"](d) + self.place["core"])

    def forward(self, d):
        one = self.fin.at[self.place["core"], self.place["behind"](d)]
        return self.copy(one, one, 31 + d, self.place["sibling"])

    def step(self, n):
        core, chip = self.place["core"], self.place["chip"]

        def each(low, run):
            def body(d, _):
                run(d)
                return 0

            lax.fori_loop(low, 16, body, 0)

        if n == 0:
            self.pair().start()
        elif n == 1:
            self.pair().wait_recv()

            def add(c):
                self.s0[c] = (self.g[core, c].astype(F32) + self.r0[c].astype(F32)).astype(BF)

            def send(d):
                add(chip(d))
                self.scatter(d).start()

            each(1, send)
            add(chip(0))
        elif n == 2:
            each(1, lambda d: self.scatter(d).wait_recv())
            v = self.s0[chip(0)].astype(F32)
            for d in range(15):
                v = v + self.r1[d].astype(F32)
            self.fin[core, chip(0)] = v.astype(BF)
            each(1, lambda d: self.gather(d).start())
            self.forward(0).start()
        elif n == 3:

            def pass_on(d):
                self.gather(d).wait_recv()
                self.forward(d).start()

            each(1, pass_on)
        else:
            each(0, lambda d: self.forward(d).wait_recv())

    def drain(self):
        self.pair().wait_send()

        def body(d, _):
            self.scatter(d).wait_send()
            self.gather(d).wait_send()
            self.forward(d).wait_send()
            return 0

        self.forward(0).wait_send()
        lax.fori_loop(1, 16, body, 0)


def silu_parts(v):
    s = 1.0 / (1.0 + jnp.exp(-v))
    return s, s * (1.0 + v * (1.0 - s))


def kernel(
    scale,
    feats_h, mask_h, nbr_ref, w1_h, w2_h, cot_h,
    out_h, gin_h, gw2a_h, gw2b_h, gw1a_h, gw1b_h,
    feats, mask, w1, w2, cot, out_s,
    xin, xhid, xg, taps, maskb, pre1, early, gt,
    o0, o1, o2, o3, i0, i1, i2, i3,
    load_sem, store_sem, face_send, face_recv,
    *red_refs,
):
    grads_h = (gw2a_h, gw2b_h, gw1a_h, gw1b_h)
    me = lax.axis_index("space")
    n_space = 32
    core = lax.rem(me, 2)
    chip = me // 2
    z = lax.rem(chip, 4)
    y = chip // 4
    right, left = lax.rem(me + 1, n_space), lax.rem(me + n_space - 1, n_space)

    def chip_at(d):
        return 4 * lax.rem(y + d // 4, 4) + lax.rem(z + lax.rem(d, 4), 4)

    def behind(d):
        return 4 * lax.rem(y + 4 - d // 4, 4) + lax.rem(z + 4 - lax.rem(d, 4), 4)

    place = {"core": core, "sibling": me + 1 - 2 * core, "chip": chip_at, "behind": behind}
    first = 8 * (me - 1)
    red2a, red2b, red1a, red1b = (
        Reduction(place, taps_of, red_refs[7 * i : 7 * i + 7])
        for i, taps_of in enumerate((12, 15, 12, 15))
    )

    loads = [
        pltpu.make_async_copy(src, dst, load_sem.at[i])
        for i, (src, dst) in enumerate(
            ((feats_h, feats), (mask_h, mask), (w1_h, w1), (w2_h, w2), (cot_h, cot))
        )
    ]
    for c in loads:
        c.start()

    barrier = pltpu.get_barrier_semaphore()
    for peer in (left, right):
        pl.semaphore_signal(barrier, inc=1, device_id={"space": peer}, device_id_type=MESH)

    def greet(d, _):
        peer = 2 * chip_at(d) + core
        pl.semaphore_signal(barrier, inc=1, device_id={"space": peer}, device_id_type=MESH)
        return 0

    lax.fori_loop(1, 16, greet, 0)
    pl.semaphore_wait(barrier, 17)

    faces = ((o0, i0), (o1, i1), (o2, i2), (o3, i3))

    def plane_copies(n, ref, slab, a):
        return [
            pltpu.make_async_remote_copy(
                src_ref=ref.at[slab, pl.ds(8, 8)],
                dst_ref=ref.at[slab, pl.ds(at, 8)],
                send_sem=face_send.at[n, side, a],
                recv_sem=face_recv.at[n, side, a],
                device_id={"space": peer},
                device_id_type=MESH,
            )
            for side, (at, peer) in enumerate(((0, right), (16, left)))
        ]

    def send_plane(n, a, v):
        outer, inner = faces[n]
        keep_faces(outer, inner, a, v)

        def start(ref, slab):
            for c in plane_copies(n, ref, slab, a):
                c.start()

        when_outer(a, lambda: start(outer, a // 7), lambda: start(inner, a - 1))

    def face_copies(n):
        outer, inner = faces[n]
        copies = []
        for a in range(8):
            if a in (0, 7):
                copies += plane_copies(n, outer, a // 7, a)
            else:
                copies += plane_copies(n, inner, a - 1, a)
        return copies

    def receive_faces(n, x_ref):
        for c in face_copies(n):
            c.wait_recv()
        fill_rim(x_ref, faces[n], nbr_ref, first)

    for outer, inner in faces:
        for side in range(2):
            outer[side, 24] = jnp.zeros((8, 8, C), BF)
        for a in range(6):
            inner[a, 24] = jnp.zeros((2, 8, C), BF)
    for red in (red2a, red2b, red1a, red1b):
        red.clear()
    for side in range(2):
        for a in (0, 1, 10, 11):
            gt[side, a] = jnp.zeros((C, 2 * C), BF)

    for x_ref in (xin, xhid):
        for column in (0, 9):
            x_ref[:, :, column] = jnp.zeros((4, 10, 16, 3 * C), BF)

    loads[1].wait()
    loads[0].wait()

    def mask_plane(t, _):
        a = jnp.where(t == 0, 0, jnp.where(t == 1, 7, t - 1))
        row = lax.broadcasted_iota(jnp.int32, (C, C), 0)
        lane = lax.broadcasted_iota(jnp.int32, (C, C), 1)
        hit = lane == lax.rem(a, 2) * 64 + (row // 16) * 8 + lax.rem(row, 8)
        second = lax.rem(row // 8, 2) == 1
        at = pl.ds(pl.multiple_of((a // 2) * C, C), C)
        pieces = []
        for p in range(4):
            m0 = mask[2 * p : 2 * p + 1, at].astype(F32)
            m1 = mask[2 * p + 1 : 2 * p + 2, at].astype(F32)
            pieces.append(jnp.where(hit, jnp.where(second, m1, m0), 0.0).astype(BF))
        spread = jnp.dot(
            jnp.concatenate(pieces, axis=0), jnp.ones((C, C), BF), preferred_element_type=F32
        )
        m = spread.reshape(4, 8, 16, C)
        maskb[a] = m.astype(BF)
        v = pair_plane(feats, a) * m
        send_plane(0, a, v)
        put_plane(xin, a, v)
        return 0

    lax.fori_loop(0, 8, mask_plane, 0)

    loads[2].wait()
    loads[3].wait()
    build_taps(taps.at[0], w1, False)
    build_taps(taps.at[2], w2, True)
    def first_done(a, v):
        pre1[a] = v
        s, _ = silu_parts(v)
        h = maskb[a].astype(F32) * (v * s)
        send_plane(1, a, h)
        put_plane(xhid, a, h)

    convolve_split(xin, taps.at[0], early, lambda: receive_faces(0, xin), first_done)
    build_taps(taps.at[1], w2, False)
    build_taps(taps.at[3], w1, True)
    loads[4].wait()

    def second_done(a, v):
        s, slope = silu_parts(v)
        m = maskb[a].astype(F32)
        unpair_plane(out_s, a, m * (v * s))
        g = pair_plane(cot, a) * m * slope
        send_plane(2, a, g)
        put_plane(xg, a, g)
        put_transposed(gt, a, g)

    convolve_split(xhid, taps.at[1], early, lambda: receive_faces(1, xhid), second_done)
    store_out = pltpu.make_async_copy(out_s, out_h, store_sem.at[0])
    store_out.start()

    weight_grad(xhid, gt, LEFT_COLUMNS, scale, lambda q, c, v: red2a.put(4 * (2 - q) + c, v))
    red2a.step(0)
    weight_grad(xhid, gt, RIGHT_COLUMNS, scale, lambda q, c, v: red2b.put(5 * (2 - q) + c - 4, v))
    red2b.step(0)
    red2a.step(1)
    receive_faces(2, xg)

    def third_done(a, v):
        _, slope = silu_parts(pre1[a])
        g = maskb[a].astype(F32) * slope * v
        send_plane(3, a, g)
        put_plane(xhid, a, g)
        put_transposed(gt, a, g)

    def third_between(q):
        @pl.when(q == 0)
        def _():
            red2b.step(1)

        @pl.when(q == 3)
        def _():
            red2a.step(2)

    convolve(xg, taps.at[2], third_done, third_between)
    store_out.wait()

    weight_grad(xin, gt, LEFT_COLUMNS, scale, lambda q, c, v: red1a.put(4 * (2 - q) + c, v))
    red1a.step(0)
    red2b.step(2)
    weight_grad(xin, gt, RIGHT_COLUMNS, scale, lambda q, c, v: red1b.put(5 * (2 - q) + c - 4, v))
    red1b.step(0)
    red1a.step(1)
    receive_faces(3, xhid)

    def last_done(a, v):
        unpair_plane(out_s, a, maskb[a].astype(F32) * v)

    def last_between(q):
        @pl.when(q == 0)
        def _():
            red1b.step(1)

        @pl.when(q == 1)
        def _():
            red2a.step(3)

        @pl.when(q == 2)
        def _():
            red1a.step(2)

        @pl.when(q == 3)
        def _():
            red1b.step(2)

    convolve(xhid, taps.at[3], last_done, last_between)
    reductions = (red2a, red2b, red1a, red1b)
    stores = [
        pltpu.make_async_copy(src, dst, store_sem.at[1 + i])
        for i, (src, dst) in enumerate(
            ((out_s, gin_h), *((red.fin, dst) for red, dst in zip(reductions, grads_h)))
        )
    ]
    stores[0].start()
    red2b.step(3)
    red1a.step(3)
    red2a.step(4)
    stores[1].start()
    red2b.step(4)
    stores[2].start()
    red1b.step(3)
    red1a.step(4)
    stores[3].start()
    red1b.step(4)
    stores[4].start()
    for n in range(4):
        for c in face_copies(n):
            c.wait_send()
    for red in (red2a, red2b, red1a, red1b):
        red.drain()
    for c in stores:
        c.wait()


def finish(
    out_t, gin_t, gw2a_t, gw2b_t, gw1a_t, gw1b_t,
    out_h, gin_h, gw1_h, gw2_h,
    fin2a, fin2b, fin1a, fin1b, w1, w2, out_s, gin_s, sem,
):
    pairs = (
        (gw2a_t, fin2a), (gw2b_t, fin2b), (gw1a_t, fin1a), (gw1b_t, fin1b),
        (out_t, out_s), (gin_t, gin_s),
    )
    reads = [pltpu.make_async_copy(src, dst, sem.at[i]) for i, (src, dst) in enumerate(pairs)]
    pairs = ((w2, gw2_h), (w1, gw1_h), (out_s, out_h), (gin_s, gin_h))
    writes = [pltpu.make_async_copy(src, dst, sem.at[6 + i]) for i, (src, dst) in enumerate(pairs)]
    for c in reads:
        c.start()

    def order(fin, tap, dst, to):
        for u in range(16):
            n = 8 * tap + u // 2
            dst[to, 8 * u : 8 * u + 8] = fin[u % 2, n % 16, n // 16].astype(F32)

    for i, (left, right, dst) in enumerate(((fin2a, fin2b, w2), (fin1a, fin1b, w1))):
        reads[2 * i].wait()
        reads[2 * i + 1].wait()
        for k in range(3):
            for c in LEFT_COLUMNS:
                order(left, 4 * k + c, dst, 9 * k + c)
            for c in RIGHT_COLUMNS:
                order(right, 5 * k + c - 4, dst, 9 * k + c)
        writes[i].start()
    for i in (4, 5):
        reads[i].wait()
        writes[i - 2].start()
    for c in writes:
        c.wait()


def body(feats, mask, neighbours, weight_one, weight_two, cotangent):
    bricks, voxels, channels = feats.shape
    scale = 1.0 / math.sqrt(voxels * bricks)
    cube = (bricks, 8, 8, 8, channels)
    field = pltpu.VMEM((4, 10, 10, 16, 3 * C), BF)
    outer, inner = pltpu.VMEM((2, 25, 8, 8, C), BF), pltpu.VMEM((6, 25, 2, 8, C), BF)
    anywhere = pl.BlockSpec(memory_space=pl.ANY)
    parts = [
        jax.ShapeDtypeStruct((4, 2, 8, 8, 8, C), BF),
        jax.ShapeDtypeStruct((4, 2, 8, 8, 8, C), BF),
        *(jax.ShapeDtypeStruct((2, 16, slots_of(n), 8, C), BF) for n in (12, 15, 12, 15)),
    ]
    left_over = pl.pallas_call(
        functools.partial(kernel, scale),
        out_shape=tuple(parts),
        in_specs=[
            anywhere, anywhere, pl.BlockSpec(memory_space=pltpu.SMEM), anywhere, anywhere, anywhere,
        ],
        out_specs=(anywhere,) * 6,
        scratch_shapes=[
            pltpu.VMEM(cube, BF),
            pltpu.VMEM((bricks, voxels), jnp.int32),
            pltpu.VMEM((27, C, C), BF),
            pltpu.VMEM((27, C, C), BF),
            pltpu.VMEM(cube, BF),
            pltpu.VMEM((4, 2, 8, 8, 8, C), BF),
            field, field, field,
            pltpu.VMEM((4, 36, C, 2 * C), BF),
            pltpu.VMEM((8, 4, 8, 16, C), BF),
            pltpu.VMEM((8, 4, 8, 16, C), F32),
            pltpu.VMEM((4, 4, 8, 16, C), F32),
            pltpu.VMEM((2, 12, C, 2 * C), BF),
            *[outer] * 4,
            *[inner] * 4,
            pltpu.SemaphoreType.DMA((5,)),
            pltpu.SemaphoreType.DMA((6,)),
            pltpu.SemaphoreType.DMA((4, 2, 8)),
            pltpu.SemaphoreType.DMA((4, 2, 8)),
            *(ref for n in (12, 15, 12, 15) for ref in Reduction.scratch(n)),
        ],
        compiler_params=pltpu.CompilerParams(
            collective_id=0, has_side_effects=True, vmem_limit_bytes=60 * 2**20
        ),
        name="bricks",
    )(feats.reshape(cube), mask, neighbours, weight_one, weight_two, cotangent.reshape(cube))

    out, gin, gw1, gw2 = pl.pallas_call(
        finish,
        out_shape=(
            *parts[:2],
            jax.ShapeDtypeStruct((27, C, C), F32),
            jax.ShapeDtypeStruct((27, C, C), F32),
        ),
        in_specs=[anywhere] * 6,
        out_specs=(anywhere,) * 4,
        scratch_shapes=[
            *(pltpu.VMEM(p.shape, BF) for p in parts[2:]),
            pltpu.VMEM((27, C, C), F32),
            pltpu.VMEM((27, C, C), F32),
            pltpu.VMEM(parts[0].shape, BF),
            pltpu.VMEM(parts[1].shape, BF),
            pltpu.SemaphoreType.DMA((10,)),
        ],
        name="outputs",
    )(*left_over)
    return (
        out.reshape(bricks, voxels, channels),
        gin.reshape(bricks, voxels, channels),
        gw1,
        gw2,
    )


def solution(mesh):
    in_specs = (
        P(("scene", "space"), None, None),
        P(("scene", "space"), None),
        P(("scene", "space"), None),
        P(),
        P(),
        P(("scene", "space"), None, None),
    )
    out_specs = (
        P(("scene", "space"), None, None),
        P(("scene", "space"), None, None),
        P("scene", None, None),
        P("scene", None, None),
    )
    return jax.shard_map(body, mesh=mesh, in_specs=in_specs, out_specs=out_specs, check_vma=False)
```

```python
import functools
import math

import jax
import jax.numpy as jnp
from jax import lax
from jax.experimental import pallas as pl
from jax.experimental.pallas import tpu as pltpu
from jax.sharding import PartitionSpec as P

BF = jnp.bfloat16
F32 = jnp.float32
C = 128
MESH = pl.DeviceIdType.MESH


def shifted(v):
    row = lax.broadcasted_iota(jnp.int32, v.shape, v.ndim - 1 - 1)
    down = jnp.where(row == 0, 0.0, pltpu.roll(v, 1, v.ndim - 2))
    up = jnp.where(row == 7, 0.0, pltpu.roll(v, 7, v.ndim - 2))
    return down, v, up


def put_plane(x_ref, a, v):
    for k, s in enumerate(shifted(v.reshape(64, 8, C))):
        x_ref[:, 1 + a, 1:9, :, C * k : C * k + C] = s.reshape(4, 8, 16, C).astype(BF)


def pair_plane(ref, a):
    v = ref[:, a].astype(F32).reshape(4, 2, 8, 8, C)
    return jnp.stack([v[:, 0], v[:, 1]], axis=2).reshape(4, 8, 16, C)


def unpair_plane(ref, a, v):
    w = v.reshape(4, 8, 2, 8, C)
    for half in range(2):
        ref[:, half, a] = w[:, :, half].astype(BF)


def when_outer(a, run_outer, run_inner):
    if isinstance(a, int):
        run_outer() if a in (0, 7) else run_inner()
        return
    pl.when((a == 0) | (a == 7))(run_outer)
    pl.when((a > 0) & (a < 7))(run_inner)


def keep_faces(outer, inner, a, v):
    w = v.reshape(4, 8, 2, 8, C)

    def whole():
        for p in range(4):
            for half in range(2):
                outer[a // 7, 8 + 2 * p + half] = w[p, :, half].astype(BF)

    def ends():
        for p in range(4):
            for half in range(2):
                inner[a - 1, 8 + 2 * p + half, 0] = w[p, 0, half].astype(BF)
                inner[a - 1, 8 + 2 * p + half, 1] = w[p, 7, half].astype(BF)

    when_outer(a, whole, ends)


def fill_rim(x_ref, faces, nbr_ref, first):
    outer, inner = faces

    def body(p, _):
        def source(column):
            out = []
            for half in range(2):
                n = nbr_ref[2 * p + half, column]
                out.append(jnp.where(n >= 0, jnp.clip(n - first, 0, 23), 24))
            return out

        def cell(x, y, i, j):
            w = jnp.stack([x.astype(F32), y.astype(F32)], axis=0)
            for k, s in enumerate(shifted(w)):
                x_ref[p, i, j, :, C * k : C * k + C] = s.reshape(16, C).astype(BF)

        for column, side, where, i, j in (
            (0, 1, 7, 0, 0), (2, 1, 0, 0, 9), (5, 0, 7, 9, 0), (7, 0, 0, 9, 9),
        ):
            m, n = source(column)
            cell(outer[side, m, where], outer[side, n, where], i, j)
        for column, side, i in ((1, 1, 0), (6, 0, 9)):
            m, n = source(column)
            u, v = outer[side, m].astype(F32), outer[side, n].astype(F32)
            w = jnp.stack([u, v], axis=1).reshape(16, 8, C)
            for k, s in enumerate(shifted(w)):
                x_ref[p, i, 1:9, :, C * k : C * k + C] = s.reshape(8, 16, C).astype(BF)
        for column, end, j in ((3, 1, 0), (4, 0, 9)):
            m, n = source(column)
            cell(outer[0, m, 7 * end], outer[0, n, 7 * end], 1, j)
            for a in range(1, 7):
                cell(inner[a - 1, m, end], inner[a - 1, n, end], 1 + a, j)
            cell(outer[1, m, 7 * end], outer[1, n, 7 * end], 8, j)
        return 0

    lax.fori_loop(0, 4, body, 0)


def build_taps(t_ref, w_ref, flipped):
    def body(t, _):
        zero = jnp.zeros((C, C), BF)
        t_ref[t, :, C:] = zero
        t_ref[27 + t, :, :C] = zero
        for k in range(3):
            if flipped:
                w = w_ref[26 - (9 * k + t)].T
            else:
                w = w_ref[9 * k + t]
            t_ref[9 * k + t, :, :C] = w
            t_ref[9 * k + 9 + t, :, C:] = w
        return 0

    lax.fori_loop(0, 9, body, 0)


def convolve(x_ref, t_ref, epilogue, between=None):
    def body(t, _):
        q = jnp.where(t == 0, 0, jnp.where(t == 1, 3, t - 1))
        windows = [
            x_ref[:, 2 * q + p, k : k + 8].reshape(512, 3 * C) for p in range(4) for k in range(3)
        ]
        total = jnp.dot(
            jnp.concatenate(windows, axis=1),
            t_ref[...].reshape(36 * C, 2 * C),
            preferred_element_type=F32,
        )
        for u in range(2):
            epilogue(2 * q + u, total[:, C * u : C * u + C].reshape(4, 8, 16, C))
        if between is not None:
            between(t)
        return 0

    lax.fori_loop(0, 4, body, 0)


def convolve_split(x_ref, t_ref, inner_ref, arrive, epilogue):
    def pair(q):
        windows = [
            x_ref[:, 2 * q + p, k : k + 8].reshape(512, 3 * C) for p in range(4) for k in range(3)
        ]
        total = jnp.dot(
            jnp.concatenate(windows, axis=1),
            t_ref[...].reshape(36 * C, 2 * C),
            preferred_element_type=F32,
        )
        return [total[:, C * u : C * u + C].reshape(4, 8, 16, C) for u in range(2)]

    def early(t, _):
        for u, v in enumerate(pair(1 + t)):
            inner_ref[2 * t + u] = v
        return 0

    lax.fori_loop(0, 2, early, 0)
    arrive()
    for end, column, k in ((0, 0, 0), (7, 9, 2)):
        left = [x_ref[:, 2 + p : 6 + p, column].reshape(256, 3 * C) for p in range(3)]
        right = [t_ref[9 * p + 3 * k : 9 * p + 3 * k + 3, :, :C].reshape(3 * C, C) for p in range(3)]
        d = jnp.dot(
            jnp.concatenate(left, axis=1),
            jnp.concatenate(right, axis=0),
            preferred_element_type=F32,
        ).reshape(4, 4, 16, C)
        for a in range(4):
            inner_ref[a, :, end] += d[:, a]
    for t in range(2):
        outer = pair(3 * t)
        for u in range(2):
            epilogue(2 + 2 * t + u, inner_ref[2 * t + u])
        for u in range(2):
            epilogue(6 * t + u, outer[u])


def put_transposed(gt_ref, a, v):
    flat = v.reshape(4, C, C).astype(BF)
    for p in range(4):
        gt_ref[p // 2, a + 2, :, C * (p % 2) : C * (p % 2) + C] = flat[p].T


def weight_grad(x_ref, gt_ref, columns, scale, store):
    totals = [None] * 3
    for i in range(0, 10, 2):
        low, high = (1 if i == 0 else 0), (2 if i == 8 else 3)
        left = jnp.concatenate(
            [
                gt_ref[h, i + q + low : i + q + high].reshape(C * (high - low), 2 * C)
                for q in range(2)
                for h in range(2)
            ],
            axis=1,
        )
        right = jnp.concatenate(
            [
                jnp.concatenate(
                    [
                        x_ref[:, i + q, c // 3 : c // 3 + 8, :, C * (c % 3) : C * (c % 3) + C]
                        .reshape(512, C)
                        for c in columns
                    ],
                    axis=1,
                )
                for q in range(2)
            ],
            axis=0,
        )
        d = jnp.dot(left, right, preferred_element_type=F32)
        for q in range(low, high):
            part = d[C * (q - low) : C * (q - low) + C]
            totals[q] = part if totals[q] is None else totals[q] + part
    for q in range(3):
        for n, c in enumerate(columns):
            store(q, c, (totals[q][:, C * n : C * n + C] * scale).T)


LEFT_COLUMNS, RIGHT_COLUMNS = range(4), range(4, 9)


def slots_of(taps):
    return (taps + 1) // 2


class Reduction:
    def __init__(self, place, taps, refs):
        self.place = place
        self.taps = taps
        self.g, self.r0, self.s0, self.r1, self.fin, self.send, self.recv = refs

    @staticmethod
    def scratch(taps):
        n = slots_of(taps)
        return [
            pltpu.VMEM((2, 16, n, 8, C), BF),
            pltpu.VMEM((16, n, 8, C), BF),
            pltpu.VMEM((16, n, 8, C), BF),
            pltpu.VMEM((15, n, 8, C), BF),
            pltpu.VMEM((2, 16, n, 8, C), BF),
            pltpu.SemaphoreType.DMA((47,)),
            pltpu.SemaphoreType.DMA((47,)),
        ]

    def clear(self):
        if self.taps % 2:
            self.g[:, 8:, slots_of(self.taps) - 1] = jnp.zeros((2, 8, 8, C), BF)

    def put(self, tap, block):
        for u in range(16):
            n = 8 * tap + u // 2
            self.g[u % 2, n % 16, n // 16] = block[8 * u : 8 * u + 8].astype(BF)

    def copy(self, src, dst, slot, peer):
        return pltpu.make_async_remote_copy(
            src_ref=src,
            dst_ref=dst,
            send_sem=self.send.at[slot],
            recv_sem=self.recv.at[slot],
            device_id={"space": peer},
            device_id_type=MESH,
        )

    def pair(self):
        return self.copy(self.g.at[1 - self.place["core"]], self.r0, 0, self.place["sibling"])

    def scatter(self, d):
        chip = self.place["chip"](d)
        return self.copy(
            self.s0.at[chip], self.r1.at[d - 1], d, 2 * chip + self.place["core"]
        )

    def gather(self, d):
        mine = self.fin.at[self.place["core"], self.place["chip"](0)]
        return self.copy(mine, mine, 15 + d, 2 * self.place["chip"](d) + self.place["core"])

    def forward(self, d):
        one = self.fin.at[self.place["core"], self.place["behind"](d)]
        return self.copy(one, one, 31 + d, self.place["sibling"])

    def step(self, n):
        core, chip = self.place["core"], self.place["chip"]

        def each(low, run):
            def body(d, _):
                run(d)
                return 0

            lax.fori_loop(low, 16, body, 0)

        if n == 0:
            self.pair().start()
        elif n == 1:
            self.pair().wait_recv()

            def add(c):
                self.s0[c] = (self.g[core, c].astype(F32) + self.r0[c].astype(F32)).astype(BF)

            def send(d):
                add(chip(d))
                self.scatter(d).start()

            each(1, send)
            add(chip(0))
        elif n == 2:
            each(1, lambda d: self.scatter(d).wait_recv())
            v = self.s0[chip(0)].astype(F32)
            for d in range(15):
                v = v + self.r1[d].astype(F32)
            self.fin[core, chip(0)] = v.astype(BF)
            each(1, lambda d: self.gather(d).start())
            self.forward(0).start()
        elif n == 3:

            def pass_on(d):
                self.gather(d).wait_recv()
                self.forward(d).start()

            each(1, pass_on)
        else:
            each(0, lambda d: self.forward(d).wait_recv())

    def drain(self):
        self.pair().wait_send()

        def body(d, _):
            self.scatter(d).wait_send()
            self.gather(d).wait_send()
            self.forward(d).wait_send()
            return 0

        self.forward(0).wait_send()
        lax.fori_loop(1, 16, body, 0)


def silu_parts(v):
    s = 1.0 / (1.0 + jnp.exp(-v))
    return s, s * (1.0 + v * (1.0 - s))


def kernel(
    scale,
    feats_h, mask_h, nbr_ref, w1_h, w2_h, cot_h,
    out_h, gin_h, gw2a_h, gw2b_h, gw1a_h, gw1b_h,
    feats, mask, w1, w2, cot, out_s,
    xin, xhid, xg, taps, maskb, pre1, early, gt,
    o0, o1, o2, o3, i0, i1, i2, i3,
    load_sem, store_sem, face_send, face_recv,
    *red_refs,
):
    grads_h = (gw2a_h, gw2b_h, gw1a_h, gw1b_h)
    me = lax.axis_index("space")
    n_space = 32
    core = lax.rem(me, 2)
    chip = me // 2
    z = lax.rem(chip, 4)
    y = chip // 4
    right, left = lax.rem(me + 1, n_space), lax.rem(me + n_space - 1, n_space)

    def chip_at(d):
        return 4 * lax.rem(y + d // 4, 4) + lax.rem(z + lax.rem(d, 4), 4)

    def behind(d):
        return 4 * lax.rem(y + 4 - d // 4, 4) + lax.rem(z + 4 - lax.rem(d, 4), 4)

    place = {"core": core, "sibling": me + 1 - 2 * core, "chip": chip_at, "behind": behind}
    first = 8 * (me - 1)
    red2a, red2b, red1a, red1b = (
        Reduction(place, taps_of, red_refs[7 * i : 7 * i + 7])
        for i, taps_of in enumerate((12, 15, 12, 15))
    )

    loads = [
        pltpu.make_async_copy(src, dst, load_sem.at[i])
        for i, (src, dst) in enumerate(
            ((feats_h, feats), (mask_h, mask), (w1_h, w1), (w2_h, w2), (cot_h, cot))
        )
    ]
    for c in loads:
        c.start()

    barrier = pltpu.get_barrier_semaphore()
    for peer in (left, right):
        pl.semaphore_signal(barrier, inc=1, device_id={"space": peer}, device_id_type=MESH)

    def greet(d, _):
        peer = 2 * chip_at(d) + core
        pl.semaphore_signal(barrier, inc=1, device_id={"space": peer}, device_id_type=MESH)
        return 0

    lax.fori_loop(1, 16, greet, 0)
    pl.semaphore_wait(barrier, 17)

    faces = ((o0, i0), (o1, i1), (o2, i2), (o3, i3))

    def plane_copies(n, ref, slab, a):
        return [
            pltpu.make_async_remote_copy(
                src_ref=ref.at[slab, pl.ds(8, 8)],
                dst_ref=ref.at[slab, pl.ds(at, 8)],
                send_sem=face_send.at[n, side, a],
                recv_sem=face_recv.at[n, side, a],
                device_id={"space": peer},
                device_id_type=MESH,
            )
            for side, (at, peer) in enumerate(((0, right), (16, left)))
        ]

    def send_plane(n, a, v):
        outer, inner = faces[n]
        keep_faces(outer, inner, a, v)

        def start(ref, slab):
            for c in plane_copies(n, ref, slab, a):
                c.start()

        when_outer(a, lambda: start(outer, a // 7), lambda: start(inner, a - 1))

    def face_copies(n):
        outer, inner = faces[n]
        copies = []
        for a in range(8):
            if a in (0, 7):
                copies += plane_copies(n, outer, a // 7, a)
            else:
                copies += plane_copies(n, inner, a - 1, a)
        return copies

    def receive_faces(n, x_ref):
        for c in face_copies(n):
            c.wait_recv()
        fill_rim(x_ref, faces[n], nbr_ref, first)

    for outer, inner in faces:
        for side in range(2):
            outer[side, 24] = jnp.zeros((8, 8, C), BF)
        for a in range(6):
            inner[a, 24] = jnp.zeros((2, 8, C), BF)
    for red in (red2a, red2b, red1a, red1b):
        red.clear()
    for side in range(2):
        for a in (0, 1, 10, 11):
            gt[side, a] = jnp.zeros((C, 2 * C), BF)

    for x_ref in (xin, xhid):
        for column in (0, 9):
            x_ref[:, :, column] = jnp.zeros((4, 10, 16, 3 * C), BF)

    loads[1].wait()
    loads[0].wait()

    def mask_plane(t, _):
        a = jnp.where(t == 0, 0, jnp.where(t == 1, 7, t - 1))
        row = lax.broadcasted_iota(jnp.int32, (C, C), 0)
        lane = lax.broadcasted_iota(jnp.int32, (C, C), 1)
        hit = lane == lax.rem(a, 2) * 64 + (row // 16) * 8 + lax.rem(row, 8)
        second = lax.rem(row // 8, 2) == 1
        at = pl.ds(pl.multiple_of((a // 2) * C, C), C)
        pieces = []
        for p in range(4):
            m0 = mask[2 * p : 2 * p + 1, at].astype(F32)
            m1 = mask[2 * p + 1 : 2 * p + 2, at].astype(F32)
            pieces.append(jnp.where(hit, jnp.where(second, m1, m0), 0.0).astype(BF))
        spread = jnp.dot(
            jnp.concatenate(pieces, axis=0), jnp.ones((C, C), BF), preferred_element_type=F32
        )
        m = spread.reshape(4, 8, 16, C)
        maskb[a] = m.astype(BF)
        v = pair_plane(feats, a) * m
        send_plane(0, a, v)
        put_plane(xin, a, v)
        return 0

    lax.fori_loop(0, 8, mask_plane, 0)

    loads[2].wait()
    loads[3].wait()
    build_taps(taps.at[0], w1, False)
    build_taps(taps.at[2], w2, True)
    def first_done(a, v):
        pre1[a] = v
        s, _ = silu_parts(v)
        h = maskb[a].astype(F32) * (v * s)
        send_plane(1, a, h)
        put_plane(xhid, a, h)

    convolve_split(xin, taps.at[0], early, lambda: receive_faces(0, xin), first_done)
    build_taps(taps.at[1], w2, False)
    build_taps(taps.at[3], w1, True)
    loads[4].wait()

    def second_done(a, v):
        s, slope = silu_parts(v)
        m = maskb[a].astype(F32)
        unpair_plane(out_s, a, m * (v * s))
        g = pair_plane(cot, a) * m * slope
        send_plane(2, a, g)
        put_plane(xg, a, g)
        put_transposed(gt, a, g)

    convolve_split(xhid, taps.at[1], early, lambda: receive_faces(1, xhid), second_done)
    store_out = pltpu.make_async_copy(out_s, out_h, store_sem.at[0])
    store_out.start()

    weight_grad(xhid, gt, LEFT_COLUMNS, scale, lambda q, c, v: red2a.put(4 * (2 - q) + c, v))
    red2a.step(0)
    weight_grad(xhid, gt, RIGHT_COLUMNS, scale, lambda q, c, v: red2b.put(5 * (2 - q) + c - 4, v))
    red2b.step(0)
    red2a.step(1)
    receive_faces(2, xg)

    def third_done(a, v):
        _, slope = silu_parts(pre1[a])
        g = maskb[a].astype(F32) * slope * v
        send_plane(3, a, g)
        put_plane(xhid, a, g)
        put_transposed(gt, a, g)

    def third_between(q):
        @pl.when(q == 0)
        def _():
            red2b.step(1)

        @pl.when(q == 3)
        def _():
            red2a.step(2)

    convolve(xg, taps.at[2], third_done, third_between)
    store_out.wait()

    weight_grad(xin, gt, LEFT_COLUMNS, scale, lambda q, c, v: red1a.put(4 * (2 - q) + c, v))
    red1a.step(0)
    weight_grad(xin, gt, RIGHT_COLUMNS, scale, lambda q, c, v: red1b.put(5 * (2 - q) + c - 4, v))
    red1b.step(0)
    red1a.step(1)
    red1b.step(1)
    red2b.step(2)
    receive_faces(3, xhid)

    def last_done(a, v):
        unpair_plane(out_s, a, maskb[a].astype(F32) * v)

    def last_between(q):
        @pl.when(q == 1)
        def _():
            red1a.step(2)

        @pl.when(q == 2)
        def _():
            red1b.step(2)

    convolve(xhid, taps.at[3], last_done, last_between)
    reductions = (red2a, red2b, red1a, red1b)
    stores = [
        pltpu.make_async_copy(src, dst, store_sem.at[1 + i])
        for i, (src, dst) in enumerate(
            ((out_s, gin_h), *((red.fin, dst) for red, dst in zip(reductions, grads_h)))
        )
    ]
    stores[0].start()
    red2a.step(3)
    red1a.step(3)
    red2b.step(3)
    red2a.step(4)
    stores[1].start()
    red2b.step(4)
    stores[2].start()
    red1b.step(3)
    red1a.step(4)
    stores[3].start()
    red1b.step(4)
    stores[4].start()
    for n in range(4):
        for c in face_copies(n):
            c.wait_send()
    for red in (red2a, red2b, red1a, red1b):
        red.drain()
    for c in stores:
        c.wait()


def finish(
    out_t, gin_t, gw2a_t, gw2b_t, gw1a_t, gw1b_t,
    out_h, gin_h, gw1_h, gw2_h,
    fin2a, fin2b, fin1a, fin1b, w1, w2, out_s, gin_s, sem,
):
    pairs = (
        (gw2a_t, fin2a), (gw2b_t, fin2b), (gw1a_t, fin1a), (gw1b_t, fin1b),
        (out_t, out_s), (gin_t, gin_s),
    )
    reads = [pltpu.make_async_copy(src, dst, sem.at[i]) for i, (src, dst) in enumerate(pairs)]
    pairs = ((w2, gw2_h), (w1, gw1_h), (out_s, out_h), (gin_s, gin_h))
    writes = [pltpu.make_async_copy(src, dst, sem.at[6 + i]) for i, (src, dst) in enumerate(pairs)]
    for c in reads:
        c.start()

    def order(fin, tap, dst, to):
        for u in range(16):
            n = 8 * tap + u // 2
            dst[to, 8 * u : 8 * u + 8] = fin[u % 2, n % 16, n // 16].astype(F32)

    for i, (left, right, dst) in enumerate(((fin2a, fin2b, w2), (fin1a, fin1b, w1))):
        reads[2 * i].wait()
        reads[2 * i + 1].wait()
        for k in range(3):
            for c in LEFT_COLUMNS:
                order(left, 4 * k + c, dst, 9 * k + c)
            for c in RIGHT_COLUMNS:
                order(right, 5 * k + c - 4, dst, 9 * k + c)
        writes[i].start()
    for i in (4, 5):
        reads[i].wait()
        writes[i - 2].start()
    for c in writes:
        c.wait()


def body(feats, mask, neighbours, weight_one, weight_two, cotangent):
    bricks, voxels, channels = feats.shape
    scale = 1.0 / math.sqrt(voxels * bricks)
    cube = (bricks, 8, 8, 8, channels)
    field = pltpu.VMEM((4, 10, 10, 16, 3 * C), BF)
    outer, inner = pltpu.VMEM((2, 25, 8, 8, C), BF), pltpu.VMEM((6, 25, 2, 8, C), BF)
    anywhere = pl.BlockSpec(memory_space=pl.ANY)
    parts = [
        jax.ShapeDtypeStruct((4, 2, 8, 8, 8, C), BF),
        jax.ShapeDtypeStruct((4, 2, 8, 8, 8, C), BF),
        *(jax.ShapeDtypeStruct((2, 16, slots_of(n), 8, C), BF) for n in (12, 15, 12, 15)),
    ]
    left_over = pl.pallas_call(
        functools.partial(kernel, scale),
        out_shape=tuple(parts),
        in_specs=[
            anywhere, anywhere, pl.BlockSpec(memory_space=pltpu.SMEM), anywhere, anywhere, anywhere,
        ],
        out_specs=(anywhere,) * 6,
        scratch_shapes=[
            pltpu.VMEM(cube, BF),
            pltpu.VMEM((bricks, voxels), jnp.int32),
            pltpu.VMEM((27, C, C), BF),
            pltpu.VMEM((27, C, C), BF),
            pltpu.VMEM(cube, BF),
            pltpu.VMEM((4, 2, 8, 8, 8, C), BF),
            field, field, field,
            pltpu.VMEM((4, 36, C, 2 * C), BF),
            pltpu.VMEM((8, 4, 8, 16, C), BF),
            pltpu.VMEM((8, 4, 8, 16, C), F32),
            pltpu.VMEM((4, 4, 8, 16, C), F32),
            pltpu.VMEM((2, 12, C, 2 * C), BF),
            *[outer] * 4,
            *[inner] * 4,
            pltpu.SemaphoreType.DMA((5,)),
            pltpu.SemaphoreType.DMA((6,)),
            pltpu.SemaphoreType.DMA((4, 2, 8)),
            pltpu.SemaphoreType.DMA((4, 2, 8)),
            *(ref for n in (12, 15, 12, 15) for ref in Reduction.scratch(n)),
        ],
        compiler_params=pltpu.CompilerParams(
            collective_id=0, has_side_effects=True, vmem_limit_bytes=60 * 2**20
        ),
        name="bricks",
    )(feats.reshape(cube), mask, neighbours, weight_one, weight_two, cotangent.reshape(cube))

    out, gin, gw1, gw2 = pl.pallas_call(
        finish,
        out_shape=(
            *parts[:2],
            jax.ShapeDtypeStruct((27, C, C), F32),
            jax.ShapeDtypeStruct((27, C, C), F32),
        ),
        in_specs=[anywhere] * 6,
        out_specs=(anywhere,) * 4,
        scratch_shapes=[
            *(pltpu.VMEM(p.shape, BF) for p in parts[2:]),
            pltpu.VMEM((27, C, C), F32),
            pltpu.VMEM((27, C, C), F32),
            pltpu.VMEM(parts[0].shape, BF),
            pltpu.VMEM(parts[1].shape, BF),
            pltpu.SemaphoreType.DMA((10,)),
        ],
        name="outputs",
    )(*left_over)
    return (
        out.reshape(bricks, voxels, channels),
        gin.reshape(bricks, voxels, channels),
        gw1,
        gw2,
    )


def solution(mesh):
    in_specs = (
        P(("scene", "space"), None, None),
        P(("scene", "space"), None),
        P(("scene", "space"), None),
        P(),
        P(),
        P(("scene", "space"), None, None),
    )
    out_specs = (
        P(("scene", "space"), None, None),
        P(("scene", "space"), None, None),
        P("scene", None, None),
        P("scene", None, None),
    )
    return jax.shard_map(body, mesh=mesh, in_specs=in_specs, out_specs=out_specs, check_vma=False)
```

```python
import functools
import math

import jax
import jax.numpy as jnp
from jax import lax
from jax.experimental import pallas as pl
from jax.experimental.pallas import tpu as pltpu
from jax.sharding import PartitionSpec as P

BF = jnp.bfloat16
F32 = jnp.float32
C = 128
MESH = pl.DeviceIdType.MESH


def shifted(v):
    row = lax.broadcasted_iota(jnp.int32, v.shape, v.ndim - 1 - 1)
    down = jnp.where(row == 0, 0.0, pltpu.roll(v, 1, v.ndim - 2))
    up = jnp.where(row == 7, 0.0, pltpu.roll(v, 7, v.ndim - 2))
    return down, v, up


def put_plane(x_ref, a, v):
    for k, s in enumerate(shifted(v.reshape(64, 8, C))):
        x_ref[:, 1 + a, 1:9, :, C * k : C * k + C] = s.reshape(4, 8, 16, C).astype(BF)


def pair_plane(ref, a):
    v = ref[:, a].astype(F32).reshape(4, 2, 8, 8, C)
    return jnp.stack([v[:, 0], v[:, 1]], axis=2).reshape(4, 8, 16, C)


def unpair_plane(ref, a, v):
    w = v.reshape(4, 8, 2, 8, C)
    for half in range(2):
        ref[:, half, a] = w[:, :, half].astype(BF)


def when_outer(a, run_outer, run_inner):
    if isinstance(a, int):
        run_outer() if a in (0, 7) else run_inner()
        return
    pl.when((a == 0) | (a == 7))(run_outer)
    pl.when((a > 0) & (a < 7))(run_inner)


def keep_faces(outer, inner, a, v):
    w = v.reshape(4, 8, 2, 8, C)

    def whole():
        for p in range(4):
            for half in range(2):
                outer[a // 7, 8 + 2 * p + half] = w[p, :, half].astype(BF)

    def ends():
        for p in range(4):
            for half in range(2):
                inner[a - 1, 8 + 2 * p + half, 0] = w[p, 0, half].astype(BF)
                inner[a - 1, 8 + 2 * p + half, 1] = w[p, 7, half].astype(BF)

    when_outer(a, whole, ends)


def fill_rim(x_ref, faces, nbr_ref, first):
    outer, inner = faces

    def body(p, _):
        def source(column):
            out = []
            for half in range(2):
                n = nbr_ref[2 * p + half, column]
                out.append(jnp.where(n >= 0, jnp.clip(n - first, 0, 23), 24))
            return out

        def cell(x, y, i, j):
            w = jnp.stack([x.astype(F32), y.astype(F32)], axis=0)
            for k, s in enumerate(shifted(w)):
                x_ref[p, i, j, :, C * k : C * k + C] = s.reshape(16, C).astype(BF)

        for column, side, where, i, j in (
            (0, 1, 7, 0, 0), (2, 1, 0, 0, 9), (5, 0, 7, 9, 0), (7, 0, 0, 9, 9),
        ):
            m, n = source(column)
            cell(outer[side, m, where], outer[side, n, where], i, j)
        for column, side, i in ((1, 1, 0), (6, 0, 9)):
            m, n = source(column)
            u, v = outer[side, m].astype(F32), outer[side, n].astype(F32)
            w = jnp.stack([u, v], axis=1).reshape(16, 8, C)
            for k, s in enumerate(shifted(w)):
                x_ref[p, i, 1:9, :, C * k : C * k + C] = s.reshape(8, 16, C).astype(BF)
        for column, end, j in ((3, 1, 0), (4, 0, 9)):
            m, n = source(column)
            cell(outer[0, m, 7 * end], outer[0, n, 7 * end], 1, j)
            for a in range(1, 7):
                cell(inner[a - 1, m, end], inner[a - 1, n, end], 1 + a, j)
            cell(outer[1, m, 7 * end], outer[1, n, 7 * end], 8, j)
        return 0

    lax.fori_loop(0, 4, body, 0)


def build_taps(t_ref, w_ref, flipped):
    def body(t, _):
        zero = jnp.zeros((C, C), BF)
        t_ref[t, :, C:] = zero
        t_ref[27 + t, :, :C] = zero
        for k in range(3):
            if flipped:
                w = w_ref[26 - (9 * k + t)].T
            else:
                w = w_ref[9 * k + t]
            t_ref[9 * k + t, :, :C] = w
            t_ref[9 * k + 9 + t, :, C:] = w
        return 0

    lax.fori_loop(0, 9, body, 0)


def convolve(x_ref, t_ref, epilogue, between=None):
    def body(t, _):
        q = jnp.where(t == 0, 0, jnp.where(t == 1, 3, t - 1))
        windows = [
            x_ref[:, 2 * q + p, k : k + 8].reshape(512, 3 * C) for p in range(4) for k in range(3)
        ]
        total = jnp.dot(
            jnp.concatenate(windows, axis=1),
            t_ref[...].reshape(36 * C, 2 * C),
            preferred_element_type=F32,
        )
        for u in range(2):
            epilogue(2 * q + u, total[:, C * u : C * u + C].reshape(4, 8, 16, C))
        if between is not None:
            between(t)
        return 0

    lax.fori_loop(0, 4, body, 0)


def convolve_split(x_ref, t_ref, inner_ref, arrive, epilogue):
    def pair(q):
        windows = [
            x_ref[:, 2 * q + p, k : k + 8].reshape(512, 3 * C) for p in range(4) for k in range(3)
        ]
        total = jnp.dot(
            jnp.concatenate(windows, axis=1),
            t_ref[...].reshape(36 * C, 2 * C),
            preferred_element_type=F32,
        )
        return [total[:, C * u : C * u + C].reshape(4, 8, 16, C) for u in range(2)]

    def early(t, _):
        for u, v in enumerate(pair(1 + t)):
            inner_ref[2 * t + u] = v
        return 0

    lax.fori_loop(0, 2, early, 0)
    arrive()
    for end, column, k in ((0, 0, 0), (7, 9, 2)):
        left = [x_ref[:, 2 + p : 6 + p, column].reshape(256, 3 * C) for p in range(3)]
        right = [t_ref[9 * p + 3 * k : 9 * p + 3 * k + 3, :, :C].reshape(3 * C, C) for p in range(3)]
        d = jnp.dot(
            jnp.concatenate(left, axis=1),
            jnp.concatenate(right, axis=0),
            preferred_element_type=F32,
        ).reshape(4, 4, 16, C)
        for a in range(4):
            inner_ref[a, :, end] += d[:, a]
    for t in range(2):
        outer = pair(3 * t)
        for u in range(2):
            epilogue(2 + 2 * t + u, inner_ref[2 * t + u])
        for u in range(2):
            epilogue(6 * t + u, outer[u])


def put_transposed(gt_ref, a, v):
    flat = v.reshape(4, C, C).astype(BF)
    for p in range(4):
        gt_ref[p // 2, a + 2, :, C * (p % 2) : C * (p % 2) + C] = flat[p].T


def weight_grad(x_ref, gt_ref, columns, scale, store):
    totals = [None] * 3
    for i in range(0, 10, 2):
        low, high = (1 if i == 0 else 0), (2 if i == 8 else 3)
        left = jnp.concatenate(
            [
                gt_ref[h, i + q + low : i + q + high].reshape(C * (high - low), 2 * C)
                for q in range(2)
                for h in range(2)
            ],
            axis=1,
        )
        right = jnp.concatenate(
            [
                jnp.concatenate(
                    [
                        x_ref[:, i + q, c // 3 : c // 3 + 8, :, C * (c % 3) : C * (c % 3) + C]
                        .reshape(512, C)
                        for c in columns
                    ],
                    axis=1,
                )
                for q in range(2)
            ],
            axis=0,
        )
        d = jnp.dot(left, right, preferred_element_type=F32)
        for q in range(low, high):
            part = d[C * (q - low) : C * (q - low) + C]
            totals[q] = part if totals[q] is None else totals[q] + part
    for q in range(3):
        for n, c in enumerate(columns):
            store(q, c, (totals[q][:, C * n : C * n + C] * scale).T)


LEFT_COLUMNS, RIGHT_COLUMNS = range(4), range(4, 9)


def slots_of(taps):
    return (taps + 1) // 2


class Reduction:
    def __init__(self, place, taps, refs):
        self.place = place
        self.taps = taps
        self.g, self.r0, self.s0, self.r1, self.fin, self.send, self.recv = refs

    @staticmethod
    def scratch(taps):
        n = slots_of(taps)
        return [
            pltpu.VMEM((2, 16, n, 8, C), BF),
            pltpu.VMEM((16, n, 8, C), BF),
            pltpu.VMEM((16, n, 8, C), BF),
            pltpu.VMEM((15, n, 8, C), BF),
            pltpu.VMEM((2, 16, n, 8, C), BF),
            pltpu.SemaphoreType.DMA((47,)),
            pltpu.SemaphoreType.DMA((47,)),
        ]

    def clear(self):
        if self.taps % 2:
            self.g[:, 8:, slots_of(self.taps) - 1] = jnp.zeros((2, 8, 8, C), BF)

    def put(self, tap, block):
        for u in range(16):
            n = 8 * tap + u // 2
            self.g[u % 2, n % 16, n // 16] = block[8 * u : 8 * u + 8].astype(BF)

    def copy(self, src, dst, slot, peer):
        return pltpu.make_async_remote_copy(
            src_ref=src,
            dst_ref=dst,
            send_sem=self.send.at[slot],
            recv_sem=self.recv.at[slot],
            device_id={"space": peer},
            device_id_type=MESH,
        )

    def pair(self):
        return self.copy(self.g.at[1 - self.place["core"]], self.r0, 0, self.place["sibling"])

    def scatter(self, d):
        chip = self.place["chip"](d)
        return self.copy(
            self.s0.at[chip], self.r1.at[d - 1], d, 2 * chip + self.place["core"]
        )

    def gather(self, d):
        mine = self.fin.at[self.place["core"], self.place["chip"](0)]
        return self.copy(mine, mine, 15 + d, 2 * self.place["chip"](d) + self.place["core"])

    def forward(self, d):
        one = self.fin.at[self.place["core"], self.place["behind"](d)]
        return self.copy(one, one, 31 + d, self.place["sibling"])

    def step(self, n):
        core, chip = self.place["core"], self.place["chip"]

        def each(low, run):
            def body(d, _):
                run(d)
                return 0

            lax.fori_loop(low, 16, body, 0)

        if n == 0:
            self.pair().start()
        elif n == 1:
            self.pair().wait_recv()

            def add(c):
                self.s0[c] = (self.g[core, c].astype(F32) + self.r0[c].astype(F32)).astype(BF)

            def send(d):
                add(chip(d))
                self.scatter(d).start()

            each(1, send)
            add(chip(0))
        elif n == 2:
            each(1, lambda d: self.scatter(d).wait_recv())
            v = self.s0[chip(0)].astype(F32)
            for d in range(15):
                v = v + self.r1[d].astype(F32)
            self.fin[core, chip(0)] = v.astype(BF)
            each(1, lambda d: self.gather(d).start())
            self.forward(0).start()
        elif n == 3:

            def pass_on(d):
                self.gather(d).wait_recv()
                self.forward(d).start()

            each(1, pass_on)
        else:
            each(0, lambda d: self.forward(d).wait_recv())

    def drain_scatter(self):
        self.pair().wait_send()

        def body(d, _):
            self.scatter(d).wait_send()
            return 0

        lax.fori_loop(1, 16, body, 0)

    def drain_gather(self):
        def body(d, _):
            self.gather(d).wait_send()
            self.forward(d).wait_send()
            return 0

        self.forward(0).wait_send()
        lax.fori_loop(1, 16, body, 0)


def silu_parts(v):
    s = 1.0 / (1.0 + jnp.exp(-v))
    return s, s * (1.0 + v * (1.0 - s))


def kernel(
    scale,
    feats_h, mask_h, nbr_ref, w1_h, w2_h, cot_h,
    out_h, gin_h, gw2a_h, gw2b_h, gw1a_h, gw1b_h,
    feats, mask, w1, w2, cot, out_s,
    xin, xhid, xg, taps, maskb, pre1, early, gt,
    o0, o1, o2, o3, i0, i1, i2, i3,
    load_sem, store_sem, face_send, face_recv,
    *red_refs,
):
    grads_h = (gw2a_h, gw2b_h, gw1a_h, gw1b_h)
    me = lax.axis_index("space")
    n_space = 32
    core = lax.rem(me, 2)
    chip = me // 2
    z = lax.rem(chip, 4)
    y = chip // 4
    right, left = lax.rem(me + 1, n_space), lax.rem(me + n_space - 1, n_space)

    def chip_at(d):
        return 4 * lax.rem(y + d // 4, 4) + lax.rem(z + lax.rem(d, 4), 4)

    def behind(d):
        return 4 * lax.rem(y + 4 - d // 4, 4) + lax.rem(z + 4 - lax.rem(d, 4), 4)

    place = {"core": core, "sibling": me + 1 - 2 * core, "chip": chip_at, "behind": behind}
    first = 8 * (me - 1)
    red2a, red2b, red1a, red1b = (
        Reduction(place, taps_of, red_refs[7 * i : 7 * i + 7])
        for i, taps_of in enumerate((12, 15, 12, 15))
    )

    loads = [
        pltpu.make_async_copy(src, dst, load_sem.at[i])
        for i, (src, dst) in enumerate(
            ((feats_h, feats), (mask_h, mask), (w1_h, w1), (w2_h, w2), (cot_h, cot))
        )
    ]
    for c in loads:
        c.start()

    barrier = pltpu.get_barrier_semaphore()
    for peer in (left, right):
        pl.semaphore_signal(barrier, inc=1, device_id={"space": peer}, device_id_type=MESH)

    def greet(d, _):
        peer = 2 * chip_at(d) + core
        pl.semaphore_signal(barrier, inc=1, device_id={"space": peer}, device_id_type=MESH)
        return 0

    lax.fori_loop(1, 16, greet, 0)
    pl.semaphore_wait(barrier, 17)

    faces = ((o0, i0), (o1, i1), (o2, i2), (o3, i3))

    def plane_copies(n, ref, slab, a):
        return [
            pltpu.make_async_remote_copy(
                src_ref=ref.at[slab, pl.ds(8, 8)],
                dst_ref=ref.at[slab, pl.ds(at, 8)],
                send_sem=face_send.at[n, side, a],
                recv_sem=face_recv.at[n, side, a],
                device_id={"space": peer},
                device_id_type=MESH,
            )
            for side, (at, peer) in enumerate(((0, right), (16, left)))
        ]

    def send_plane(n, a, v):
        outer, inner = faces[n]
        keep_faces(outer, inner, a, v)

        def start(ref, slab):
            for c in plane_copies(n, ref, slab, a):
                c.start()

        when_outer(a, lambda: start(outer, a // 7), lambda: start(inner, a - 1))

    def face_copies(n):
        outer, inner = faces[n]
        copies = []
        for a in range(8):
            if a in (0, 7):
                copies += plane_copies(n, outer, a // 7, a)
            else:
                copies += plane_copies(n, inner, a - 1, a)
        return copies

    def receive_faces(n, x_ref):
        for c in face_copies(n):
            c.wait_recv()
        fill_rim(x_ref, faces[n], nbr_ref, first)

    for outer, inner in faces:
        for side in range(2):
            outer[side, 24] = jnp.zeros((8, 8, C), BF)
        for a in range(6):
            inner[a, 24] = jnp.zeros((2, 8, C), BF)
    for red in (red2a, red2b, red1a, red1b):
        red.clear()
    for side in range(2):
        for a in (0, 1, 10, 11):
            gt[side, a] = jnp.zeros((C, 2 * C), BF)

    for x_ref in (xin, xhid):
        for column in (0, 9):
            x_ref[:, :, column] = jnp.zeros((4, 10, 16, 3 * C), BF)

    loads[1].wait()
    loads[0].wait()

    def mask_plane(t, _):
        a = jnp.where(t == 0, 0, jnp.where(t == 1, 7, t - 1))
        row = lax.broadcasted_iota(jnp.int32, (C, C), 0)
        lane = lax.broadcasted_iota(jnp.int32, (C, C), 1)
        hit = lane == lax.rem(a, 2) * 64 + (row // 16) * 8 + lax.rem(row, 8)
        second = lax.rem(row // 8, 2) == 1
        at = pl.ds(pl.multiple_of((a // 2) * C, C), C)
        pieces = []
        for p in range(4):
            m0 = mask[2 * p : 2 * p + 1, at].astype(F32)
            m1 = mask[2 * p + 1 : 2 * p + 2, at].astype(F32)
            pieces.append(jnp.where(hit, jnp.where(second, m1, m0), 0.0).astype(BF))
        spread = jnp.dot(
            jnp.concatenate(pieces, axis=0), jnp.ones((C, C), BF), preferred_element_type=F32
        )
        m = spread.reshape(4, 8, 16, C)
        maskb[a] = m.astype(BF)
        v = pair_plane(feats, a) * m
        send_plane(0, a, v)
        put_plane(xin, a, v)
        return 0

    lax.fori_loop(0, 8, mask_plane, 0)

    loads[2].wait()
    loads[3].wait()
    build_taps(taps.at[0], w1, False)
    build_taps(taps.at[2], w2, True)
    def first_done(a, v):
        pre1[a] = v
        s, _ = silu_parts(v)
        h = maskb[a].astype(F32) * (v * s)
        send_plane(1, a, h)
        put_plane(xhid, a, h)

    convolve_split(xin, taps.at[0], early, lambda: receive_faces(0, xin), first_done)
    build_taps(taps.at[1], w2, False)
    build_taps(taps.at[3], w1, True)
    loads[4].wait()

    def second_done(a, v):
        s, slope = silu_parts(v)
        m = maskb[a].astype(F32)
        unpair_plane(out_s, a, m * (v * s))
        g = pair_plane(cot, a) * m * slope
        send_plane(2, a, g)
        put_plane(xg, a, g)
        put_transposed(gt, a, g)

    convolve_split(xhid, taps.at[1], early, lambda: receive_faces(1, xhid), second_done)
    store_out = pltpu.make_async_copy(out_s, out_h, store_sem.at[0])
    store_out.start()

    weight_grad(xhid, gt, LEFT_COLUMNS, scale, lambda q, c, v: red2a.put(4 * (2 - q) + c, v))
    red2a.step(0)
    weight_grad(xhid, gt, RIGHT_COLUMNS, scale, lambda q, c, v: red2b.put(5 * (2 - q) + c - 4, v))
    red2b.step(0)
    red2a.step(1)
    receive_faces(2, xg)

    def third_done(a, v):
        _, slope = silu_parts(pre1[a])
        g = maskb[a].astype(F32) * slope * v
        send_plane(3, a, g)
        put_plane(xhid, a, g)
        put_transposed(gt, a, g)

    def third_between(q):
        @pl.when(q == 0)
        def _():
            red2b.step(1)

        @pl.when(q == 3)
        def _():
            red2a.step(2)

    convolve(xg, taps.at[2], third_done, third_between)
    store_out.wait()

    weight_grad(xin, gt, LEFT_COLUMNS, scale, lambda q, c, v: red1a.put(4 * (2 - q) + c, v))
    red1a.step(0)
    weight_grad(xin, gt, RIGHT_COLUMNS, scale, lambda q, c, v: red1b.put(5 * (2 - q) + c - 4, v))
    red1b.step(0)
    red1a.step(1)
    red1b.step(1)
    red2b.step(2)
    receive_faces(3, xhid)

    def last_done(a, v):
        unpair_plane(out_s, a, maskb[a].astype(F32) * v)

    def last_between(q):
        @pl.when(q == 1)
        def _():
            red1a.step(2)

        @pl.when(q == 2)
        def _():
            red1b.step(2)

    convolve(xhid, taps.at[3], last_done, last_between)
    reductions = (red2a, red2b, red1a, red1b)
    stores = [
        pltpu.make_async_copy(src, dst, store_sem.at[1 + i])
        for i, (src, dst) in enumerate(
            ((out_s, gin_h), *((red.fin, dst) for red, dst in zip(reductions, grads_h)))
        )
    ]
    stores[0].start()
    red2a.step(3)
    red1a.step(3)
    red2b.step(3)
    red2a.step(4)
    stores[1].start()
    red2b.step(4)
    stores[2].start()
    for n in range(4):
        for c in face_copies(n):
            c.wait_send()
    for red in reductions:
        red.drain_scatter()
    red2a.drain_gather()
    red2b.drain_gather()
    red1b.step(3)
    red1a.step(4)
    stores[3].start()
    red1a.drain_gather()
    red1b.step(4)
    stores[4].start()
    red1b.drain_gather()
    for c in stores:
        c.wait()


def finish(
    out_t, gin_t, gw2a_t, gw2b_t, gw1a_t, gw1b_t,
    out_h, gin_h, gw1_h, gw2_h,
    fin2a, fin2b, fin1a, fin1b, w1, w2, out_s, gin_s, sem,
):
    pairs = (
        (gw2a_t, fin2a), (gw2b_t, fin2b), (gw1a_t, fin1a), (gw1b_t, fin1b),
        (out_t, out_s), (gin_t, gin_s),
    )
    reads = [pltpu.make_async_copy(src, dst, sem.at[i]) for i, (src, dst) in enumerate(pairs)]
    pairs = ((w2, gw2_h), (w1, gw1_h), (out_s, out_h), (gin_s, gin_h))
    writes = [pltpu.make_async_copy(src, dst, sem.at[6 + i]) for i, (src, dst) in enumerate(pairs)]
    for c in reads:
        c.start()

    def order(fin, tap, dst, to):
        for u in range(16):
            n = 8 * tap + u // 2
            dst[to, 8 * u : 8 * u + 8] = fin[u % 2, n % 16, n // 16].astype(F32)

    for i, (left, right, dst) in enumerate(((fin2a, fin2b, w2), (fin1a, fin1b, w1))):
        reads[2 * i].wait()
        reads[2 * i + 1].wait()
        for k in range(3):
            for c in LEFT_COLUMNS:
                order(left, 4 * k + c, dst, 9 * k + c)
            for c in RIGHT_COLUMNS:
                order(right, 5 * k + c - 4, dst, 9 * k + c)
        writes[i].start()
        if i == 0:
            for n in (4, 5):
                reads[n].wait()
                writes[n - 2].start()
    for c in writes:
        c.wait()


def body(feats, mask, neighbours, weight_one, weight_two, cotangent):
    bricks, voxels, channels = feats.shape
    scale = 1.0 / math.sqrt(voxels * bricks)
    cube = (bricks, 8, 8, 8, channels)
    field = pltpu.VMEM((4, 10, 10, 16, 3 * C), BF)
    outer, inner = pltpu.VMEM((2, 25, 8, 8, C), BF), pltpu.VMEM((6, 25, 2, 8, C), BF)
    anywhere = pl.BlockSpec(memory_space=pl.ANY)
    parts = [
        jax.ShapeDtypeStruct((4, 2, 8, 8, 8, C), BF),
        jax.ShapeDtypeStruct((4, 2, 8, 8, 8, C), BF),
        *(jax.ShapeDtypeStruct((2, 16, slots_of(n), 8, C), BF) for n in (12, 15, 12, 15)),
    ]
    left_over = pl.pallas_call(
        functools.partial(kernel, scale),
        out_shape=tuple(parts),
        in_specs=[
            anywhere, anywhere, pl.BlockSpec(memory_space=pltpu.SMEM), anywhere, anywhere, anywhere,
        ],
        out_specs=(anywhere,) * 6,
        scratch_shapes=[
            pltpu.VMEM(cube, BF),
            pltpu.VMEM((bricks, voxels), jnp.int32),
            pltpu.VMEM((27, C, C), BF),
            pltpu.VMEM((27, C, C), BF),
            pltpu.VMEM(cube, BF),
            pltpu.VMEM((4, 2, 8, 8, 8, C), BF),
            field, field, field,
            pltpu.VMEM((4, 36, C, 2 * C), BF),
            pltpu.VMEM((8, 4, 8, 16, C), BF),
            pltpu.VMEM((8, 4, 8, 16, C), F32),
            pltpu.VMEM((4, 4, 8, 16, C), F32),
            pltpu.VMEM((2, 12, C, 2 * C), BF),
            *[outer] * 4,
            *[inner] * 4,
            pltpu.SemaphoreType.DMA((5,)),
            pltpu.SemaphoreType.DMA((6,)),
            pltpu.SemaphoreType.DMA((4, 2, 8)),
            pltpu.SemaphoreType.DMA((4, 2, 8)),
            *(ref for n in (12, 15, 12, 15) for ref in Reduction.scratch(n)),
        ],
        compiler_params=pltpu.CompilerParams(
            collective_id=0, has_side_effects=True, vmem_limit_bytes=60 * 2**20
        ),
        name="bricks",
    )(feats.reshape(cube), mask, neighbours, weight_one, weight_two, cotangent.reshape(cube))

    out, gin, gw1, gw2 = pl.pallas_call(
        finish,
        out_shape=(
            *parts[:2],
            jax.ShapeDtypeStruct((27, C, C), F32),
            jax.ShapeDtypeStruct((27, C, C), F32),
        ),
        in_specs=[anywhere] * 6,
        out_specs=(anywhere,) * 4,
        scratch_shapes=[
            *(pltpu.VMEM(p.shape, BF) for p in parts[2:]),
            pltpu.VMEM((27, C, C), F32),
            pltpu.VMEM((27, C, C), F32),
            pltpu.VMEM(parts[0].shape, BF),
            pltpu.VMEM(parts[1].shape, BF),
            pltpu.SemaphoreType.DMA((10,)),
        ],
        name="outputs",
    )(*left_over)
    return (
        out.reshape(bricks, voxels, channels),
        gin.reshape(bricks, voxels, channels),
        gw1,
        gw2,
    )


def solution(mesh):
    in_specs = (
        P(("scene", "space"), None, None),
        P(("scene", "space"), None),
        P(("scene", "space"), None),
        P(),
        P(),
        P(("scene", "space"), None, None),
    )
    out_specs = (
        P(("scene", "space"), None, None),
        P(("scene", "space"), None, None),
        P("scene", None, None),
        P("scene", None, None),
    )
    return jax.shard_map(body, mesh=mesh, in_specs=in_specs, out_specs=out_specs, check_vma=False)
```
